128 devices in a mesh: seq: 16 (over y, x), hg: 8 (over z, core).
Axes of the slice: x: 4, y: 4, z: 4, core: 2. Of those that a mesh axis runs over, the one named last changes fastest.
Arguments:
- hidden_in: bfloat16 [6144, 2048], P('seq'), may hold values from -6 to 6
- w_query: bfloat16 [2048, 2048], P(None, 'hg'), may hold values from -0.125 to 0.125
- w_key: bfloat16 [2048, 2048], P(None, 'hg'), may hold values from -0.125 to 0.125
- w_value: bfloat16 [2048, 4096], P(None, 'hg'), may hold values from -0.125 to 0.125
- w_zgate: bfloat16 [2048, 4096], P(None, 'hg'), may hold values from -0.125 to 0.125
- w_decay: bfloat16 [2048, 32], P(None, 'hg'), may hold values from -0.125 to 0.125
- w_beta: bfloat16 [2048, 32], P(None, 'hg'), may hold values from -0.125 to 0.125
- conv_query: bfloat16 [4, 2048], P(None, 'hg'), may hold values from -3 to 3
- conv_key: bfloat16 [4, 2048], P(None, 'hg'), may hold values from -3 to 3
- conv_value: bfloat16 [4, 4096], P(None, 'hg'), may hold values from -3 to 3
- a_log: float32 [32], P('hg'), may hold values from -2 to 1
- dt_bias: float32 [32], P('hg'), may hold values from -9 to -3
- norm_gain: float32 [128], replicated, may hold values from 0.5 to 1.5
- w_out: bfloat16 [4096, 2048], P('hg'), may hold values from -0.09375 to 0.09375
Outputs:
- mixer_out: bfloat16 [6144, 2048], P(('seq', 'hg'))
The draws below stay inside these ranges and needn't reach their ends.
All inputs are finite; a program needn't handle non-finite values.
Results may differ from the reference program's by a relative error of at most 0.02.
Values may be sent and summed in bfloat16 or wider, within the bound.
A program may use at most 128 MiB of HBM per device.

```python
import jax
import jax.numpy as jnp
from jax import lax

D = 2048
VH = 32
KH = 16
DK = 128
DV = 128
KCONV = 4
SPAN = 64
TOKENS = 6144
N_HG = 8


def shard_levels(key, shape, split, least, high):
    factor_of = 1.0
    for dim, shards_of in split:
        steps = jax.random.uniform(jax.random.fold_in(jax.random.fold_in(key, 6), dim), (shards_of,), jnp.float32, least / len(split), high / len(split))
        factor_of = factor_of * jnp.repeat(jnp.exp(steps), shape[dim] // shards_of).reshape((-1,) + (1,) * (len(shape) - 1 - dim))
    return factor_of


def noise(stream_key, extent, width, limit, pieces=(), kind=jnp.bfloat16):
    loudness = shard_levels(stream_key, extent, pieces, -0.22, 0.18) if pieces else 1.0
    result = jax.random.normal(stream_key, extent, jnp.float32) * width * loudness
    return jnp.minimum(jnp.maximum(result, -limit), limit).astype(kind)


def setup_inputs(seed: int = 0) -> dict:
    keys = jax.random.split(jax.random.key(seed), 15)
    return {
        "hidden_in": noise(keys[0], (TOKENS, D), 1.0, 6.0, ((0, 16),)),
        "w_query": noise(keys[1], (D, KH * DK), D ** -0.5, 0.125, ((1, 8),)),
        "w_key": noise(keys[2], (D, KH * DK), D ** -0.5, 0.125, ((1, 8),)),
        "w_value": noise(keys[3], (D, VH * DV), D ** -0.5, 0.125, ((1, 8),)),
        "w_zgate": noise(keys[4], (D, VH * DV), D ** -0.5, 0.125, ((1, 8),)),
        "w_decay": noise(keys[5], (D, VH), D ** -0.5, 0.125, ((1, 8),)),
        "w_beta": noise(keys[6], (D, VH), D ** -0.5, 0.125, ((1, 8),)),
        "conv_query": noise(keys[7], (KCONV, KH * DK), KCONV ** -0.5, 3.0, ((1, 8),)),
        "conv_key": noise(keys[8], (KCONV, KH * DK), KCONV ** -0.5, 3.0, ((1, 8),)),
        "conv_value": noise(keys[9], (KCONV, VH * DV), KCONV ** -0.5, 3.0, ((1, 8),)),
        "a_log": jnp.clip(-2.0 + 3.0 * jax.random.uniform(keys[10], (VH,), jnp.float32) ** shard_levels(keys[10], (VH,), ((0, 8),), -0.2, 0.2), -2.0, 1.0),
        "dt_bias": jnp.clip(-9.0 + 6.0 * jax.random.uniform(keys[11], (VH,), jnp.float32) ** shard_levels(keys[11], (VH,), ((0, 8),), -0.2, 0.2), -9.0, -3.0),
        "norm_gain": jnp.clip(1.0 + 0.1 * jax.random.normal(keys[12], (DV,), jnp.float32), 0.5, 1.5),
        "w_out": noise(keys[13], (VH * DV, D), (VH * DV) ** -0.5, 0.09375, ((0, 8),)),
    }


highest = lax.Precision.HIGHEST
norm_eps = 1e-06

def project_inputs(hidden_in, w_query, w_key, w_value):
    pre_query = jnp.dot(hidden_in.astype(jnp.float32), w_query.astype(jnp.float32), preferred_element_type=jnp.float32).astype(jnp.bfloat16)
    pre_key = jnp.dot(hidden_in.astype(jnp.float32), w_key.astype(jnp.float32), preferred_element_type=jnp.float32).astype(jnp.bfloat16)
    pre_value = jnp.dot(hidden_in.astype(jnp.float32), w_value.astype(jnp.float32), preferred_element_type=jnp.float32).astype(jnp.bfloat16)
    return (pre_query, pre_key, pre_value)

def conv_silu(projected, kernel, prior):
    kernel_len = kernel.shape[0]
    tok_rows = projected.shape[0]
    padded = jnp.concatenate([prior.astype(jnp.float32), projected.astype(jnp.float32)], axis=0)
    summed = jnp.zeros((tok_rows, projected.shape[1]), jnp.float32)
    for offset in range(kernel_len):
        summed = summed + kernel[offset].astype(jnp.float32) * padded[offset:offset + tok_rows]
    return jax.nn.silu(summed)

def unit_length(vectors):
    return vectors * lax.rsqrt(lax.optimization_barrier(jnp.sum(vectors * vectors, axis=-1, keepdims=True)) + norm_eps)

def mixer_inputs(hidden_in, pre_query, pre_key, pre_value, prior, conv_query, conv_key, conv_value, w_zgate, w_decay, w_beta, a_log, dt_bias):
    tok_rows = hidden_in.shape[0]
    query_cols = pre_query.shape[1]
    key_cols = pre_key.shape[1]
    ratio = VH // KH
    queries = unit_length(conv_silu(pre_query, conv_query, prior[:, :query_cols]).reshape(tok_rows, -1, DK)) * DK ** (-0.5)
    key_vecs = unit_length(conv_silu(pre_key, conv_key, prior[:, query_cols:query_cols + key_cols]).reshape(tok_rows, -1, DK))
    values = conv_silu(pre_value, conv_value, prior[:, query_cols + key_cols:]).reshape(tok_rows, -1, DV)
    queries = jnp.repeat(queries, ratio, axis=1)
    key_vecs = jnp.repeat(key_vecs, ratio, axis=1)
    zgate = jnp.dot(hidden_in.astype(jnp.float32), w_zgate.astype(jnp.float32), preferred_element_type=jnp.float32).astype(jnp.bfloat16)
    rate_logits = jnp.dot(hidden_in.astype(jnp.float32), w_decay.astype(jnp.float32), preferred_element_type=jnp.float32)
    log_decay = -jnp.exp(a_log) * jax.nn.softplus(rate_logits + dt_bias)
    write_rate = jax.nn.sigmoid(jnp.dot(hidden_in.astype(jnp.float32), w_beta.astype(jnp.float32), preferred_element_type=jnp.float32))
    return (queries, key_vecs, values, log_decay, write_rate, zgate)

def to_blocks(array_3d):
    tok_rows, head_count = (array_3d.shape[0], array_3d.shape[1])
    return array_3d.reshape(tok_rows // SPAN, SPAN, head_count, -1).transpose(0, 2, 1, 3)

def span_terms(queries, key_vecs, values, log_decay, write_rate):
    block_len = log_decay.shape[-1]
    cum_decay = jnp.cumsum(log_decay, axis=-1)
    row_ids = lax.broadcasted_iota(jnp.int32, (block_len, block_len), 0)
    col_ids = lax.broadcasted_iota(jnp.int32, (block_len, block_len), 1)
    inclusive = row_ids >= col_ids
    strict = row_ids > col_ids
    gap_mat = cum_decay[..., :, None] - cum_decay[..., None, :]
    falloff = jnp.where(inclusive, jnp.exp(jnp.where(inclusive, gap_mat, 0.0)), 0.0)
    key_dots = jnp.einsum('...sd,...td->...st', key_vecs, key_vecs, precision=highest)
    lower_part = jnp.where(strict, write_rate[..., :, None] * falloff * key_dots, 0.0)
    unit_lower = lower_part + jnp.eye(block_len, dtype=jnp.float32)
    wy_keys = lax.linalg.triangular_solve(unit_lower, (write_rate * jnp.exp(cum_decay))[..., None] * key_vecs, left_side=True, lower=True, unit_diagonal=True)
    wy_values = lax.linalg.triangular_solve(unit_lower, write_rate[..., None] * values, left_side=True, lower=True, unit_diagonal=True)
    scores = falloff * jnp.einsum('...sd,...td->...st', queries, key_vecs, precision=highest)
    tail_keys = jnp.exp(cum_decay[..., -1:] - cum_decay)[..., None] * key_vecs
    whole_decay = jnp.exp(cum_decay[..., -1])[..., None, None]
    transition = whole_decay * jnp.eye(key_vecs.shape[-1], dtype=jnp.float32) - jnp.einsum('...sd,...se->...de', tail_keys, wy_keys, precision=highest)
    written = jnp.einsum('...sd,...se->...de', tail_keys, wy_values, precision=highest)
    carry_map = jnp.exp(cum_decay)[..., None] * queries - jnp.einsum('...st,...td->...sd', scores, wy_keys, precision=highest)
    local_out = jnp.einsum('...st,...te->...se', scores, wy_values, precision=highest)
    return (transition, written, carry_map, local_out)

def gated_output(produced, zgate, norm_gain):
    tok_rows = produced.shape[0]
    mean_sq = lax.optimization_barrier(jnp.mean(produced * produced, axis=-1, keepdims=True))
    gate_vals = jax.nn.silu(zgate.astype(jnp.float32).reshape(produced.shape))
    normed = produced * lax.rsqrt(mean_sq + norm_eps) * norm_gain * gate_vals
    return normed.reshape(tok_rows, -1).astype(jnp.bfloat16)

def advance(state_now, per_span):
    transition, written, carry_map, local_out = per_span
    produced = jnp.einsum('hsd,hde->hse', carry_map, state_now, precision=highest) + local_out
    state_next = jnp.einsum('hde,hef->hdf', transition, state_now, precision=highest) + written
    return (state_next, produced)

def reference(hidden_in, w_query, w_key, w_value, w_zgate, w_decay, w_beta, conv_query, conv_key, conv_value, a_log, dt_bias, norm_gain, w_out):
    tok_rows = hidden_in.shape[0]
    pre_query, pre_key, pre_value = project_inputs(hidden_in, w_query, w_key, w_value)
    kernel_len = conv_query.shape[0]
    prior = jnp.zeros((kernel_len - 1, pre_query.shape[1] + pre_key.shape[1] + pre_value.shape[1]), jnp.bfloat16)
    queries, key_vecs, values, log_decay, write_rate, zgate = mixer_inputs(hidden_in, pre_query, pre_key, pre_value, prior, conv_query, conv_key, conv_value, w_zgate, w_decay, w_beta, a_log, dt_bias)
    terms = span_terms(to_blocks(queries), to_blocks(key_vecs), to_blocks(values), to_blocks(log_decay[..., None])[..., 0], to_blocks(write_rate[..., None])[..., 0])
    start_state = jnp.zeros((VH, DK, DV), jnp.float32)
    final_state, produced = lax.scan(advance, start_state, terms)
    produced = produced.transpose(0, 2, 1, 3).reshape(tok_rows, VH, DV)
    gated = gated_output(produced, zgate, norm_gain)
    group_cols = VH * DV // N_HG
    summed = jnp.zeros((tok_rows, w_out.shape[1]), jnp.float32)
    for group_index in range(N_HG):
        lo_col = group_index * group_cols
        part_out = jnp.dot(gated[:, lo_col:lo_col + group_cols].astype(jnp.float32), w_out[lo_col:lo_col + group_cols].astype(jnp.float32), preferred_element_type=jnp.float32).astype(jnp.bfloat16)
        summed = summed + lax.optimization_barrier(part_out).astype(jnp.float32)
    return summed.astype(jnp.bfloat16)
```

```python
import jax
import numpy as np
import jax.numpy as jnp
from jax import lax
from jax.sharding import PartitionSpec as P

VH = 32
KH = 16
DK = 128
DV = 128
SPAN = 64


highest = lax.Precision.HIGHEST
norm_eps = 1e-06


def passed_along(block, axis, distance):
    devices = range(lax.axis_size(axis))
    route = [(i - distance, i) for i in devices if i - distance in devices]
    return lax.ppermute(block, axis, route)


def project_inputs(hidden_in, w_query, w_key, w_value):
    pre_query = jnp.dot(hidden_in, w_query, preferred_element_type=jnp.float32).astype(jnp.bfloat16)
    pre_key = jnp.dot(hidden_in, w_key, preferred_element_type=jnp.float32).astype(jnp.bfloat16)
    pre_value = jnp.dot(hidden_in, w_value, preferred_element_type=jnp.float32).astype(jnp.bfloat16)
    return (pre_query, pre_key, pre_value)


def conv_silu(projected, kernel, prior):
    kernel_len = kernel.shape[0]
    tok_rows = projected.shape[0]
    padded = jnp.concatenate([prior.astype(jnp.float32), projected.astype(jnp.float32)], axis=0)
    summed = jnp.zeros((tok_rows, projected.shape[1]), jnp.float32)
    for offset in range(kernel_len):
        summed = summed + kernel[offset].astype(jnp.float32) * padded[offset : offset + tok_rows]
    return jax.nn.silu(summed)


def unit_length(vectors):
    return vectors * lax.rsqrt(jnp.sum(vectors * vectors, axis=-1, keepdims=True) + norm_eps)


def mixer_inputs(
    hidden_in,
    pre_query,
    pre_key,
    pre_value,
    prior,
    conv_query,
    conv_key,
    conv_value,
    w_zgate,
    w_decay,
    w_beta,
    a_log,
    dt_bias,
):
    tok_rows = hidden_in.shape[0]
    query_cols = pre_query.shape[1]
    key_cols = pre_key.shape[1]
    ratio = VH // KH
    queries = unit_length(
        conv_silu(pre_query, conv_query, prior[:, :query_cols]).reshape(tok_rows, -1, DK)
    ) * DK ** (-0.5)
    key_vecs = unit_length(
        conv_silu(pre_key, conv_key, prior[:, query_cols : query_cols + key_cols]).reshape(
            tok_rows, -1, DK
        )
    )
    values = conv_silu(pre_value, conv_value, prior[:, query_cols + key_cols :]).reshape(
        tok_rows, -1, DV
    )
    queries = jnp.repeat(queries, ratio, axis=1)
    key_vecs = jnp.repeat(key_vecs, ratio, axis=1)
    zgate = jnp.dot(hidden_in, w_zgate, preferred_element_type=jnp.float32).astype(jnp.bfloat16)
    rate_logits = jnp.dot(hidden_in, w_decay, preferred_element_type=jnp.float32)
    log_decay = -jnp.exp(a_log) * jax.nn.softplus(rate_logits + dt_bias)
    write_rate = jax.nn.sigmoid(jnp.dot(hidden_in, w_beta, preferred_element_type=jnp.float32))
    return (queries, key_vecs, values, log_decay, write_rate, zgate)


def to_blocks(array_3d):
    tok_rows, head_count = (array_3d.shape[0], array_3d.shape[1])
    return array_3d.reshape(tok_rows // SPAN, SPAN, head_count, -1).transpose(0, 2, 1, 3)


def unit_lower_inverse(lower_part):
    block_len = lower_part.shape[-1]
    row_ids = np.arange(block_len)[:, None]
    col_ids = np.arange(block_len)[None, :]
    first = jnp.asarray((row_ids // 2 == col_ids // 2) & (row_ids != col_ids), jnp.float32)
    inverse = lax.optimization_barrier(
        jnp.asarray(np.eye(block_len), jnp.float32) - lower_part * first
    )
    size = 2
    while size < block_len:
        band = (row_ids // (2 * size) == col_ids // (2 * size)) & (row_ids // size != col_ids // size)
        off_blocks = lower_part * jnp.asarray(band, jnp.float32)
        step = jnp.einsum("...st,...tu->...su", inverse, off_blocks, precision=highest)
        inverse = inverse - jnp.einsum("...st,...tu->...su", step, inverse, precision=highest)
        size *= 2
    return inverse


def span_terms(queries, key_vecs, values, log_decay, write_rate):
    block_len = log_decay.shape[-1]
    cum_decay = jnp.cumsum(log_decay, axis=-1)
    row_ids = lax.broadcasted_iota(jnp.int32, (block_len, block_len), 0)
    col_ids = lax.broadcasted_iota(jnp.int32, (block_len, block_len), 1)
    inclusive = row_ids >= col_ids
    strict = row_ids > col_ids
    gap_mat = cum_decay[..., :, None] - cum_decay[..., None, :]
    falloff = jnp.where(inclusive, jnp.exp(jnp.where(inclusive, gap_mat, 0.0)), 0.0)
    key_dots = jnp.einsum("...sd,...td->...st", key_vecs, key_vecs, precision=highest)
    lower_part = jnp.where(strict, write_rate[..., :, None] * falloff * key_dots, 0.0)
    inverse = unit_lower_inverse(lower_part)
    wy_keys = jnp.einsum(
        "...st,...td->...sd",
        inverse,
        (write_rate * jnp.exp(cum_decay))[..., None] * key_vecs,
        precision=highest,
    )
    wy_values = jnp.einsum(
        "...st,...td->...sd", inverse, write_rate[..., None] * values, precision=highest
    )
    scores = falloff * jnp.einsum("...sd,...td->...st", queries, key_vecs, precision=highest)
    tail_keys = jnp.exp(cum_decay[..., -1:] - cum_decay)[..., None] * key_vecs
    whole_decay = jnp.exp(cum_decay[..., -1])[..., None, None]
    transition = whole_decay * jnp.eye(key_vecs.shape[-1], dtype=jnp.float32) - jnp.einsum(
        "...sd,...se->...de", tail_keys, wy_keys, precision=highest
    )
    written = jnp.einsum("...sd,...se->...de", tail_keys, wy_values, precision=highest)
    carry_map = jnp.exp(cum_decay)[..., None] * queries - jnp.einsum(
        "...st,...td->...sd", scores, wy_keys, precision=highest
    )
    local_out = jnp.einsum("...st,...te->...se", scores, wy_values, precision=highest)
    return (transition, written, carry_map, local_out)


def gated_output(produced, zgate, norm_gain):
    tok_rows = produced.shape[0]
    mean_sq = jnp.mean(produced * produced, axis=-1, keepdims=True)
    gate_vals = jax.nn.silu(zgate.astype(jnp.float32).reshape(produced.shape))
    normed = produced * lax.rsqrt(mean_sq + norm_eps) * norm_gain * gate_vals
    return normed.reshape(tok_rows, -1).astype(jnp.bfloat16)


def advance(state_now, per_span):
    transition, written, carry_map, local_out = per_span
    produced = jnp.einsum("hsd,hde->hse", carry_map, state_now, precision=highest) + local_out
    state_next = jnp.einsum("hde,hef->hdf", transition, state_now, precision=highest) + written
    return (state_next, produced)


def apply_shard(trans_mat, state_now, written):
    return jnp.einsum("hde,hef->hdf", trans_mat, state_now, precision=highest) + written


def on_device(
    hidden_in,
    w_query,
    w_key,
    w_value,
    w_zgate,
    w_decay,
    w_beta,
    conv_query,
    conv_key,
    conv_value,
    a_log,
    dt_bias,
    norm_gain,
    w_out,
):
    tok_rows = hidden_in.shape[0]
    pre_query, pre_key, pre_value = project_inputs(hidden_in, w_query, w_key, w_value)
    kernel_len = conv_query.shape[0]
    rim_rows = tok_rows - kernel_len + 1
    rim_block = jnp.concatenate(
        [pre_query[rim_rows:], pre_key[rim_rows:], pre_value[rim_rows:]], axis=1
    )
    prior = passed_along(rim_block, "seq", 1)
    queries, key_vecs, values, log_decay, write_rate, zgate = mixer_inputs(
        hidden_in,
        pre_query,
        pre_key,
        pre_value,
        prior,
        conv_query,
        conv_key,
        conv_value,
        w_zgate,
        w_decay,
        w_beta,
        a_log,
        dt_bias,
    )
    terms = span_terms(
        to_blocks(queries),
        to_blocks(key_vecs),
        to_blocks(values),
        to_blocks(log_decay[..., None])[..., 0],
        to_blocks(write_rate[..., None])[..., 0],
    )
    head_count = values.shape[1]
    identity = jnp.broadcast_to(jnp.eye(DK, dtype=jnp.float32), (head_count, DK, DK))
    empty_state = jnp.zeros((head_count, DK, DV), jnp.float32)

    def compose(carried, per_span):
        prefix_a, prefix_b = carried
        step_trans, step_written, step_carry, step_local = per_span
        local_mix = (
            jnp.einsum("hsd,hde->hse", step_carry, prefix_b, precision=highest) + step_local
        )
        entry_map = jnp.einsum("hsd,hde->hse", step_carry, prefix_a, precision=highest)
        new_a = jnp.einsum("hde,hef->hdf", step_trans, prefix_a, precision=highest)
        new_b = apply_shard(step_trans, prefix_b, step_written)
        return ((new_a, new_b), (local_mix, entry_map))

    (shard_a, shard_b), (local_mix, entry_map) = lax.scan(
        compose, (identity, empty_state), terms
    )

    shard_count = lax.axis_size("seq")
    shard_index = lax.axis_index("seq")
    acc_a, acc_b = shard_a, shard_b
    distance = 1
    while distance < shard_count:
        has_prev = shard_index >= distance
        prev_b = passed_along(acc_b, "seq", distance)
        new_b = jnp.where(has_prev, apply_shard(acc_a, prev_b, acc_b), acc_b)
        if 2 * distance < shard_count:
            prev_a = passed_along(acc_a, "seq", distance)
            acc_a = jnp.where(
                has_prev,
                jnp.einsum("hde,hef->hdf", acc_a, prev_a, precision=highest),
                acc_a,
            )
        acc_b = new_b
        distance *= 2
    state_in = passed_along(acc_b, "seq", 1)
    produced = local_mix + jnp.einsum("jhsd,hde->jhse", entry_map, state_in, precision=highest)
    produced = produced.transpose(0, 2, 1, 3).reshape(tok_rows, head_count, DV)
    gated = gated_output(produced, zgate, norm_gain)
    return lax.psum_scatter(
        jnp.dot(gated, w_out, preferred_element_type=jnp.float32).astype(jnp.bfloat16),
        "hg",
        scatter_dimension=0,
        tiled=True,
    )


def solution(mesh):
    return jax.shard_map(
        on_device,
        mesh=mesh,
        in_specs=(
            P("seq", None),
            P(None, "hg"),
            P(None, "hg"),
            P(None, "hg"),
            P(None, "hg"),
            P(None, "hg"),
            P(None, "hg"),
            P(None, "hg"),
            P(None, "hg"),
            P(None, "hg"),
            P("hg"),
            P("hg"),
            P(),
            P("hg", None),
        ),
        out_specs=P(("seq", "hg"), None),
        check_vma=False,
    )
```

```python
import functools

import jax
import numpy as np
import jax.numpy as jnp
from jax import lax
from jax.experimental import pallas as pl
from jax.experimental.pallas import tpu as pltpu
from jax.sharding import PartitionSpec as P

MESH = pl.DeviceIdType.MESH

VH = 32
KH = 16
DK = 128
DV = 128
SPAN = 64


highest = lax.Precision.HIGHEST
norm_eps = 1e-06


def passed_along(block, axis, distance):
    devices = range(lax.axis_size(axis))
    route = [(i - distance, i) for i in devices if i - distance in devices]
    return lax.ppermute(block, axis, route)


def project_inputs(hidden_in, w_query, w_key, w_value):
    pre_query = jnp.dot(hidden_in, w_query, preferred_element_type=jnp.float32).astype(jnp.bfloat16)
    pre_key = jnp.dot(hidden_in, w_key, preferred_element_type=jnp.float32).astype(jnp.bfloat16)
    pre_value = jnp.dot(hidden_in, w_value, preferred_element_type=jnp.float32).astype(jnp.bfloat16)
    return (pre_query, pre_key, pre_value)


def conv_silu(projected, kernel, prior):
    kernel_len = kernel.shape[0]
    tok_rows = projected.shape[0]
    padded = jnp.concatenate([prior.astype(jnp.float32), projected.astype(jnp.float32)], axis=0)
    summed = jnp.zeros((tok_rows, projected.shape[1]), jnp.float32)
    for offset in range(kernel_len):
        summed = summed + kernel[offset].astype(jnp.float32) * padded[offset : offset + tok_rows]
    return jax.nn.silu(summed)


def unit_length(vectors):
    return vectors * lax.rsqrt(jnp.sum(vectors * vectors, axis=-1, keepdims=True) + norm_eps)


def mixer_inputs(
    hidden_in,
    pre_query,
    pre_key,
    pre_value,
    prior,
    conv_query,
    conv_key,
    conv_value,
    w_zgate,
    w_decay,
    w_beta,
    a_log,
    dt_bias,
):
    tok_rows = hidden_in.shape[0]
    query_cols = pre_query.shape[1]
    key_cols = pre_key.shape[1]
    ratio = VH // KH
    queries = unit_length(
        conv_silu(pre_query, conv_query, prior[:, :query_cols]).reshape(tok_rows, -1, DK)
    ) * DK ** (-0.5)
    key_vecs = unit_length(
        conv_silu(pre_key, conv_key, prior[:, query_cols : query_cols + key_cols]).reshape(
            tok_rows, -1, DK
        )
    )
    values = conv_silu(pre_value, conv_value, prior[:, query_cols + key_cols :]).reshape(
        tok_rows, -1, DV
    )
    queries = jnp.repeat(queries, ratio, axis=1)
    key_vecs = jnp.repeat(key_vecs, ratio, axis=1)
    zgate = jnp.dot(hidden_in, w_zgate, preferred_element_type=jnp.float32).astype(jnp.bfloat16)
    rate_logits = jnp.dot(hidden_in, w_decay, preferred_element_type=jnp.float32)
    log_decay = -jnp.exp(a_log) * jax.nn.softplus(rate_logits + dt_bias)
    write_rate = jax.nn.sigmoid(jnp.dot(hidden_in, w_beta, preferred_element_type=jnp.float32))
    return (queries, key_vecs, values, log_decay, write_rate, zgate)


def to_blocks(array_3d):
    tok_rows, head_count = (array_3d.shape[0], array_3d.shape[1])
    return array_3d.reshape(tok_rows // SPAN, SPAN, head_count, -1).transpose(0, 2, 1, 3)


def unit_lower_inverse(lower_part):
    block_len = lower_part.shape[-1]
    row_ids = np.arange(block_len)[:, None]
    col_ids = np.arange(block_len)[None, :]
    first = jnp.asarray((row_ids // 2 == col_ids // 2) & (row_ids != col_ids), jnp.float32)
    inverse = lax.optimization_barrier(
        jnp.asarray(np.eye(block_len), jnp.float32) - lower_part * first
    )
    size = 2
    while size < block_len:
        band = (row_ids // (2 * size) == col_ids // (2 * size)) & (row_ids // size != col_ids // size)
        off_blocks = lower_part * jnp.asarray(band, jnp.float32)
        step = jnp.einsum("...st,...tu->...su", inverse, off_blocks, precision=highest)
        inverse = inverse - jnp.einsum("...st,...tu->...su", step, inverse, precision=highest)
        size *= 2
    return inverse


def span_terms(queries, key_vecs, values, log_decay, write_rate):
    block_len = log_decay.shape[-1]
    cum_decay = jnp.cumsum(log_decay, axis=-1)
    row_ids = lax.broadcasted_iota(jnp.int32, (block_len, block_len), 0)
    col_ids = lax.broadcasted_iota(jnp.int32, (block_len, block_len), 1)
    inclusive = row_ids >= col_ids
    strict = row_ids > col_ids
    gap_mat = cum_decay[..., :, None] - cum_decay[..., None, :]
    falloff = jnp.where(inclusive, jnp.exp(jnp.where(inclusive, gap_mat, 0.0)), 0.0)
    key_dots = jnp.einsum("...sd,...td->...st", key_vecs, key_vecs, precision=highest)
    lower_part = jnp.where(strict, write_rate[..., :, None] * falloff * key_dots, 0.0)
    inverse = unit_lower_inverse(lower_part)
    wy_keys = jnp.einsum(
        "...st,...td->...sd",
        inverse,
        (write_rate * jnp.exp(cum_decay))[..., None] * key_vecs,
        precision=highest,
    )
    wy_values = jnp.einsum(
        "...st,...td->...sd", inverse, write_rate[..., None] * values, precision=highest
    )
    scores = falloff * jnp.einsum("...sd,...td->...st", queries, key_vecs, precision=highest)
    tail_keys = jnp.exp(cum_decay[..., -1:] - cum_decay)[..., None] * key_vecs
    whole_decay = jnp.exp(cum_decay[..., -1])[..., None, None]
    transition = whole_decay * jnp.eye(key_vecs.shape[-1], dtype=jnp.float32) - jnp.einsum(
        "...sd,...se->...de", tail_keys, wy_keys, precision=highest
    )
    written = jnp.einsum("...sd,...se->...de", tail_keys, wy_values, precision=highest)
    carry_map = jnp.exp(cum_decay)[..., None] * queries - jnp.einsum(
        "...st,...td->...sd", scores, wy_keys, precision=highest
    )
    local_out = jnp.einsum("...st,...te->...se", scores, wy_values, precision=highest)
    return (transition, written, carry_map, local_out)


def gated_output(produced, zgate, norm_gain):
    tok_rows = produced.shape[0]
    mean_sq = jnp.mean(produced * produced, axis=-1, keepdims=True)
    gate_vals = jax.nn.silu(zgate.astype(jnp.float32).reshape(produced.shape))
    normed = produced * lax.rsqrt(mean_sq + norm_eps) * norm_gain * gate_vals
    return normed.reshape(tok_rows, -1).astype(jnp.bfloat16)


def advance(state_now, per_span):
    transition, written, carry_map, local_out = per_span
    produced = jnp.einsum("hsd,hde->hse", carry_map, state_now, precision=highest) + local_out
    state_next = jnp.einsum("hde,hef->hdf", transition, state_now, precision=highest) + written
    return (state_next, produced)


def apply_shard(trans_mat, state_now, written):
    return jnp.einsum("hde,hef->hdf", trans_mat, state_now, precision=highest) + written


def group_sum_kernel(group_count, part_ref, out_ref, landed, send_sems, recv_sems, own_sem):
    me = lax.axis_index("hg")
    seq_me = lax.axis_index("seq")
    rows = out_ref.shape[0]
    barrier = pltpu.get_barrier_semaphore()
    for step in range(1, group_count):
        peer = lax.rem(me + step, group_count)
        pl.semaphore_signal(barrier, inc=1, device_id=(seq_me, peer), device_id_type=MESH)
    pl.semaphore_wait(barrier, group_count - 1)
    sends = []
    for step in range(1, group_count):
        peer = lax.rem(me + step, group_count)
        copy = pltpu.make_async_remote_copy(
            src_ref=part_ref.at[pl.ds(pl.multiple_of(peer * rows, 8), rows)],
            dst_ref=landed.at[me],
            send_sem=send_sems.at[step],
            recv_sem=recv_sems.at[me],
            device_id=(seq_me, peer),
            device_id_type=MESH,
        )
        copy.start()
        sends.append(copy)
    own = pltpu.make_async_copy(
        part_ref.at[pl.ds(pl.multiple_of(me * rows, 8), rows)], landed.at[me], own_sem
    )
    own.start()
    own.wait()
    for step in range(1, group_count):
        source = lax.rem(me + group_count - step, group_count)
        pltpu.make_async_remote_copy(
            src_ref=part_ref.at[pl.ds(0, rows)],
            dst_ref=landed.at[source],
            send_sem=send_sems.at[step],
            recv_sem=recv_sems.at[source],
            device_id=(seq_me, source),
            device_id_type=MESH,
        ).wait_recv()
    for copy in sends:
        copy.wait_send()
    total = landed[0].astype(jnp.float32)
    for slot in range(1, group_count):
        total = total + landed[slot].astype(jnp.float32)
    out_ref[...] = total.astype(out_ref.dtype)


def group_sum(part, group_count):
    rows = part.shape[0] // group_count
    cols = part.shape[1]
    return pl.pallas_call(
        functools.partial(group_sum_kernel, group_count),
        out_shape=jax.ShapeDtypeStruct((rows, cols), part.dtype),
        in_specs=[pl.BlockSpec(memory_space=pltpu.VMEM)],
        out_specs=pl.BlockSpec(memory_space=pltpu.VMEM),
        scratch_shapes=[
            pltpu.VMEM((group_count, rows, cols), part.dtype),
            pltpu.SemaphoreType.DMA((group_count,)),
            pltpu.SemaphoreType.DMA((group_count,)),
            pltpu.SemaphoreType.DMA,
        ],
        compiler_params=pltpu.CompilerParams(collective_id=0, has_side_effects=True),
    )(part)


def on_device(
    hidden_in,
    w_query,
    w_key,
    w_value,
    w_zgate,
    w_decay,
    w_beta,
    conv_query,
    conv_key,
    conv_value,
    a_log,
    dt_bias,
    norm_gain,
    w_out,
):
    tok_rows = hidden_in.shape[0]
    pre_query, pre_key, pre_value = project_inputs(hidden_in, w_query, w_key, w_value)
    kernel_len = conv_query.shape[0]
    rim_rows = tok_rows - kernel_len + 1
    rim_block = jnp.concatenate(
        [pre_query[rim_rows:], pre_key[rim_rows:], pre_value[rim_rows:]], axis=1
    )
    prior = passed_along(rim_block, "seq", 1)
    queries, key_vecs, values, log_decay, write_rate, zgate = mixer_inputs(
        hidden_in,
        pre_query,
        pre_key,
        pre_value,
        prior,
        conv_query,
        conv_key,
        conv_value,
        w_zgate,
        w_decay,
        w_beta,
        a_log,
        dt_bias,
    )
    terms = span_terms(
        to_blocks(queries),
        to_blocks(key_vecs),
        to_blocks(values),
        to_blocks(log_decay[..., None])[..., 0],
        to_blocks(write_rate[..., None])[..., 0],
    )
    head_count = values.shape[1]
    identity = jnp.broadcast_to(jnp.eye(DK, dtype=jnp.float32), (head_count, DK, DK))
    empty_state = jnp.zeros((head_count, DK, DV), jnp.float32)

    def compose(carried, per_span):
        prefix_a, prefix_b = carried
        step_trans, step_written, step_carry, step_local = per_span
        local_mix = (
            jnp.einsum("hsd,hde->hse", step_carry, prefix_b, precision=highest) + step_local
        )
        entry_map = jnp.einsum("hsd,hde->hse", step_carry, prefix_a, precision=highest)
        new_a = jnp.einsum("hde,hef->hdf", step_trans, prefix_a, precision=highest)
        new_b = apply_shard(step_trans, prefix_b, step_written)
        return ((new_a, new_b), (local_mix, entry_map))

    (shard_a, shard_b), (local_mix, entry_map) = lax.scan(
        compose, (identity, empty_state), terms, unroll=True
    )

    shard_count = lax.axis_size("seq")
    shard_index = lax.axis_index("seq")
    acc_a, acc_b = shard_a, shard_b
    distance = 1
    while distance < shard_count:
        has_prev = shard_index >= distance
        prev_b = passed_along(acc_b, "seq", distance)
        new_b = jnp.where(has_prev, apply_shard(acc_a, prev_b, acc_b), acc_b)
        if 2 * distance < shard_count:
            prev_a = passed_along(acc_a, "seq", distance)
            acc_a = jnp.where(
                has_prev,
                jnp.einsum("hde,hef->hdf", acc_a, prev_a, precision=highest),
                acc_a,
            )
        acc_b = new_b
        distance *= 2
    state_in = passed_along(acc_b, "seq", 1)
    produced = local_mix + jnp.einsum("jhsd,hde->jhse", entry_map, state_in, precision=highest)
    produced = produced.transpose(0, 2, 1, 3).reshape(tok_rows, head_count, DV)
    gated = gated_output(produced, zgate, norm_gain)
    part = jnp.dot(gated, w_out, preferred_element_type=jnp.float32).astype(jnp.bfloat16)
    return group_sum(part, lax.axis_size("hg"))


def solution(mesh):
    return jax.shard_map(
        on_device,
        mesh=mesh,
        in_specs=(
            P("seq", None),
            P(None, "hg"),
            P(None, "hg"),
            P(None, "hg"),
            P(None, "hg"),
            P(None, "hg"),
            P(None, "hg"),
            P(None, "hg"),
            P(None, "hg"),
            P(None, "hg"),
            P("hg"),
            P("hg"),
            P(),
            P("hg", None),
        ),
        out_specs=P(("seq", "hg"), None),
        check_vma=False,
    )
```

```python
import functools

import jax
import numpy as np
import jax.numpy as jnp
from jax import lax
from jax.experimental import pallas as pl
from jax.experimental.pallas import tpu as pltpu
from jax.sharding import PartitionSpec as P

MESH = pl.DeviceIdType.MESH

VH = 32
KH = 16
DK = 128
DV = 128
SPAN = 64


highest = lax.Precision.HIGHEST
norm_eps = 1e-06


def passed_along(block, axis, distance):
    devices = range(lax.axis_size(axis))
    route = [(i - distance, i) for i in devices if i - distance in devices]
    return lax.ppermute(block, axis, route)


def project_inputs(hidden_in, w_query, w_key, w_value):
    pre_query = jnp.dot(hidden_in, w_query, preferred_element_type=jnp.float32).astype(jnp.bfloat16)
    pre_key = jnp.dot(hidden_in, w_key, preferred_element_type=jnp.float32).astype(jnp.bfloat16)
    pre_value = jnp.dot(hidden_in, w_value, preferred_element_type=jnp.float32).astype(jnp.bfloat16)
    return (pre_query, pre_key, pre_value)


def conv_silu(projected, kernel, prior):
    kernel_len = kernel.shape[0]
    tok_rows = projected.shape[0]
    padded = jnp.concatenate([prior.astype(jnp.float32), projected.astype(jnp.float32)], axis=0)
    summed = jnp.zeros((tok_rows, projected.shape[1]), jnp.float32)
    for offset in range(kernel_len):
        summed = summed + kernel[offset].astype(jnp.float32) * padded[offset : offset + tok_rows]
    return jax.nn.silu(summed)


def unit_length(vectors):
    return vectors * lax.rsqrt(jnp.sum(vectors * vectors, axis=-1, keepdims=True) + norm_eps)


def mixer_inputs(
    hidden_in,
    pre_query,
    pre_key,
    pre_value,
    prior,
    conv_query,
    conv_key,
    conv_value,
    w_zgate,
    w_decay,
    w_beta,
    a_log,
    dt_bias,
):
    tok_rows = hidden_in.shape[0]
    query_cols = pre_query.shape[1]
    key_cols = pre_key.shape[1]
    ratio = VH // KH
    queries = unit_length(
        conv_silu(pre_query, conv_query, prior[:, :query_cols]).reshape(tok_rows, -1, DK)
    ) * DK ** (-0.5)
    key_vecs = unit_length(
        conv_silu(pre_key, conv_key, prior[:, query_cols : query_cols + key_cols]).reshape(
            tok_rows, -1, DK
        )
    )
    values = conv_silu(pre_value, conv_value, prior[:, query_cols + key_cols :]).reshape(
        tok_rows, -1, DV
    )
    queries = jnp.repeat(queries, ratio, axis=1)
    key_vecs = jnp.repeat(key_vecs, ratio, axis=1)
    zgate = jnp.dot(hidden_in, w_zgate, preferred_element_type=jnp.float32).astype(jnp.bfloat16)
    rate_logits = jnp.dot(hidden_in, w_decay, preferred_element_type=jnp.float32)
    log_decay = -jnp.exp(a_log) * jax.nn.softplus(rate_logits + dt_bias)
    write_rate = jax.nn.sigmoid(jnp.dot(hidden_in, w_beta, preferred_element_type=jnp.float32))
    return (queries, key_vecs, values, log_decay, write_rate, zgate)


def to_blocks(array_3d):
    tok_rows, head_count = (array_3d.shape[0], array_3d.shape[1])
    return array_3d.reshape(tok_rows // SPAN, SPAN, head_count, -1).transpose(0, 2, 1, 3)


def unit_lower_inverse(lower_part):
    block_len = lower_part.shape[-1]
    row_ids = np.arange(block_len)[:, None]
    col_ids = np.arange(block_len)[None, :]
    first = jnp.asarray((row_ids // 2 == col_ids // 2) & (row_ids != col_ids), jnp.float32)
    inverse = lax.optimization_barrier(
        jnp.asarray(np.eye(block_len), jnp.float32) - lower_part * first
    )
    size = 2
    while size < block_len:
        band = (row_ids // (2 * size) == col_ids // (2 * size)) & (row_ids // size != col_ids // size)
        off_blocks = lower_part * jnp.asarray(band, jnp.float32)
        step = jnp.einsum("...st,...tu->...su", inverse, off_blocks, precision=highest)
        inverse = inverse - jnp.einsum("...st,...tu->...su", step, inverse, precision=highest)
        size *= 2
    return inverse


def span_terms(queries, key_vecs, values, log_decay, write_rate):
    block_len = log_decay.shape[-1]
    cum_decay = jnp.cumsum(log_decay, axis=-1)
    row_ids = lax.broadcasted_iota(jnp.int32, (block_len, block_len), 0)
    col_ids = lax.broadcasted_iota(jnp.int32, (block_len, block_len), 1)
    inclusive = row_ids >= col_ids
    strict = row_ids > col_ids
    gap_mat = cum_decay[..., :, None] - cum_decay[..., None, :]
    falloff = jnp.where(inclusive, jnp.exp(jnp.where(inclusive, gap_mat, 0.0)), 0.0)
    key_dots = jnp.einsum("...sd,...td->...st", key_vecs, key_vecs, precision=highest)
    lower_part = jnp.where(strict, write_rate[..., :, None] * falloff * key_dots, 0.0)
    inverse = unit_lower_inverse(lower_part)
    wy_keys = jnp.einsum(
        "...st,...td->...sd",
        inverse,
        (write_rate * jnp.exp(cum_decay))[..., None] * key_vecs,
        precision=highest,
    )
    wy_values = jnp.einsum(
        "...st,...td->...sd", inverse, write_rate[..., None] * values, precision=highest
    )
    scores = falloff * jnp.einsum("...sd,...td->...st", queries, key_vecs, precision=highest)
    tail_keys = jnp.exp(cum_decay[..., -1:] - cum_decay)[..., None] * key_vecs
    whole_decay = jnp.exp(cum_decay[..., -1])[..., None, None]
    transition = whole_decay * jnp.eye(key_vecs.shape[-1], dtype=jnp.float32) - jnp.einsum(
        "...sd,...se->...de", tail_keys, wy_keys, precision=highest
    )
    written = jnp.einsum("...sd,...se->...de", tail_keys, wy_values, precision=highest)
    carry_map = jnp.exp(cum_decay)[..., None] * queries - jnp.einsum(
        "...st,...td->...sd", scores, wy_keys, precision=highest
    )
    local_out = jnp.einsum("...st,...te->...se", scores, wy_values, precision=highest)
    return (transition, written, carry_map, local_out)


def gated_output(produced, zgate, norm_gain):
    tok_rows = produced.shape[0]
    mean_sq = jnp.mean(produced * produced, axis=-1, keepdims=True)
    gate_vals = jax.nn.silu(zgate.astype(jnp.float32).reshape(produced.shape))
    normed = produced * lax.rsqrt(mean_sq + norm_eps) * norm_gain * gate_vals
    return normed.reshape(tok_rows, -1).astype(jnp.bfloat16)


def advance(state_now, per_span):
    transition, written, carry_map, local_out = per_span
    produced = jnp.einsum("hsd,hde->hse", carry_map, state_now, precision=highest) + local_out
    state_next = jnp.einsum("hde,hef->hdf", transition, state_now, precision=highest) + written
    return (state_next, produced)


def apply_shard(trans_mat, state_now, written):
    return jnp.einsum("hde,hef->hdf", trans_mat, state_now, precision=highest) + written


def shard_scan_kernel(shard_count, a_ref, b_ref, out_ref, cur_a, cur_b, got_a, got_b, send_sems, recv_sems):
    me = lax.axis_index("seq")
    hg_me = lax.axis_index("hg")
    head_count = a_ref.shape[0]
    distances = []
    distance = 1
    while distance < shard_count:
        distances.append(distance)
        distance *= 2
    barrier = pltpu.get_barrier_semaphore()
    for distance in distances:
        for target in (lax.rem(me + distance, shard_count), lax.rem(me + shard_count - distance, shard_count)):
            pl.semaphore_signal(barrier, inc=1, device_id=(target, hg_me), device_id_type=MESH)
    pl.semaphore_wait(barrier, 2 * len(distances))
    cur_a[0] = a_ref[...]
    cur_b[0] = b_ref[...]
    sem_index = 0
    for round_index, distance in enumerate(distances):
        target = lax.rem(me + distance, shard_count)
        sends_a = round_index + 1 < len(distances)
        copies = [
            pltpu.make_async_remote_copy(
                src_ref=cur_b.at[round_index],
                dst_ref=got_b.at[round_index],
                send_sem=send_sems.at[sem_index],
                recv_sem=recv_sems.at[sem_index],
                device_id=(target, hg_me),
                device_id_type=MESH,
            )
        ]
        if sends_a:
            copies.append(
                pltpu.make_async_remote_copy(
                    src_ref=cur_a.at[round_index],
                    dst_ref=got_a.at[round_index],
                    send_sem=send_sems.at[sem_index + 1],
                    recv_sem=recv_sems.at[sem_index + 1],
                    device_id=(target, hg_me),
                    device_id_type=MESH,
                )
            )
        sem_index += len(copies)
        for copy in copies:
            copy.start()
        for copy in copies:
            copy.wait()
        has_prev = me >= distance
        for head in range(head_count):
            own_a = cur_a[round_index, head]
            own_b = cur_b[round_index, head]
            joined_b = (
                jnp.dot(own_a, got_b[round_index, head], precision=highest,
                        preferred_element_type=jnp.float32)
                + own_b
            )
            cur_b[round_index + 1, head] = jnp.where(has_prev, joined_b, own_b)
            if sends_a:
                joined_a = jnp.dot(own_a, got_a[round_index, head], precision=highest,
                                   preferred_element_type=jnp.float32)
                cur_a[round_index + 1, head] = jnp.where(has_prev, joined_a, own_a)
    last = len(distances)
    shift = pltpu.make_async_remote_copy(
        src_ref=cur_b.at[last],
        dst_ref=got_b.at[last],
        send_sem=send_sems.at[sem_index],
        recv_sem=recv_sems.at[sem_index],
        device_id=(lax.rem(me + 1, shard_count), hg_me),
        device_id_type=MESH,
    )
    shift.start()
    shift.wait()
    out_ref[...] = jnp.where(me >= 1, got_b[last], 0.0)


def shard_scan(shard_a, shard_b, shard_count):
    rounds = max(1, (shard_count - 1).bit_length())
    return pl.pallas_call(
        functools.partial(shard_scan_kernel, shard_count),
        out_shape=jax.ShapeDtypeStruct(shard_b.shape, jnp.float32),
        in_specs=[pl.BlockSpec(memory_space=pltpu.VMEM)] * 2,
        out_specs=pl.BlockSpec(memory_space=pltpu.VMEM),
        scratch_shapes=[
            pltpu.VMEM((rounds + 1,) + shard_a.shape, jnp.float32),
            pltpu.VMEM((rounds + 1,) + shard_b.shape, jnp.float32),
            pltpu.VMEM((rounds + 1,) + shard_a.shape, jnp.float32),
            pltpu.VMEM((rounds + 1,) + shard_b.shape, jnp.float32),
            pltpu.SemaphoreType.DMA((2 * rounds + 1,)),
            pltpu.SemaphoreType.DMA((2 * rounds + 1,)),
        ],
        compiler_params=pltpu.CompilerParams(collective_id=1, has_side_effects=True),
    )(shard_a, shard_b)


def group_sum_kernel(group_count, part_ref, out_ref, landed, send_sems, recv_sems, own_sem):
    me = lax.axis_index("hg")
    seq_me = lax.axis_index("seq")
    rows = out_ref.shape[0]
    barrier = pltpu.get_barrier_semaphore()
    for step in range(1, group_count):
        peer = lax.rem(me + step, group_count)
        pl.semaphore_signal(barrier, inc=1, device_id=(seq_me, peer), device_id_type=MESH)
    pl.semaphore_wait(barrier, group_count - 1)
    sends = []
    for step in range(1, group_count):
        peer = lax.rem(me + step, group_count)
        copy = pltpu.make_async_remote_copy(
            src_ref=part_ref.at[pl.ds(pl.multiple_of(peer * rows, 8), rows)],
            dst_ref=landed.at[me],
            send_sem=send_sems.at[step],
            recv_sem=recv_sems.at[me],
            device_id=(seq_me, peer),
            device_id_type=MESH,
        )
        copy.start()
        sends.append(copy)
    own = pltpu.make_async_copy(
        part_ref.at[pl.ds(pl.multiple_of(me * rows, 8), rows)], landed.at[me], own_sem
    )
    own.start()
    own.wait()
    for step in range(1, group_count):
        source = lax.rem(me + group_count - step, group_count)
        pltpu.make_async_remote_copy(
            src_ref=part_ref.at[pl.ds(0, rows)],
            dst_ref=landed.at[source],
            send_sem=send_sems.at[step],
            recv_sem=recv_sems.at[source],
            device_id=(seq_me, source),
            device_id_type=MESH,
        ).wait_recv()
    for copy in sends:
        copy.wait_send()
    total = landed[0].astype(jnp.float32)
    for slot in range(1, group_count):
        total = total + landed[slot].astype(jnp.float32)
    out_ref[...] = total.astype(out_ref.dtype)


def group_sum(part, group_count):
    rows = part.shape[0] // group_count
    cols = part.shape[1]
    return pl.pallas_call(
        functools.partial(group_sum_kernel, group_count),
        out_shape=jax.ShapeDtypeStruct((rows, cols), part.dtype),
        in_specs=[pl.BlockSpec(memory_space=pltpu.VMEM)],
        out_specs=pl.BlockSpec(memory_space=pltpu.VMEM),
        scratch_shapes=[
            pltpu.VMEM((group_count, rows, cols), part.dtype),
            pltpu.SemaphoreType.DMA((group_count,)),
            pltpu.SemaphoreType.DMA((group_count,)),
            pltpu.SemaphoreType.DMA,
        ],
        compiler_params=pltpu.CompilerParams(collective_id=0, has_side_effects=True),
    )(part)


def on_device(
    hidden_in,
    w_query,
    w_key,
    w_value,
    w_zgate,
    w_decay,
    w_beta,
    conv_query,
    conv_key,
    conv_value,
    a_log,
    dt_bias,
    norm_gain,
    w_out,
):
    tok_rows = hidden_in.shape[0]
    pre_query, pre_key, pre_value = project_inputs(hidden_in, w_query, w_key, w_value)
    kernel_len = conv_query.shape[0]
    rim_rows = tok_rows - kernel_len + 1
    rim_block = jnp.concatenate(
        [pre_query[rim_rows:], pre_key[rim_rows:], pre_value[rim_rows:]], axis=1
    )
    prior = passed_along(rim_block, "seq", 1)
    queries, key_vecs, values, log_decay, write_rate, zgate = mixer_inputs(
        hidden_in,
        pre_query,
        pre_key,
        pre_value,
        prior,
        conv_query,
        conv_key,
        conv_value,
        w_zgate,
        w_decay,
        w_beta,
        a_log,
        dt_bias,
    )
    terms = span_terms(
        to_blocks(queries),
        to_blocks(key_vecs),
        to_blocks(values),
        to_blocks(log_decay[..., None])[..., 0],
        to_blocks(write_rate[..., None])[..., 0],
    )
    head_count = values.shape[1]
    identity = jnp.broadcast_to(jnp.eye(DK, dtype=jnp.float32), (head_count, DK, DK))
    empty_state = jnp.zeros((head_count, DK, DV), jnp.float32)

    def compose(carried, per_span):
        prefix_a, prefix_b = carried
        step_trans, step_written, step_carry, step_local = per_span
        local_mix = (
            jnp.einsum("hsd,hde->hse", step_carry, prefix_b, precision=highest) + step_local
        )
        entry_map = jnp.einsum("hsd,hde->hse", step_carry, prefix_a, precision=highest)
        new_a = jnp.einsum("hde,hef->hdf", step_trans, prefix_a, precision=highest)
        new_b = apply_shard(step_trans, prefix_b, step_written)
        return ((new_a, new_b), (local_mix, entry_map))

    (shard_a, shard_b), (local_mix, entry_map) = lax.scan(
        compose, (identity, empty_state), terms, unroll=True
    )

    state_in = shard_scan(shard_a, shard_b, lax.axis_size("seq"))
    produced = local_mix + jnp.einsum("jhsd,hde->jhse", entry_map, state_in, precision=highest)
    produced = produced.transpose(0, 2, 1, 3).reshape(tok_rows, head_count, DV)
    gated = gated_output(produced, zgate, norm_gain)
    part = jnp.dot(gated, w_out, preferred_element_type=jnp.float32).astype(jnp.bfloat16)
    return group_sum(part, lax.axis_size("hg"))


def solution(mesh):
    return jax.shard_map(
        on_device,
        mesh=mesh,
        in_specs=(
            P("seq", None),
            P(None, "hg"),
            P(None, "hg"),
            P(None, "hg"),
            P(None, "hg"),
            P(None, "hg"),
            P(None, "hg"),
            P(None, "hg"),
            P(None, "hg"),
            P(None, "hg"),
            P("hg"),
            P("hg"),
            P(),
            P("hg", None),
        ),
        out_specs=P(("seq", "hg"), None),
        check_vma=False,
    )
```

```python
import functools

import jax
import numpy as np
import jax.numpy as jnp
from jax import lax
from jax.experimental import pallas as pl
from jax.experimental.pallas import tpu as pltpu
from jax.sharding import PartitionSpec as P

MESH = pl.DeviceIdType.MESH

VH = 32
KH = 16
DK = 128
DV = 128
SPAN = 64


highest = lax.Precision.HIGHEST
norm_eps = 1e-06


def passed_along(block, axis, distance):
    devices = range(lax.axis_size(axis))
    route = [(i - distance, i) for i in devices if i - distance in devices]
    return lax.ppermute(block, axis, route)


def project_inputs(hidden_in, w_query, w_key, w_value):
    pre_query = jnp.dot(hidden_in, w_query, preferred_element_type=jnp.float32).astype(jnp.bfloat16)
    pre_key = jnp.dot(hidden_in, w_key, preferred_element_type=jnp.float32).astype(jnp.bfloat16)
    pre_value = jnp.dot(hidden_in, w_value, preferred_element_type=jnp.float32).astype(jnp.bfloat16)
    return (pre_query, pre_key, pre_value)


def conv_silu(projected, kernel, prior):
    kernel_len = kernel.shape[0]
    tok_rows = projected.shape[0]
    padded = jnp.concatenate([prior.astype(jnp.float32), projected.astype(jnp.float32)], axis=0)
    summed = jnp.zeros((tok_rows, projected.shape[1]), jnp.float32)
    for offset in range(kernel_len):
        summed = summed + kernel[offset].astype(jnp.float32) * padded[offset : offset + tok_rows]
    return jax.nn.silu(summed)


def unit_length(vectors):
    return vectors * lax.rsqrt(jnp.sum(vectors * vectors, axis=-1, keepdims=True) + norm_eps)


def mixer_inputs(
    hidden_in,
    pre_query,
    pre_key,
    pre_value,
    prior,
    conv_query,
    conv_key,
    conv_value,
    w_zgate,
    w_decay,
    w_beta,
    a_log,
    dt_bias,
):
    tok_rows = hidden_in.shape[0]
    query_cols = pre_query.shape[1]
    key_cols = pre_key.shape[1]
    ratio = VH // KH
    queries = unit_length(
        conv_silu(pre_query, conv_query, prior[:, :query_cols]).reshape(tok_rows, -1, DK)
    ) * DK ** (-0.5)
    key_vecs = unit_length(
        conv_silu(pre_key, conv_key, prior[:, query_cols : query_cols + key_cols]).reshape(
            tok_rows, -1, DK
        )
    )
    values = conv_silu(pre_value, conv_value, prior[:, query_cols + key_cols :]).reshape(
        tok_rows, -1, DV
    )
    queries = jnp.repeat(queries, ratio, axis=1)
    key_vecs = jnp.repeat(key_vecs, ratio, axis=1)
    zgate = jnp.dot(hidden_in, w_zgate, preferred_element_type=jnp.float32).astype(jnp.bfloat16)
    rate_logits = jnp.dot(hidden_in, w_decay, preferred_element_type=jnp.float32)
    log_decay = -jnp.exp(a_log) * jax.nn.softplus(rate_logits + dt_bias)
    write_rate = jax.nn.sigmoid(jnp.dot(hidden_in, w_beta, preferred_element_type=jnp.float32))
    return (queries, key_vecs, values, log_decay, write_rate, zgate)


def to_blocks(array_3d):
    tok_rows, head_count = (array_3d.shape[0], array_3d.shape[1])
    return array_3d.reshape(tok_rows // SPAN, SPAN, head_count, -1).transpose(0, 2, 1, 3)


def unit_lower_inverse(lower_part):
    block_len = lower_part.shape[-1]
    row_ids = np.arange(block_len)[:, None]
    col_ids = np.arange(block_len)[None, :]
    first = jnp.asarray((row_ids // 2 == col_ids // 2) & (row_ids != col_ids), jnp.float32)
    inverse = lax.optimization_barrier(
        jnp.asarray(np.eye(block_len), jnp.float32) - lower_part * first
    )
    size = 2
    while size < block_len:
        band = (row_ids // (2 * size) == col_ids // (2 * size)) & (row_ids // size != col_ids // size)
        off_blocks = lower_part * jnp.asarray(band, jnp.float32)
        step = jnp.einsum("...st,...tu->...su", inverse, off_blocks, precision=highest)
        inverse = inverse - jnp.einsum("...st,...tu->...su", step, inverse, precision=highest)
        size *= 2
    return inverse


def span_terms(queries, key_vecs, values, log_decay, write_rate):
    block_len = log_decay.shape[-1]
    cum_decay = jnp.cumsum(log_decay, axis=-1)
    row_ids = lax.broadcasted_iota(jnp.int32, (block_len, block_len), 0)
    col_ids = lax.broadcasted_iota(jnp.int32, (block_len, block_len), 1)
    inclusive = row_ids >= col_ids
    strict = row_ids > col_ids
    gap_mat = cum_decay[..., :, None] - cum_decay[..., None, :]
    falloff = jnp.where(inclusive, jnp.exp(jnp.where(inclusive, gap_mat, 0.0)), 0.0)
    key_dots = jnp.einsum("...sd,...td->...st", key_vecs, key_vecs, precision=highest)
    lower_part = jnp.where(strict, write_rate[..., :, None] * falloff * key_dots, 0.0)
    inverse = unit_lower_inverse(lower_part)
    wy_keys = jnp.einsum(
        "...st,...td->...sd",
        inverse,
        (write_rate * jnp.exp(cum_decay))[..., None] * key_vecs,
        precision=highest,
    )
    wy_values = jnp.einsum(
        "...st,...td->...sd", inverse, write_rate[..., None] * values, precision=highest
    )
    scores = falloff * jnp.einsum("...sd,...td->...st", queries, key_vecs, precision=highest)
    tail_keys = jnp.exp(cum_decay[..., -1:] - cum_decay)[..., None] * key_vecs
    whole_decay = jnp.exp(cum_decay[..., -1])[..., None, None]
    transition = whole_decay * jnp.eye(key_vecs.shape[-1], dtype=jnp.float32) - jnp.einsum(
        "...sd,...se->...de", tail_keys, wy_keys, precision=highest
    )
    written = jnp.einsum("...sd,...se->...de", tail_keys, wy_values, precision=highest)
    carry_map = jnp.exp(cum_decay)[..., None] * queries - jnp.einsum(
        "...st,...td->...sd", scores, wy_keys, precision=highest
    )
    local_out = jnp.einsum("...st,...te->...se", scores, wy_values, precision=highest)
    return (transition, written, carry_map, local_out)


def gated_output(produced, zgate, norm_gain):
    tok_rows = produced.shape[0]
    mean_sq = jnp.mean(produced * produced, axis=-1, keepdims=True)
    gate_vals = jax.nn.silu(zgate.astype(jnp.float32).reshape(produced.shape))
    normed = produced * lax.rsqrt(mean_sq + norm_eps) * norm_gain * gate_vals
    return normed.reshape(tok_rows, -1).astype(jnp.bfloat16)


def advance(state_now, per_span):
    transition, written, carry_map, local_out = per_span
    produced = jnp.einsum("hsd,hde->hse", carry_map, state_now, precision=highest) + local_out
    state_next = jnp.einsum("hde,hef->hdf", transition, state_now, precision=highest) + written
    return (state_next, produced)


def apply_shard(trans_mat, state_now, written):
    return jnp.einsum("hde,hef->hdf", trans_mat, state_now, precision=highest) + written


def shard_scan_kernel(
    shard_count, a_ref, b_ref, out_ref, cur_a, cur_b, out_a, out_b, got_a, got_b, send_sems, recv_sems
):
    me = lax.axis_index("seq")
    hg_me = lax.axis_index("hg")
    head_count = a_ref.shape[0]
    distances = []
    distance = 1
    while distance < shard_count:
        distances.append(distance)
        distance *= 2
    barrier = pltpu.get_barrier_semaphore()
    for distance in distances:
        for target in (lax.rem(me + distance, shard_count), lax.rem(me + shard_count - distance, shard_count)):
            pl.semaphore_signal(barrier, inc=1, device_id=(target, hg_me), device_id_type=MESH)
    pl.semaphore_wait(barrier, 2 * len(distances))
    cur_a[0] = a_ref[...]
    cur_b[0] = b_ref[...]
    out_a[0] = a_ref[...].astype(out_a.dtype)
    out_b[0] = b_ref[...].astype(out_b.dtype)
    sem_index = 0
    for round_index, distance in enumerate(distances):
        target = lax.rem(me + distance, shard_count)
        sends_a = round_index + 1 < len(distances)
        copies = [
            pltpu.make_async_remote_copy(
                src_ref=out_b.at[round_index],
                dst_ref=got_b.at[round_index],
                send_sem=send_sems.at[sem_index],
                recv_sem=recv_sems.at[sem_index],
                device_id=(target, hg_me),
                device_id_type=MESH,
            )
        ]
        if sends_a:
            copies.append(
                pltpu.make_async_remote_copy(
                    src_ref=out_a.at[round_index],
                    dst_ref=got_a.at[round_index],
                    send_sem=send_sems.at[sem_index + 1],
                    recv_sem=recv_sems.at[sem_index + 1],
                    device_id=(target, hg_me),
                    device_id_type=MESH,
                )
            )
        sem_index += len(copies)
        for copy in copies:
            copy.start()
        for copy in copies:
            copy.wait()
        has_prev = me >= distance
        for head in range(head_count):
            own_a = cur_a[round_index, head]
            own_b = cur_b[round_index, head]
            joined_b = (
                jnp.dot(own_a, got_b[round_index, head].astype(jnp.float32), precision=highest,
                        preferred_element_type=jnp.float32)
                + own_b
            )
            next_b = jnp.where(has_prev, joined_b, own_b)
            cur_b[round_index + 1, head] = next_b
            out_b[round_index + 1, head] = next_b.astype(out_b.dtype)
            if sends_a:
                joined_a = jnp.dot(own_a, got_a[round_index, head].astype(jnp.float32),
                                   precision=highest, preferred_element_type=jnp.float32)
                next_a = jnp.where(has_prev, joined_a, own_a)
                cur_a[round_index + 1, head] = next_a
                out_a[round_index + 1, head] = next_a.astype(out_a.dtype)
    last = len(distances)
    shift = pltpu.make_async_remote_copy(
        src_ref=out_b.at[last],
        dst_ref=got_b.at[last],
        send_sem=send_sems.at[sem_index],
        recv_sem=recv_sems.at[sem_index],
        device_id=(lax.rem(me + 1, shard_count), hg_me),
        device_id_type=MESH,
    )
    shift.start()
    shift.wait()
    out_ref[...] = jnp.where(me >= 1, got_b[last].astype(jnp.float32), 0.0)


def shard_scan(shard_a, shard_b, shard_count):
    rounds = max(1, (shard_count - 1).bit_length())
    return pl.pallas_call(
        functools.partial(shard_scan_kernel, shard_count),
        out_shape=jax.ShapeDtypeStruct(shard_b.shape, jnp.float32),
        in_specs=[pl.BlockSpec(memory_space=pltpu.VMEM)] * 2,
        out_specs=pl.BlockSpec(memory_space=pltpu.VMEM),
        scratch_shapes=[
            pltpu.VMEM((rounds + 1,) + shard_a.shape, jnp.float32),
            pltpu.VMEM((rounds + 1,) + shard_b.shape, jnp.float32),
            pltpu.VMEM((rounds + 1,) + shard_a.shape, jnp.bfloat16),
            pltpu.VMEM((rounds + 1,) + shard_b.shape, jnp.bfloat16),
            pltpu.VMEM((rounds + 1,) + shard_a.shape, jnp.bfloat16),
            pltpu.VMEM((rounds + 1,) + shard_b.shape, jnp.bfloat16),
            pltpu.SemaphoreType.DMA((2 * rounds + 1,)),
            pltpu.SemaphoreType.DMA((2 * rounds + 1,)),
        ],
        compiler_params=pltpu.CompilerParams(collective_id=1, has_side_effects=True),
    )(shard_a, shard_b)


def group_sum_kernel(group_count, part_ref, out_ref, landed, send_sems, recv_sems, own_sem):
    me = lax.axis_index("hg")
    seq_me = lax.axis_index("seq")
    rows = out_ref.shape[0]
    barrier = pltpu.get_barrier_semaphore()
    for step in range(1, group_count):
        peer = lax.rem(me + step, group_count)
        pl.semaphore_signal(barrier, inc=1, device_id=(seq_me, peer), device_id_type=MESH)
    pl.semaphore_wait(barrier, group_count - 1)
    sends = []
    for step in range(1, group_count):
        peer = lax.rem(me + step, group_count)
        copy = pltpu.make_async_remote_copy(
            src_ref=part_ref.at[pl.ds(pl.multiple_of(peer * rows, 8), rows)],
            dst_ref=landed.at[me],
            send_sem=send_sems.at[step],
            recv_sem=recv_sems.at[me],
            device_id=(seq_me, peer),
            device_id_type=MESH,
        )
        copy.start()
        sends.append(copy)
    own = pltpu.make_async_copy(
        part_ref.at[pl.ds(pl.multiple_of(me * rows, 8), rows)], landed.at[me], own_sem
    )
    own.start()
    own.wait()
    for step in range(1, group_count):
        source = lax.rem(me + group_count - step, group_count)
        pltpu.make_async_remote_copy(
            src_ref=part_ref.at[pl.ds(0, rows)],
            dst_ref=landed.at[source],
            send_sem=send_sems.at[step],
            recv_sem=recv_sems.at[source],
            device_id=(seq_me, source),
            device_id_type=MESH,
        ).wait_recv()
    for copy in sends:
        copy.wait_send()
    total = landed[0].astype(jnp.float32)
    for slot in range(1, group_count):
        total = total + landed[slot].astype(jnp.float32)
    out_ref[...] = total.astype(out_ref.dtype)


def group_sum(part, group_count):
    rows = part.shape[0] // group_count
    cols = part.shape[1]
    return pl.pallas_call(
        functools.partial(group_sum_kernel, group_count),
        out_shape=jax.ShapeDtypeStruct((rows, cols), part.dtype),
        in_specs=[pl.BlockSpec(memory_space=pltpu.VMEM)],
        out_specs=pl.BlockSpec(memory_space=pltpu.VMEM),
        scratch_shapes=[
            pltpu.VMEM((group_count, rows, cols), part.dtype),
            pltpu.SemaphoreType.DMA((group_count,)),
            pltpu.SemaphoreType.DMA((group_count,)),
            pltpu.SemaphoreType.DMA,
        ],
        compiler_params=pltpu.CompilerParams(collective_id=0, has_side_effects=True),
    )(part)


def on_device(
    hidden_in,
    w_query,
    w_key,
    w_value,
    w_zgate,
    w_decay,
    w_beta,
    conv_query,
    conv_key,
    conv_value,
    a_log,
    dt_bias,
    norm_gain,
    w_out,
):
    tok_rows = hidden_in.shape[0]
    pre_query, pre_key, pre_value = project_inputs(hidden_in, w_query, w_key, w_value)
    kernel_len = conv_query.shape[0]
    rim_rows = tok_rows - kernel_len + 1
    rim_block = jnp.concatenate(
        [pre_query[rim_rows:], pre_key[rim_rows:], pre_value[rim_rows:]], axis=1
    )
    prior = passed_along(rim_block, "seq", 1)
    queries, key_vecs, values, log_decay, write_rate, zgate = mixer_inputs(
        hidden_in,
        pre_query,
        pre_key,
        pre_value,
        prior,
        conv_query,
        conv_key,
        conv_value,
        w_zgate,
        w_decay,
        w_beta,
        a_log,
        dt_bias,
    )
    terms = span_terms(
        to_blocks(queries),
        to_blocks(key_vecs),
        to_blocks(values),
        to_blocks(log_decay[..., None])[..., 0],
        to_blocks(write_rate[..., None])[..., 0],
    )
    head_count = values.shape[1]
    identity = jnp.broadcast_to(jnp.eye(DK, dtype=jnp.float32), (head_count, DK, DK))
    empty_state = jnp.zeros((head_count, DK, DV), jnp.float32)

    def compose(carried, per_span):
        prefix_a, prefix_b = carried
        step_trans, step_written, step_carry, step_local = per_span
        local_mix = (
            jnp.einsum("hsd,hde->hse", step_carry, prefix_b, precision=highest) + step_local
        )
        entry_map = jnp.einsum("hsd,hde->hse", step_carry, prefix_a, precision=highest)
        new_a = jnp.einsum("hde,hef->hdf", step_trans, prefix_a, precision=highest)
        new_b = apply_shard(step_trans, prefix_b, step_written)
        return ((new_a, new_b), (local_mix, entry_map))

    (shard_a, shard_b), (local_mix, entry_map) = lax.scan(
        compose, (identity, empty_state), terms, unroll=True
    )

    state_in = shard_scan(shard_a, shard_b, lax.axis_size("seq"))
    produced = local_mix + jnp.einsum("jhsd,hde->jhse", entry_map, state_in, precision=highest)
    produced = produced.transpose(0, 2, 1, 3).reshape(tok_rows, head_count, DV)
    gated = gated_output(produced, zgate, norm_gain)
    part = jnp.dot(gated, w_out, preferred_element_type=jnp.float32).astype(jnp.bfloat16)
    return group_sum(part, lax.axis_size("hg"))


def solution(mesh):
    return jax.shard_map(
        on_device,
        mesh=mesh,
        in_specs=(
            P("seq", None),
            P(None, "hg"),
            P(None, "hg"),
            P(None, "hg"),
            P(None, "hg"),
            P(None, "hg"),
            P(None, "hg"),
            P(None, "hg"),
            P(None, "hg"),
            P(None, "hg"),
            P("hg"),
            P("hg"),
            P(),
            P("hg", None),
        ),
        out_specs=P(("seq", "hg"), None),
        check_vma=False,
    )
```

```python
import functools

import jax
import numpy as np
import jax.numpy as jnp
from jax import lax
from jax.experimental import pallas as pl
from jax.experimental.pallas import tpu as pltpu
from jax.sharding import PartitionSpec as P

MESH = pl.DeviceIdType.MESH

VH = 32
KH = 16
DK = 128
DV = 128
SPAN = 64


highest = lax.Precision.HIGH
norm_eps = 1e-06


def passed_along(block, axis, distance):
    devices = range(lax.axis_size(axis))
    route = [(i - distance, i) for i in devices if i - distance in devices]
    return lax.ppermute(block, axis, route)


def project_inputs(hidden_in, w_query, w_key, w_value):
    pre_query = jnp.dot(hidden_in, w_query, preferred_element_type=jnp.float32).astype(jnp.bfloat16)
    pre_key = jnp.dot(hidden_in, w_key, preferred_element_type=jnp.float32).astype(jnp.bfloat16)
    pre_value = jnp.dot(hidden_in, w_value, preferred_element_type=jnp.float32).astype(jnp.bfloat16)
    return (pre_query, pre_key, pre_value)


def conv_silu(projected, kernel, prior):
    kernel_len = kernel.shape[0]
    tok_rows = projected.shape[0]
    padded = jnp.concatenate([prior.astype(jnp.float32), projected.astype(jnp.float32)], axis=0)
    summed = jnp.zeros((tok_rows, projected.shape[1]), jnp.float32)
    for offset in range(kernel_len):
        summed = summed + kernel[offset].astype(jnp.float32) * padded[offset : offset + tok_rows]
    return jax.nn.silu(summed)


def unit_length(vectors):
    return vectors * lax.rsqrt(jnp.sum(vectors * vectors, axis=-1, keepdims=True) + norm_eps)


def mixer_inputs(
    hidden_in,
    pre_query,
    pre_key,
    pre_value,
    prior,
    conv_query,
    conv_key,
    conv_value,
    w_zgate,
    w_decay,
    w_beta,
    a_log,
    dt_bias,
):
    tok_rows = hidden_in.shape[0]
    query_cols = pre_query.shape[1]
    key_cols = pre_key.shape[1]
    ratio = VH // KH
    queries = unit_length(
        conv_silu(pre_query, conv_query, prior[:, :query_cols]).reshape(tok_rows, -1, DK)
    ) * DK ** (-0.5)
    key_vecs = unit_length(
        conv_silu(pre_key, conv_key, prior[:, query_cols : query_cols + key_cols]).reshape(
            tok_rows, -1, DK
        )
    )
    values = conv_silu(pre_value, conv_value, prior[:, query_cols + key_cols :]).reshape(
        tok_rows, -1, DV
    )
    queries = jnp.repeat(queries, ratio, axis=1)
    key_vecs = jnp.repeat(key_vecs, ratio, axis=1)
    zgate = jnp.dot(hidden_in, w_zgate, preferred_element_type=jnp.float32).astype(jnp.bfloat16)
    rate_logits = jnp.dot(hidden_in, w_decay, preferred_element_type=jnp.float32)
    log_decay = -jnp.exp(a_log) * jax.nn.softplus(rate_logits + dt_bias)
    write_rate = jax.nn.sigmoid(jnp.dot(hidden_in, w_beta, preferred_element_type=jnp.float32))
    return (queries, key_vecs, values, log_decay, write_rate, zgate)


def to_blocks(array_3d):
    tok_rows, head_count = (array_3d.shape[0], array_3d.shape[1])
    return array_3d.reshape(tok_rows // SPAN, SPAN, head_count, -1).transpose(0, 2, 1, 3)


def unit_lower_inverse(lower_part):
    block_len = lower_part.shape[-1]
    row_ids = np.arange(block_len)[:, None]
    col_ids = np.arange(block_len)[None, :]
    first = jnp.asarray((row_ids // 2 == col_ids // 2) & (row_ids != col_ids), jnp.float32)
    inverse = lax.optimization_barrier(
        jnp.asarray(np.eye(block_len), jnp.float32) - lower_part * first
    )
    size = 2
    while size < block_len:
        band = (row_ids // (2 * size) == col_ids // (2 * size)) & (row_ids // size != col_ids // size)
        off_blocks = lower_part * jnp.asarray(band, jnp.float32)
        step = jnp.einsum("...st,...tu->...su", inverse, off_blocks, precision=highest)
        inverse = inverse - jnp.einsum("...st,...tu->...su", step, inverse, precision=highest)
        size *= 2
    return inverse


def span_terms(queries, key_vecs, values, log_decay, write_rate):
    block_len = log_decay.shape[-1]
    cum_decay = jnp.cumsum(log_decay, axis=-1)
    row_ids = lax.broadcasted_iota(jnp.int32, (block_len, block_len), 0)
    col_ids = lax.broadcasted_iota(jnp.int32, (block_len, block_len), 1)
    inclusive = row_ids >= col_ids
    strict = row_ids > col_ids
    gap_mat = cum_decay[..., :, None] - cum_decay[..., None, :]
    falloff = jnp.where(inclusive, jnp.exp(jnp.where(inclusive, gap_mat, 0.0)), 0.0)
    key_dots = jnp.einsum("...sd,...td->...st", key_vecs, key_vecs, precision=highest)
    lower_part = jnp.where(strict, write_rate[..., :, None] * falloff * key_dots, 0.0)
    inverse = unit_lower_inverse(lower_part)
    wy_keys = jnp.einsum(
        "...st,...td->...sd",
        inverse,
        (write_rate * jnp.exp(cum_decay))[..., None] * key_vecs,
        precision=highest,
    )
    wy_values = jnp.einsum(
        "...st,...td->...sd", inverse, write_rate[..., None] * values, precision=highest
    )
    scores = falloff * jnp.einsum("...sd,...td->...st", queries, key_vecs, precision=highest)
    tail_keys = jnp.exp(cum_decay[..., -1:] - cum_decay)[..., None] * key_vecs
    whole_decay = jnp.exp(cum_decay[..., -1])[..., None, None]
    transition = whole_decay * jnp.eye(key_vecs.shape[-1], dtype=jnp.float32) - jnp.einsum(
        "...sd,...se->...de", tail_keys, wy_keys, precision=highest
    )
    written = jnp.einsum("...sd,...se->...de", tail_keys, wy_values, precision=highest)
    carry_map = jnp.exp(cum_decay)[..., None] * queries - jnp.einsum(
        "...st,...td->...sd", scores, wy_keys, precision=highest
    )
    local_out = jnp.einsum("...st,...te->...se", scores, wy_values, precision=highest)
    return (transition, written, carry_map, local_out)


def gated_output(produced, zgate, norm_gain):
    tok_rows = produced.shape[0]
    mean_sq = jnp.mean(produced * produced, axis=-1, keepdims=True)
    gate_vals = jax.nn.silu(zgate.astype(jnp.float32).reshape(produced.shape))
    normed = produced * lax.rsqrt(mean_sq + norm_eps) * norm_gain * gate_vals
    return normed.reshape(tok_rows, -1).astype(jnp.bfloat16)


def advance(state_now, per_span):
    transition, written, carry_map, local_out = per_span
    produced = jnp.einsum("hsd,hde->hse", carry_map, state_now, precision=highest) + local_out
    state_next = jnp.einsum("hde,hef->hdf", transition, state_now, precision=highest) + written
    return (state_next, produced)


def apply_shard(trans_mat, state_now, written):
    return jnp.einsum("hde,hef->hdf", trans_mat, state_now, precision=highest) + written


def shard_scan_kernel(
    shard_count, a_ref, b_ref, out_ref, cur_a, cur_b, out_a, out_b, got_a, got_b, send_sems, recv_sems
):
    me = lax.axis_index("seq")
    hg_me = lax.axis_index("hg")
    head_count = a_ref.shape[0]
    distances = []
    distance = 1
    while distance < shard_count:
        distances.append(distance)
        distance *= 2
    barrier = pltpu.get_barrier_semaphore()
    for distance in distances:
        for target in (lax.rem(me + distance, shard_count), lax.rem(me + shard_count - distance, shard_count)):
            pl.semaphore_signal(barrier, inc=1, device_id=(target, hg_me), device_id_type=MESH)
    pl.semaphore_wait(barrier, 2 * len(distances))
    cur_a[0] = a_ref[...]
    cur_b[0] = b_ref[...]
    out_a[0] = a_ref[...].astype(out_a.dtype)
    out_b[0] = b_ref[...].astype(out_b.dtype)
    sem_index = 0
    for round_index, distance in enumerate(distances):
        target = lax.rem(me + distance, shard_count)
        sends_a = round_index + 1 < len(distances)
        copies = [
            pltpu.make_async_remote_copy(
                src_ref=out_b.at[round_index],
                dst_ref=got_b.at[round_index],
                send_sem=send_sems.at[sem_index],
                recv_sem=recv_sems.at[sem_index],
                device_id=(target, hg_me),
                device_id_type=MESH,
            )
        ]
        if sends_a:
            copies.append(
                pltpu.make_async_remote_copy(
                    src_ref=out_a.at[round_index],
                    dst_ref=got_a.at[round_index],
                    send_sem=send_sems.at[sem_index + 1],
                    recv_sem=recv_sems.at[sem_index + 1],
                    device_id=(target, hg_me),
                    device_id_type=MESH,
                )
            )
        sem_index += len(copies)
        for copy in copies:
            copy.start()
        for copy in copies:
            copy.wait()
        has_prev = me >= distance
        for head in range(head_count):
            own_a = cur_a[round_index, head]
            own_b = cur_b[round_index, head]
            joined_b = (
                jnp.dot(own_a, got_b[round_index, head].astype(jnp.float32), precision=highest,
                        preferred_element_type=jnp.float32)
                + own_b
            )
            next_b = jnp.where(has_prev, joined_b, own_b)
            cur_b[round_index + 1, head] = next_b
            out_b[round_index + 1, head] = next_b.astype(out_b.dtype)
            if sends_a:
                joined_a = jnp.dot(own_a, got_a[round_index, head].astype(jnp.float32),
                                   precision=highest, preferred_element_type=jnp.float32)
                next_a = jnp.where(has_prev, joined_a, own_a)
                cur_a[round_index + 1, head] = next_a
                out_a[round_index + 1, head] = next_a.astype(out_a.dtype)
    last = len(distances)
    shift = pltpu.make_async_remote_copy(
        src_ref=out_b.at[last],
        dst_ref=got_b.at[last],
        send_sem=send_sems.at[sem_index],
        recv_sem=recv_sems.at[sem_index],
        device_id=(lax.rem(me + 1, shard_count), hg_me),
        device_id_type=MESH,
    )
    shift.start()
    shift.wait()
    out_ref[...] = jnp.where(me >= 1, got_b[last].astype(jnp.float32), 0.0)


def shard_scan(shard_a, shard_b, shard_count):
    rounds = max(1, (shard_count - 1).bit_length())
    return pl.pallas_call(
        functools.partial(shard_scan_kernel, shard_count),
        out_shape=jax.ShapeDtypeStruct(shard_b.shape, jnp.float32),
        in_specs=[pl.BlockSpec(memory_space=pltpu.VMEM)] * 2,
        out_specs=pl.BlockSpec(memory_space=pltpu.VMEM),
        scratch_shapes=[
            pltpu.VMEM((rounds + 1,) + shard_a.shape, jnp.float32),
            pltpu.VMEM((rounds + 1,) + shard_b.shape, jnp.float32),
            pltpu.VMEM((rounds + 1,) + shard_a.shape, jnp.bfloat16),
            pltpu.VMEM((rounds + 1,) + shard_b.shape, jnp.bfloat16),
            pltpu.VMEM((rounds + 1,) + shard_a.shape, jnp.bfloat16),
            pltpu.VMEM((rounds + 1,) + shard_b.shape, jnp.bfloat16),
            pltpu.SemaphoreType.DMA((2 * rounds + 1,)),
            pltpu.SemaphoreType.DMA((2 * rounds + 1,)),
        ],
        compiler_params=pltpu.CompilerParams(collective_id=1, has_side_effects=True),
    )(shard_a, shard_b)


def group_sum_kernel(group_count, part_ref, out_ref, landed, send_sems, recv_sems, own_sem):
    me = lax.axis_index("hg")
    seq_me = lax.axis_index("seq")
    rows = out_ref.shape[0]
    barrier = pltpu.get_barrier_semaphore()
    for step in range(1, group_count):
        peer = lax.rem(me + step, group_count)
        pl.semaphore_signal(barrier, inc=1, device_id=(seq_me, peer), device_id_type=MESH)
    pl.semaphore_wait(barrier, group_count - 1)
    sends = []
    for step in range(1, group_count):
        peer = lax.rem(me + step, group_count)
        copy = pltpu.make_async_remote_copy(
            src_ref=part_ref.at[pl.ds(pl.multiple_of(peer * rows, 8), rows)],
            dst_ref=landed.at[me],
            send_sem=send_sems.at[step],
            recv_sem=recv_sems.at[me],
            device_id=(seq_me, peer),
            device_id_type=MESH,
        )
        copy.start()
        sends.append(copy)
    own = pltpu.make_async_copy(
        part_ref.at[pl.ds(pl.multiple_of(me * rows, 8), rows)], landed.at[me], own_sem
    )
    own.start()
    own.wait()
    for step in range(1, group_count):
        source = lax.rem(me + group_count - step, group_count)
        pltpu.make_async_remote_copy(
            src_ref=part_ref.at[pl.ds(0, rows)],
            dst_ref=landed.at[source],
            send_sem=send_sems.at[step],
            recv_sem=recv_sems.at[source],
            device_id=(seq_me, source),
            device_id_type=MESH,
        ).wait_recv()
    for copy in sends:
        copy.wait_send()
    total = landed[0].astype(jnp.float32)
    for slot in range(1, group_count):
        total = total + landed[slot].astype(jnp.float32)
    out_ref[...] = total.astype(out_ref.dtype)


def group_sum(part, group_count):
    rows = part.shape[0] // group_count
    cols = part.shape[1]
    return pl.pallas_call(
        functools.partial(group_sum_kernel, group_count),
        out_shape=jax.ShapeDtypeStruct((rows, cols), part.dtype),
        in_specs=[pl.BlockSpec(memory_space=pltpu.VMEM)],
        out_specs=pl.BlockSpec(memory_space=pltpu.VMEM),
        scratch_shapes=[
            pltpu.VMEM((group_count, rows, cols), part.dtype),
            pltpu.SemaphoreType.DMA((group_count,)),
            pltpu.SemaphoreType.DMA((group_count,)),
            pltpu.SemaphoreType.DMA,
        ],
        compiler_params=pltpu.CompilerParams(collective_id=0, has_side_effects=True),
    )(part)


def on_device(
    hidden_in,
    w_query,
    w_key,
    w_value,
    w_zgate,
    w_decay,
    w_beta,
    conv_query,
    conv_key,
    conv_value,
    a_log,
    dt_bias,
    norm_gain,
    w_out,
):
    tok_rows = hidden_in.shape[0]
    pre_query, pre_key, pre_value = project_inputs(hidden_in, w_query, w_key, w_value)
    kernel_len = conv_query.shape[0]
    rim_rows = tok_rows - kernel_len + 1
    rim_block = jnp.concatenate(
        [pre_query[rim_rows:], pre_key[rim_rows:], pre_value[rim_rows:]], axis=1
    )
    prior = passed_along(rim_block, "seq", 1)
    queries, key_vecs, values, log_decay, write_rate, zgate = mixer_inputs(
        hidden_in,
        pre_query,
        pre_key,
        pre_value,
        prior,
        conv_query,
        conv_key,
        conv_value,
        w_zgate,
        w_decay,
        w_beta,
        a_log,
        dt_bias,
    )
    terms = span_terms(
        to_blocks(queries),
        to_blocks(key_vecs),
        to_blocks(values),
        to_blocks(log_decay[..., None])[..., 0],
        to_blocks(write_rate[..., None])[..., 0],
    )
    head_count = values.shape[1]
    identity = jnp.broadcast_to(jnp.eye(DK, dtype=jnp.float32), (head_count, DK, DK))
    empty_state = jnp.zeros((head_count, DK, DV), jnp.float32)

    def compose(carried, per_span):
        prefix_a, prefix_b = carried
        step_trans, step_written, step_carry, step_local = per_span
        local_mix = (
            jnp.einsum("hsd,hde->hse", step_carry, prefix_b, precision=highest) + step_local
        )
        entry_map = jnp.einsum("hsd,hde->hse", step_carry, prefix_a, precision=highest)
        new_a = jnp.einsum("hde,hef->hdf", step_trans, prefix_a, precision=highest)
        new_b = apply_shard(step_trans, prefix_b, step_written)
        return ((new_a, new_b), (local_mix, entry_map))

    (shard_a, shard_b), (local_mix, entry_map) = lax.scan(
        compose, (identity, empty_state), terms, unroll=True
    )

    state_in = shard_scan(shard_a, shard_b, lax.axis_size("seq"))
    produced = local_mix + jnp.einsum("jhsd,hde->jhse", entry_map, state_in, precision=highest)
    produced = produced.transpose(0, 2, 1, 3).reshape(tok_rows, head_count, DV)
    gated = gated_output(produced, zgate, norm_gain)
    part = jnp.dot(gated, w_out, preferred_element_type=jnp.float32).astype(jnp.bfloat16)
    return group_sum(part, lax.axis_size("hg"))


def solution(mesh):
    return jax.shard_map(
        on_device,
        mesh=mesh,
        in_specs=(
            P("seq", None),
            P(None, "hg"),
            P(None, "hg"),
            P(None, "hg"),
            P(None, "hg"),
            P(None, "hg"),
            P(None, "hg"),
            P(None, "hg"),
            P(None, "hg"),
            P(None, "hg"),
            P("hg"),
            P("hg"),
            P(),
            P("hg", None),
        ),
        out_specs=P(("seq", "hg"), None),
        check_vma=False,
    )
```

```python
import functools

import jax
import numpy as np
import jax.numpy as jnp
from jax import lax
from jax.experimental import pallas as pl
from jax.experimental.pallas import tpu as pltpu
from jax.sharding import PartitionSpec as P

MESH = pl.DeviceIdType.MESH

VH = 32
KH = 16
DK = 128
DV = 128
SPAN = 64


highest = lax.Precision.HIGH
norm_eps = 1e-06


def passed_along(block, axis, distance):
    devices = range(lax.axis_size(axis))
    route = [(i - distance, i) for i in devices if i - distance in devices]
    return lax.ppermute(block, axis, route)


def project_inputs(hidden_in, w_query, w_key, w_value):
    pre_query = jnp.dot(hidden_in, w_query, preferred_element_type=jnp.float32).astype(jnp.bfloat16)
    pre_key = jnp.dot(hidden_in, w_key, preferred_element_type=jnp.float32).astype(jnp.bfloat16)
    pre_value = jnp.dot(hidden_in, w_value, preferred_element_type=jnp.float32).astype(jnp.bfloat16)
    return (pre_query, pre_key, pre_value)


def conv_silu(projected, kernel, prior):
    kernel_len = kernel.shape[0]
    tok_rows = projected.shape[0]
    padded = jnp.concatenate([prior.astype(jnp.float32), projected.astype(jnp.float32)], axis=0)
    summed = jnp.zeros((tok_rows, projected.shape[1]), jnp.float32)
    for offset in range(kernel_len):
        summed = summed + kernel[offset].astype(jnp.float32) * padded[offset : offset + tok_rows]
    return jax.nn.silu(summed)


def unit_length(vectors):
    return vectors * lax.rsqrt(jnp.sum(vectors * vectors, axis=-1, keepdims=True) + norm_eps)


def mixer_inputs(
    hidden_in,
    pre_query,
    pre_key,
    pre_value,
    prior,
    conv_query,
    conv_key,
    conv_value,
    w_zgate,
    w_decay,
    w_beta,
    a_log,
    dt_bias,
):
    tok_rows = hidden_in.shape[0]
    query_cols = pre_query.shape[1]
    key_cols = pre_key.shape[1]
    ratio = VH // KH
    queries = unit_length(
        conv_silu(pre_query, conv_query, prior[:, :query_cols]).reshape(tok_rows, -1, DK)
    ) * DK ** (-0.5)
    key_vecs = unit_length(
        conv_silu(pre_key, conv_key, prior[:, query_cols : query_cols + key_cols]).reshape(
            tok_rows, -1, DK
        )
    )
    values = conv_silu(pre_value, conv_value, prior[:, query_cols + key_cols :]).reshape(
        tok_rows, -1, DV
    )
    queries = jnp.repeat(queries, ratio, axis=1)
    key_vecs = jnp.repeat(key_vecs, ratio, axis=1)
    zgate = jnp.dot(hidden_in, w_zgate, preferred_element_type=jnp.float32).astype(jnp.bfloat16)
    rate_logits = jnp.dot(hidden_in, w_decay, preferred_element_type=jnp.float32)
    log_decay = -jnp.exp(a_log) * jax.nn.softplus(rate_logits + dt_bias)
    write_rate = jax.nn.sigmoid(jnp.dot(hidden_in, w_beta, preferred_element_type=jnp.float32))
    return (queries, key_vecs, values, log_decay, write_rate, zgate)


def to_blocks(array_3d):
    tok_rows, head_count = (array_3d.shape[0], array_3d.shape[1])
    return array_3d.reshape(tok_rows // SPAN, SPAN, head_count, -1).transpose(0, 2, 1, 3)


def unit_lower_inverse(lower_part):
    block_len = lower_part.shape[-1]
    row_ids = np.arange(block_len)[:, None]
    col_ids = np.arange(block_len)[None, :]
    first = jnp.asarray((row_ids // 2 == col_ids // 2) & (row_ids != col_ids), jnp.float32)
    inverse = lax.optimization_barrier(
        jnp.asarray(np.eye(block_len), jnp.float32) - lower_part * first
    )
    size = 2
    while size < block_len:
        band = (row_ids // (2 * size) == col_ids // (2 * size)) & (row_ids // size != col_ids // size)
        off_blocks = lower_part * jnp.asarray(band, jnp.float32)
        step = jnp.einsum("...st,...tu->...su", inverse, off_blocks, precision=highest)
        inverse = inverse - jnp.einsum("...st,...tu->...su", step, inverse, precision=highest)
        size *= 2
    return inverse


def span_terms(queries, key_vecs, values, log_decay, write_rate):
    block_len = log_decay.shape[-1]
    cum_decay = jnp.cumsum(log_decay, axis=-1)
    row_ids = lax.broadcasted_iota(jnp.int32, (block_len, block_len), 0)
    col_ids = lax.broadcasted_iota(jnp.int32, (block_len, block_len), 1)
    inclusive = row_ids >= col_ids
    strict = row_ids > col_ids
    gap_mat = cum_decay[..., :, None] - cum_decay[..., None, :]
    falloff = jnp.where(inclusive, jnp.exp(jnp.where(inclusive, gap_mat, 0.0)), 0.0)
    key_dots = jnp.einsum("...sd,...td->...st", key_vecs, key_vecs, precision=highest)
    lower_part = jnp.where(strict, write_rate[..., :, None] * falloff * key_dots, 0.0)
    inverse = unit_lower_inverse(lower_part)
    wy_keys = jnp.einsum(
        "...st,...td->...sd",
        inverse,
        (write_rate * jnp.exp(cum_decay))[..., None] * key_vecs,
        precision=highest,
    )
    wy_values = jnp.einsum(
        "...st,...td->...sd", inverse, write_rate[..., None] * values, precision=highest
    )
    scores = falloff * jnp.einsum("...sd,...td->...st", queries, key_vecs, precision=highest)
    tail_keys = jnp.exp(cum_decay[..., -1:] - cum_decay)[..., None] * key_vecs
    whole_decay = jnp.exp(cum_decay[..., -1])[..., None, None]
    transition = whole_decay * jnp.eye(key_vecs.shape[-1], dtype=jnp.float32) - jnp.einsum(
        "...sd,...se->...de", tail_keys, wy_keys, precision=highest
    )
    written = jnp.einsum("...sd,...se->...de", tail_keys, wy_values, precision=highest)
    carry_map = jnp.exp(cum_decay)[..., None] * queries - jnp.einsum(
        "...st,...td->...sd", scores, wy_keys, precision=highest
    )
    local_out = jnp.einsum("...st,...te->...se", scores, wy_values, precision=highest)
    return (transition, written, carry_map, local_out)


def gated_output(produced, zgate, norm_gain):
    tok_rows = produced.shape[0]
    mean_sq = jnp.mean(produced * produced, axis=-1, keepdims=True)
    gate_vals = jax.nn.silu(zgate.astype(jnp.float32).reshape(produced.shape))
    normed = produced * lax.rsqrt(mean_sq + norm_eps) * norm_gain * gate_vals
    return normed.reshape(tok_rows, -1).astype(jnp.bfloat16)


def advance(state_now, per_span):
    transition, written, carry_map, local_out = per_span
    produced = jnp.einsum("hsd,hde->hse", carry_map, state_now, precision=highest) + local_out
    state_next = jnp.einsum("hde,hef->hdf", transition, state_now, precision=highest) + written
    return (state_next, produced)


def apply_shard(trans_mat, state_now, written):
    return jnp.einsum("hde,hef->hdf", trans_mat, state_now, precision=highest) + written


def scan_plan(shard_count):
    plan = []
    cover = 0
    while cover < shard_count - 1:
        if cover == 0:
            distances = [d for d in range(1, 5) if d < shard_count]
            new_cover = 4
        else:
            distances = [cover * k for k in range(1, 4) if cover * k < shard_count]
            new_cover = cover * 4
        last = new_cover >= shard_count - 1
        plan.append([(d, (not last) or d != distances[-1]) for d in distances])
        cover = new_cover
    return plan


def shard_scan_kernel(
    shard_count, a_ref, b_ref, out_ref, own_a, own_b, sent_a, sent_b, got_a, got_b, send_sems, recv_sems
):
    me = lax.axis_index("seq")
    hg_me = lax.axis_index("hg")
    head_count = a_ref.shape[0]
    plan = scan_plan(shard_count)
    distances = sorted({d for round_plan in plan for d, _ in round_plan})
    barrier = pltpu.get_barrier_semaphore()
    for distance in distances:
        for target in (lax.rem(me + distance, shard_count), lax.rem(me + shard_count - distance, shard_count)):
            pl.semaphore_signal(barrier, inc=1, device_id=(target, hg_me), device_id_type=MESH)
    pl.semaphore_wait(barrier, 2 * len(distances))
    own_a[...] = a_ref[...]
    own_b[...] = b_ref[...]
    eye = jnp.eye(a_ref.shape[1], dtype=jnp.float32)
    slot = 0
    copy_index = 0
    result = jnp.zeros(out_ref.shape, jnp.float32)
    for round_index, round_plan in enumerate(plan):
        last = round_index == len(plan) - 1
        sent_a[round_index] = own_a[...].astype(sent_a.dtype)
        sent_b[round_index] = own_b[...].astype(sent_b.dtype)
        copies = []
        slots = []
        for distance, send_a in round_plan:
            target = (lax.rem(me + distance, shard_count), hg_me)
            pair = [(sent_b, got_b)] + ([(sent_a, got_a)] if send_a else [])
            for source, landing in pair:
                copies.append(
                    pltpu.make_async_remote_copy(
                        src_ref=source.at[round_index],
                        dst_ref=landing.at[slot],
                        send_sem=send_sems.at[copy_index],
                        recv_sem=recv_sems.at[copy_index],
                        device_id=target,
                        device_id_type=MESH,
                    )
                )
                copy_index += 1
            slots.append(slot)
            slot += 1
        for copy in copies:
            copy.start()
        for copy in copies:
            copy.wait()
        for head in range(head_count):
            acc_a = None
            acc_b = None
            for (distance, send_a), got in reversed(list(zip(round_plan, slots))):
                valid = me >= distance
                in_b = got_b[got, head].astype(jnp.float32)
                in_a = got_a[got, head].astype(jnp.float32) if send_a else None
                if acc_b is None:
                    acc_b = jnp.where(valid, in_b, 0.0)
                    if not last:
                        acc_a = jnp.where(valid, in_a, eye)
                    continue
                joined_b = jnp.dot(in_a, acc_b, precision=highest, preferred_element_type=jnp.float32) + in_b
                acc_b = jnp.where(valid, joined_b, acc_b)
                if not last:
                    joined_a = jnp.dot(in_a, acc_a, precision=highest, preferred_element_type=jnp.float32)
                    acc_a = jnp.where(valid, joined_a, acc_a)
            if round_index > 0:
                mine_a = own_a[head]
                acc_b = jnp.dot(mine_a, acc_b, precision=highest, preferred_element_type=jnp.float32) + own_b[head]
                if not last:
                    acc_a = jnp.dot(mine_a, acc_a, precision=highest, preferred_element_type=jnp.float32)
            if last:
                out_ref[head] = acc_b
            else:
                own_a[head] = acc_a
                own_b[head] = acc_b


def shard_scan(shard_a, shard_b, shard_count):
    plan = scan_plan(shard_count)
    if not plan:
        return jnp.zeros(shard_b.shape, jnp.float32)
    slots = sum(len(round_plan) for round_plan in plan)
    copies = sum(1 + int(send_a) for round_plan in plan for _, send_a in round_plan)
    return pl.pallas_call(
        functools.partial(shard_scan_kernel, shard_count),
        out_shape=jax.ShapeDtypeStruct(shard_b.shape, jnp.float32),
        in_specs=[pl.BlockSpec(memory_space=pltpu.VMEM)] * 2,
        out_specs=pl.BlockSpec(memory_space=pltpu.VMEM),
        scratch_shapes=[
            pltpu.VMEM(shard_a.shape, jnp.float32),
            pltpu.VMEM(shard_b.shape, jnp.float32),
            pltpu.VMEM((len(plan),) + shard_a.shape, jnp.bfloat16),
            pltpu.VMEM((len(plan),) + shard_b.shape, jnp.bfloat16),
            pltpu.VMEM((slots,) + shard_a.shape, jnp.bfloat16),
            pltpu.VMEM((slots,) + shard_b.shape, jnp.bfloat16),
            pltpu.SemaphoreType.DMA((copies,)),
            pltpu.SemaphoreType.DMA((copies,)),
        ],
        compiler_params=pltpu.CompilerParams(collective_id=1, has_side_effects=True),
    )(shard_a, shard_b)


def group_sum_kernel(group_count, part_ref, out_ref, landed, send_sems, recv_sems, own_sem):
    me = lax.axis_index("hg")
    seq_me = lax.axis_index("seq")
    rows = out_ref.shape[0]
    barrier = pltpu.get_barrier_semaphore()
    for step in range(1, group_count):
        peer = lax.rem(me + step, group_count)
        pl.semaphore_signal(barrier, inc=1, device_id=(seq_me, peer), device_id_type=MESH)
    pl.semaphore_wait(barrier, group_count - 1)
    sends = []
    for step in range(1, group_count):
        peer = lax.rem(me + step, group_count)
        copy = pltpu.make_async_remote_copy(
            src_ref=part_ref.at[pl.ds(pl.multiple_of(peer * rows, 8), rows)],
            dst_ref=landed.at[me],
            send_sem=send_sems.at[step],
            recv_sem=recv_sems.at[me],
            device_id=(seq_me, peer),
            device_id_type=MESH,
        )
        copy.start()
        sends.append(copy)
    own = pltpu.make_async_copy(
        part_ref.at[pl.ds(pl.multiple_of(me * rows, 8), rows)], landed.at[me], own_sem
    )
    own.start()
    own.wait()
    for step in range(1, group_count):
        source = lax.rem(me + group_count - step, group_count)
        pltpu.make_async_remote_copy(
            src_ref=part_ref.at[pl.ds(0, rows)],
            dst_ref=landed.at[source],
            send_sem=send_sems.at[step],
            recv_sem=recv_sems.at[source],
            device_id=(seq_me, source),
            device_id_type=MESH,
        ).wait_recv()
    for copy in sends:
        copy.wait_send()
    total = landed[0].astype(jnp.float32)
    for slot in range(1, group_count):
        total = total + landed[slot].astype(jnp.float32)
    out_ref[...] = total.astype(out_ref.dtype)


def group_sum(part, group_count):
    if group_count == 1:
        return part
    rows = part.shape[0] // group_count
    cols = part.shape[1]
    return pl.pallas_call(
        functools.partial(group_sum_kernel, group_count),
        out_shape=jax.ShapeDtypeStruct((rows, cols), part.dtype),
        in_specs=[pl.BlockSpec(memory_space=pltpu.VMEM)],
        out_specs=pl.BlockSpec(memory_space=pltpu.VMEM),
        scratch_shapes=[
            pltpu.VMEM((group_count, rows, cols), part.dtype),
            pltpu.SemaphoreType.DMA((group_count,)),
            pltpu.SemaphoreType.DMA((group_count,)),
            pltpu.SemaphoreType.DMA,
        ],
        compiler_params=pltpu.CompilerParams(collective_id=0, has_side_effects=True),
    )(part)


def on_device(
    hidden_in,
    w_query,
    w_key,
    w_value,
    w_zgate,
    w_decay,
    w_beta,
    conv_query,
    conv_key,
    conv_value,
    a_log,
    dt_bias,
    norm_gain,
    w_out,
):
    tok_rows = hidden_in.shape[0]
    pre_query, pre_key, pre_value = project_inputs(hidden_in, w_query, w_key, w_value)
    kernel_len = conv_query.shape[0]
    rim_rows = tok_rows - kernel_len + 1
    rim_block = jnp.concatenate(
        [pre_query[rim_rows:], pre_key[rim_rows:], pre_value[rim_rows:]], axis=1
    )
    prior = passed_along(rim_block, "seq", 1)
    queries, key_vecs, values, log_decay, write_rate, zgate = mixer_inputs(
        hidden_in,
        pre_query,
        pre_key,
        pre_value,
        prior,
        conv_query,
        conv_key,
        conv_value,
        w_zgate,
        w_decay,
        w_beta,
        a_log,
        dt_bias,
    )
    terms = span_terms(
        to_blocks(queries),
        to_blocks(key_vecs),
        to_blocks(values),
        to_blocks(log_decay[..., None])[..., 0],
        to_blocks(write_rate[..., None])[..., 0],
    )
    head_count = values.shape[1]
    identity = jnp.broadcast_to(jnp.eye(DK, dtype=jnp.float32), (head_count, DK, DK))
    empty_state = jnp.zeros((head_count, DK, DV), jnp.float32)

    def compose(carried, per_span):
        prefix_a, prefix_b = carried
        step_trans, step_written, step_carry, step_local = per_span
        local_mix = (
            jnp.einsum("hsd,hde->hse", step_carry, prefix_b, precision=highest) + step_local
        )
        entry_map = jnp.einsum("hsd,hde->hse", step_carry, prefix_a, precision=highest)
        new_a = jnp.einsum("hde,hef->hdf", step_trans, prefix_a, precision=highest)
        new_b = apply_shard(step_trans, prefix_b, step_written)
        return ((new_a, new_b), (local_mix, entry_map))

    (shard_a, shard_b), (local_mix, entry_map) = lax.scan(
        compose, (identity, empty_state), terms, unroll=True
    )

    state_in = shard_scan(shard_a, shard_b, lax.axis_size("seq"))
    produced = local_mix + jnp.einsum("jhsd,hde->jhse", entry_map, state_in, precision=highest)
    produced = produced.transpose(0, 2, 1, 3).reshape(tok_rows, head_count, DV)
    gated = gated_output(produced, zgate, norm_gain)
    part = jnp.dot(gated, w_out, preferred_element_type=jnp.float32).astype(jnp.bfloat16)
    return group_sum(part, lax.axis_size("hg"))


def solution(mesh):
    return jax.shard_map(
        on_device,
        mesh=mesh,
        in_specs=(
            P("seq", None),
            P(None, "hg"),
            P(None, "hg"),
            P(None, "hg"),
            P(None, "hg"),
            P(None, "hg"),
            P(None, "hg"),
            P(None, "hg"),
            P(None, "hg"),
            P(None, "hg"),
            P("hg"),
            P("hg"),
            P(),
            P("hg", None),
        ),
        out_specs=P(("seq", "hg"), None),
        check_vma=False,
    )
```

```python
import functools

import jax
import numpy as np
import jax.numpy as jnp
from jax import lax
from jax.experimental import pallas as pl
from jax.experimental.pallas import tpu as pltpu
from jax.sharding import PartitionSpec as P

MESH = pl.DeviceIdType.MESH

VH = 32
KH = 16
DK = 128
DV = 128
SPAN = 64


highest = lax.Precision.HIGH
norm_eps = 1e-06


def passed_along(block, axis, distance):
    devices = range(lax.axis_size(axis))
    route = [(i - distance, i) for i in devices if i - distance in devices]
    return lax.ppermute(block, axis, route)


def project_inputs(hidden_in, w_query, w_key, w_value):
    pre_query = jnp.dot(hidden_in, w_query, preferred_element_type=jnp.float32).astype(jnp.bfloat16)
    pre_key = jnp.dot(hidden_in, w_key, preferred_element_type=jnp.float32).astype(jnp.bfloat16)
    pre_value = jnp.dot(hidden_in, w_value, preferred_element_type=jnp.float32).astype(jnp.bfloat16)
    return (pre_query, pre_key, pre_value)


def conv_silu(projected, kernel, prior):
    kernel_len = kernel.shape[0]
    tok_rows = projected.shape[0]
    padded = jnp.concatenate([prior.astype(jnp.float32), projected.astype(jnp.float32)], axis=0)
    summed = jnp.zeros((tok_rows, projected.shape[1]), jnp.float32)
    for offset in range(kernel_len):
        summed = summed + kernel[offset].astype(jnp.float32) * padded[offset : offset + tok_rows]
    return jax.nn.silu(summed)


def unit_length(vectors):
    return vectors * lax.rsqrt(jnp.sum(vectors * vectors, axis=-1, keepdims=True) + norm_eps)


def mixer_inputs(
    hidden_in,
    pre_query,
    pre_key,
    pre_value,
    prior,
    conv_query,
    conv_key,
    conv_value,
    w_zgate,
    w_decay,
    w_beta,
    a_log,
    dt_bias,
):
    tok_rows = hidden_in.shape[0]
    query_cols = pre_query.shape[1]
    key_cols = pre_key.shape[1]
    ratio = VH // KH
    queries = unit_length(
        conv_silu(pre_query, conv_query, prior[:, :query_cols]).reshape(tok_rows, -1, DK)
    ) * DK ** (-0.5)
    key_vecs = unit_length(
        conv_silu(pre_key, conv_key, prior[:, query_cols : query_cols + key_cols]).reshape(
            tok_rows, -1, DK
        )
    )
    values = conv_silu(pre_value, conv_value, prior[:, query_cols + key_cols :]).reshape(
        tok_rows, -1, DV
    )
    queries = jnp.repeat(queries, ratio, axis=1)
    key_vecs = jnp.repeat(key_vecs, ratio, axis=1)
    zgate = jnp.dot(hidden_in, w_zgate, preferred_element_type=jnp.float32).astype(jnp.bfloat16)
    rate_logits = jnp.dot(hidden_in, w_decay, preferred_element_type=jnp.float32)
    log_decay = -jnp.exp(a_log) * jax.nn.softplus(rate_logits + dt_bias)
    write_rate = jax.nn.sigmoid(jnp.dot(hidden_in, w_beta, preferred_element_type=jnp.float32))
    return (queries, key_vecs, values, log_decay, write_rate, zgate)


def to_blocks(array_3d):
    tok_rows, head_count = (array_3d.shape[0], array_3d.shape[1])
    return array_3d.reshape(tok_rows // SPAN, SPAN, head_count, -1).transpose(0, 2, 1, 3)


def unit_lower_inverse(lower_part):
    block_len = lower_part.shape[-1]
    row_ids = np.arange(block_len)[:, None]
    col_ids = np.arange(block_len)[None, :]
    first = jnp.asarray((row_ids // 2 == col_ids // 2) & (row_ids != col_ids), jnp.float32)
    inverse = lax.optimization_barrier(
        jnp.asarray(np.eye(block_len), jnp.float32) - lower_part * first
    )
    size = 2
    while size < block_len:
        band = (row_ids // (2 * size) == col_ids // (2 * size)) & (row_ids // size != col_ids // size)
        off_blocks = lower_part * jnp.asarray(band, jnp.float32)
        step = jnp.einsum("...st,...tu->...su", inverse, off_blocks, precision=highest)
        inverse = inverse - jnp.einsum("...st,...tu->...su", step, inverse, precision=highest)
        size *= 2
    return inverse


def span_terms(queries, key_vecs, values, log_decay, write_rate):
    block_len = log_decay.shape[-1]
    cum_decay = jnp.cumsum(log_decay, axis=-1)
    row_ids = lax.broadcasted_iota(jnp.int32, (block_len, block_len), 0)
    col_ids = lax.broadcasted_iota(jnp.int32, (block_len, block_len), 1)
    inclusive = row_ids >= col_ids
    strict = row_ids > col_ids
    gap_mat = cum_decay[..., :, None] - cum_decay[..., None, :]
    falloff = jnp.where(inclusive, jnp.exp(jnp.where(inclusive, gap_mat, 0.0)), 0.0)
    key_dots = jnp.einsum("...sd,...td->...st", key_vecs, key_vecs, precision=highest)
    lower_part = jnp.where(strict, write_rate[..., :, None] * falloff * key_dots, 0.0)
    inverse = unit_lower_inverse(lower_part)
    wy_keys = jnp.einsum(
        "...st,...td->...sd",
        inverse,
        (write_rate * jnp.exp(cum_decay))[..., None] * key_vecs,
        precision=highest,
    )
    wy_values = jnp.einsum(
        "...st,...td->...sd", inverse, write_rate[..., None] * values, precision=highest
    )
    scores = falloff * jnp.einsum("...sd,...td->...st", queries, key_vecs, precision=highest)
    tail_keys = jnp.exp(cum_decay[..., -1:] - cum_decay)[..., None] * key_vecs
    whole_decay = jnp.exp(cum_decay[..., -1])[..., None, None]
    transition = whole_decay * jnp.eye(key_vecs.shape[-1], dtype=jnp.float32) - jnp.einsum(
        "...sd,...se->...de", tail_keys, wy_keys, precision=highest
    )
    written = jnp.einsum("...sd,...se->...de", tail_keys, wy_values, precision=highest)
    carry_map = jnp.exp(cum_decay)[..., None] * queries - jnp.einsum(
        "...st,...td->...sd", scores, wy_keys, precision=highest
    )
    local_out = jnp.einsum("...st,...te->...se", scores, wy_values, precision=highest)
    return (transition, written, carry_map, local_out)


def gated_output(produced, zgate, norm_gain):
    tok_rows = produced.shape[0]
    mean_sq = jnp.mean(produced * produced, axis=-1, keepdims=True)
    gate_vals = jax.nn.silu(zgate.astype(jnp.float32).reshape(produced.shape))
    normed = produced * lax.rsqrt(mean_sq + norm_eps) * norm_gain * gate_vals
    return normed.reshape(tok_rows, -1).astype(jnp.bfloat16)


def advance(state_now, per_span):
    transition, written, carry_map, local_out = per_span
    produced = jnp.einsum("hsd,hde->hse", carry_map, state_now, precision=highest) + local_out
    state_next = jnp.einsum("hde,hef->hdf", transition, state_now, precision=highest) + written
    return (state_next, produced)


def apply_shard(trans_mat, state_now, written):
    return jnp.einsum("hde,hef->hdf", trans_mat, state_now, precision=highest) + written


def shard_scan_kernel(
    shard_count, a_ref, b_ref, out_ref, cur_a, cur_b, out_a, out_b, got_a, got_b, send_sems, recv_sems
):
    me = lax.axis_index("seq")
    hg_me = lax.axis_index("hg")
    head_count = a_ref.shape[0]
    distances = []
    distance = 1
    while distance < shard_count:
        distances.append(distance)
        distance *= 2
    barrier = pltpu.get_barrier_semaphore()
    for distance in distances:
        for target in (lax.rem(me + distance, shard_count), lax.rem(me + shard_count - distance, shard_count)):
            pl.semaphore_signal(barrier, inc=1, device_id=(target, hg_me), device_id_type=MESH)
    pl.semaphore_wait(barrier, 2 * len(distances))
    cur_a[0] = a_ref[...]
    cur_b[0] = b_ref[...]
    out_a[0] = a_ref[...].astype(out_a.dtype)
    out_b[0] = b_ref[...].astype(out_b.dtype)
    sem_index = 0
    for round_index, distance in enumerate(distances):
        target = lax.rem(me + distance, shard_count)
        sends_a = round_index + 1 < len(distances)
        copies = [
            pltpu.make_async_remote_copy(
                src_ref=out_b.at[round_index],
                dst_ref=got_b.at[round_index],
                send_sem=send_sems.at[sem_index],
                recv_sem=recv_sems.at[sem_index],
                device_id=(target, hg_me),
                device_id_type=MESH,
            )
        ]
        if sends_a:
            copies.append(
                pltpu.make_async_remote_copy(
                    src_ref=out_a.at[round_index],
                    dst_ref=got_a.at[round_index],
                    send_sem=send_sems.at[sem_index + 1],
                    recv_sem=recv_sems.at[sem_index + 1],
                    device_id=(target, hg_me),
                    device_id_type=MESH,
                )
            )
        sem_index += len(copies)
        for copy in copies:
            copy.start()
        for copy in copies:
            copy.wait()
        has_prev = me >= distance
        for head in range(head_count):
            own_a = cur_a[round_index, head]
            own_b = cur_b[round_index, head]
            joined_b = (
                jnp.dot(own_a, got_b[round_index, head].astype(jnp.float32), precision=highest,
                        preferred_element_type=jnp.float32)
                + own_b
            )
            next_b = jnp.where(has_prev, joined_b, own_b)
            cur_b[round_index + 1, head] = next_b
            out_b[round_index + 1, head] = next_b.astype(out_b.dtype)
            if sends_a:
                joined_a = jnp.dot(own_a, got_a[round_index, head].astype(jnp.float32),
                                   precision=highest, preferred_element_type=jnp.float32)
                next_a = jnp.where(has_prev, joined_a, own_a)
                cur_a[round_index + 1, head] = next_a
                out_a[round_index + 1, head] = next_a.astype(out_a.dtype)
    last = len(distances)
    shift = pltpu.make_async_remote_copy(
        src_ref=out_b.at[last],
        dst_ref=got_b.at[last],
        send_sem=send_sems.at[sem_index],
        recv_sem=recv_sems.at[sem_index],
        device_id=(lax.rem(me + 1, shard_count), hg_me),
        device_id_type=MESH,
    )
    shift.start()
    shift.wait()
    out_ref[...] = jnp.where(me >= 1, got_b[last].astype(jnp.float32), 0.0)


def shard_scan(shard_a, shard_b, shard_count):
    rounds = max(1, (shard_count - 1).bit_length())
    return pl.pallas_call(
        functools.partial(shard_scan_kernel, shard_count),
        out_shape=jax.ShapeDtypeStruct(shard_b.shape, jnp.float32),
        in_specs=[pl.BlockSpec(memory_space=pltpu.VMEM)] * 2,
        out_specs=pl.BlockSpec(memory_space=pltpu.VMEM),
        scratch_shapes=[
            pltpu.VMEM((rounds + 1,) + shard_a.shape, jnp.float32),
            pltpu.VMEM((rounds + 1,) + shard_b.shape, jnp.float32),
            pltpu.VMEM((rounds + 1,) + shard_a.shape, jnp.bfloat16),
            pltpu.VMEM((rounds + 1,) + shard_b.shape, jnp.bfloat16),
            pltpu.VMEM((rounds + 1,) + shard_a.shape, jnp.bfloat16),
            pltpu.VMEM((rounds + 1,) + shard_b.shape, jnp.bfloat16),
            pltpu.SemaphoreType.DMA((2 * rounds + 1,)),
            pltpu.SemaphoreType.DMA((2 * rounds + 1,)),
        ],
        compiler_params=pltpu.CompilerParams(collective_id=1, has_side_effects=True),
    )(shard_a, shard_b)


def span_kernel(q_ref, k_ref, v_ref, gc_ref, gr_ref, bc_ref, trans_ref, written_ref, carry_ref, local_ref):
    queries = q_ref[...]
    key_vecs = k_ref[...]
    values = v_ref[...]
    decay_col = gc_ref[...]
    decay_row = gr_ref[...]
    rate = bc_ref[...]
    block_len = queries.shape[1]
    row_ids = lax.broadcasted_iota(jnp.int32, (1, block_len, block_len), 1)
    col_ids = lax.broadcasted_iota(jnp.int32, (1, block_len, block_len), 2)
    inclusive = row_ids >= col_ids
    strict = row_ids > col_ids
    cum_col = jnp.sum(jnp.where(inclusive, decay_row, 0.0), axis=2, keepdims=True)
    cum_row = jnp.sum(jnp.where(row_ids <= col_ids, decay_col, 0.0), axis=1, keepdims=True)
    gap_mat = cum_col - cum_row
    falloff = jnp.where(inclusive, jnp.exp(jnp.where(inclusive, gap_mat, 0.0)), 0.0)
    key_dots = jnp.einsum("bsd,btd->bst", key_vecs, key_vecs, precision=highest,
                          preferred_element_type=jnp.float32)
    lower_part = jnp.where(strict, rate * falloff * key_dots, 0.0)
    inverse = jnp.where((row_ids // 2 == col_ids // 2) & strict, -lower_part, 0.0) + jnp.where(
        row_ids == col_ids, 1.0, 0.0
    )
    size = 2
    while size < block_len:
        band = (row_ids // (2 * size) == col_ids // (2 * size)) & (row_ids // size != col_ids // size)
        off_blocks = jnp.where(band, lower_part, 0.0)
        step = jnp.einsum("bst,btu->bsu", inverse, off_blocks, precision=highest,
                          preferred_element_type=jnp.float32)
        inverse = inverse - jnp.einsum("bst,btu->bsu", step, inverse, precision=highest,
                                       preferred_element_type=jnp.float32)
        size *= 2
    grow = jnp.exp(cum_col)
    wy_keys = jnp.einsum("bst,btd->bsd", inverse, (rate * grow) * key_vecs, precision=highest,
                         preferred_element_type=jnp.float32)
    wy_values = jnp.einsum("bst,btd->bsd", inverse, rate * values, precision=highest,
                           preferred_element_type=jnp.float32)
    scores = falloff * jnp.einsum("bsd,btd->bst", queries, key_vecs, precision=highest,
                                  preferred_element_type=jnp.float32)
    last = cum_row[:, :, block_len - 1 :]
    tail_keys_t = jnp.swapaxes(jnp.exp(last - cum_col) * key_vecs, 1, 2)
    width = key_vecs.shape[2]
    eye_rows = lax.broadcasted_iota(jnp.int32, (1, width, width), 1)
    eye_cols = lax.broadcasted_iota(jnp.int32, (1, width, width), 2)
    trans_ref[...] = jnp.where(eye_rows == eye_cols, jnp.exp(last), 0.0) - jnp.einsum(
        "bds,bse->bde", tail_keys_t, wy_keys, precision=highest, preferred_element_type=jnp.float32
    )
    written_ref[...] = jnp.einsum("bds,bse->bde", tail_keys_t, wy_values, precision=highest,
                                  preferred_element_type=jnp.float32)
    carry_ref[...] = grow * queries - jnp.einsum("bst,btd->bsd", scores, wy_keys, precision=highest,
                                                 preferred_element_type=jnp.float32)
    local_ref[...] = jnp.einsum("bst,bte->bse", scores, wy_values, precision=highest,
                                preferred_element_type=jnp.float32)


def span_terms_kernel(queries, key_vecs, values, log_decay, write_rate):
    lead = queries.shape[:2]
    block_len, width = queries.shape[2], queries.shape[3]
    flat = lambda x: x.reshape((-1,) + x.shape[2:])
    pairs = lead[0] * lead[1]
    decay = log_decay.reshape(pairs, block_len)
    rate = write_rate.reshape(pairs, block_len)
    outs = pl.pallas_call(
        span_kernel,
        out_shape=[
            jax.ShapeDtypeStruct((pairs, width, width), jnp.float32),
            jax.ShapeDtypeStruct((pairs, width, values.shape[3]), jnp.float32),
            jax.ShapeDtypeStruct((pairs, block_len, width), jnp.float32),
            jax.ShapeDtypeStruct((pairs, block_len, values.shape[3]), jnp.float32),
        ],
        in_specs=[pl.BlockSpec(memory_space=pltpu.VMEM)] * 6,
        out_specs=[pl.BlockSpec(memory_space=pltpu.VMEM)] * 4,
    )(
        flat(queries),
        flat(key_vecs),
        flat(values),
        decay[:, :, None],
        decay[:, None, :],
        rate[:, :, None],
    )
    return tuple(out.reshape(lead + out.shape[1:]) for out in outs)


def group_sum_kernel(group_count, part_ref, out_ref, landed, send_sems, recv_sems, own_sem):
    me = lax.axis_index("hg")
    seq_me = lax.axis_index("seq")
    rows = out_ref.shape[0]
    barrier = pltpu.get_barrier_semaphore()
    for step in range(1, group_count):
        peer = lax.rem(me + step, group_count)
        pl.semaphore_signal(barrier, inc=1, device_id=(seq_me, peer), device_id_type=MESH)
    pl.semaphore_wait(barrier, group_count - 1)
    sends = []
    for step in range(1, group_count):
        peer = lax.rem(me + step, group_count)
        copy = pltpu.make_async_remote_copy(
            src_ref=part_ref.at[pl.ds(pl.multiple_of(peer * rows, 8), rows)],
            dst_ref=landed.at[me],
            send_sem=send_sems.at[step],
            recv_sem=recv_sems.at[me],
            device_id=(seq_me, peer),
            device_id_type=MESH,
        )
        copy.start()
        sends.append(copy)
    own = pltpu.make_async_copy(
        part_ref.at[pl.ds(pl.multiple_of(me * rows, 8), rows)], landed.at[me], own_sem
    )
    own.start()
    own.wait()
    for step in range(1, group_count):
        source = lax.rem(me + group_count - step, group_count)
        pltpu.make_async_remote_copy(
            src_ref=part_ref.at[pl.ds(0, rows)],
            dst_ref=landed.at[source],
            send_sem=send_sems.at[step],
            recv_sem=recv_sems.at[source],
            device_id=(seq_me, source),
            device_id_type=MESH,
        ).wait_recv()
    for copy in sends:
        copy.wait_send()
    total = landed[0].astype(jnp.float32)
    for slot in range(1, group_count):
        total = total + landed[slot].astype(jnp.float32)
    out_ref[...] = total.astype(out_ref.dtype)


def group_sum(part, group_count):
    if group_count == 1:
        return part
    rows = part.shape[0] // group_count
    cols = part.shape[1]
    return pl.pallas_call(
        functools.partial(group_sum_kernel, group_count),
        out_shape=jax.ShapeDtypeStruct((rows, cols), part.dtype),
        in_specs=[pl.BlockSpec(memory_space=pltpu.VMEM)],
        out_specs=pl.BlockSpec(memory_space=pltpu.VMEM),
        scratch_shapes=[
            pltpu.VMEM((group_count, rows, cols), part.dtype),
            pltpu.SemaphoreType.DMA((group_count,)),
            pltpu.SemaphoreType.DMA((group_count,)),
            pltpu.SemaphoreType.DMA,
        ],
        compiler_params=pltpu.CompilerParams(collective_id=0, has_side_effects=True),
    )(part)


def on_device(
    hidden_in,
    w_query,
    w_key,
    w_value,
    w_zgate,
    w_decay,
    w_beta,
    conv_query,
    conv_key,
    conv_value,
    a_log,
    dt_bias,
    norm_gain,
    w_out,
):
    tok_rows = hidden_in.shape[0]
    pre_query, pre_key, pre_value = project_inputs(hidden_in, w_query, w_key, w_value)
    kernel_len = conv_query.shape[0]
    rim_rows = tok_rows - kernel_len + 1
    rim_block = jnp.concatenate(
        [pre_query[rim_rows:], pre_key[rim_rows:], pre_value[rim_rows:]], axis=1
    )
    prior = passed_along(rim_block, "seq", 1)
    queries, key_vecs, values, log_decay, write_rate, zgate = mixer_inputs(
        hidden_in,
        pre_query,
        pre_key,
        pre_value,
        prior,
        conv_query,
        conv_key,
        conv_value,
        w_zgate,
        w_decay,
        w_beta,
        a_log,
        dt_bias,
    )
    terms = span_terms_kernel(
        to_blocks(queries),
        to_blocks(key_vecs),
        to_blocks(values),
        to_blocks(log_decay[..., None])[..., 0],
        to_blocks(write_rate[..., None])[..., 0],
    )
    head_count = values.shape[1]
    identity = jnp.broadcast_to(jnp.eye(DK, dtype=jnp.float32), (head_count, DK, DK))
    empty_state = jnp.zeros((head_count, DK, DV), jnp.float32)

    def compose(carried, per_span):
        prefix_a, prefix_b = carried
        step_trans, step_written, step_carry, step_local = per_span
        local_mix = (
            jnp.einsum("hsd,hde->hse", step_carry, prefix_b, precision=highest) + step_local
        )
        entry_map = jnp.einsum("hsd,hde->hse", step_carry, prefix_a, precision=highest)
        new_a = jnp.einsum("hde,hef->hdf", step_trans, prefix_a, precision=highest)
        new_b = apply_shard(step_trans, prefix_b, step_written)
        return ((new_a, new_b), (local_mix, entry_map))

    (shard_a, shard_b), (local_mix, entry_map) = lax.scan(
        compose, (identity, empty_state), terms, unroll=True
    )

    state_in = shard_scan(shard_a, shard_b, lax.axis_size("seq"))
    produced = local_mix + jnp.einsum("jhsd,hde->jhse", entry_map, state_in, precision=highest)
    produced = produced.transpose(0, 2, 1, 3).reshape(tok_rows, head_count, DV)
    gated = gated_output(produced, zgate, norm_gain)
    part = jnp.dot(gated, w_out, preferred_element_type=jnp.float32).astype(jnp.bfloat16)
    return group_sum(part, lax.axis_size("hg"))


def solution(mesh):
    return jax.shard_map(
        on_device,
        mesh=mesh,
        in_specs=(
            P("seq", None),
            P(None, "hg"),
            P(None, "hg"),
            P(None, "hg"),
            P(None, "hg"),
            P(None, "hg"),
            P(None, "hg"),
            P(None, "hg"),
            P(None, "hg"),
            P(None, "hg"),
            P("hg"),
            P("hg"),
            P(),
            P("hg", None),
        ),
        out_specs=P(("seq", "hg"), None),
        check_vma=False,
    )
```

```python
import functools

import jax
import numpy as np
import jax.numpy as jnp
from jax import lax
from jax.experimental import pallas as pl
from jax.experimental.pallas import tpu as pltpu
from jax.sharding import PartitionSpec as P

MESH = pl.DeviceIdType.MESH

VH = 32
KH = 16
DK = 128
DV = 128
SPAN = 64


highest = lax.Precision.HIGH
norm_eps = 1e-06


def passed_along(block, axis, distance):
    devices = range(lax.axis_size(axis))
    route = [(i - distance, i) for i in devices if i - distance in devices]
    return lax.ppermute(block, axis, route)


def project_inputs(hidden_in, w_query, w_key, w_value):
    pre_query = jnp.dot(hidden_in, w_query, preferred_element_type=jnp.float32).astype(jnp.bfloat16)
    pre_key = jnp.dot(hidden_in, w_key, preferred_element_type=jnp.float32).astype(jnp.bfloat16)
    pre_value = jnp.dot(hidden_in, w_value, preferred_element_type=jnp.float32).astype(jnp.bfloat16)
    return (pre_query, pre_key, pre_value)


def conv_silu(projected, kernel, prior):
    kernel_len = kernel.shape[0]
    tok_rows = projected.shape[0]
    padded = jnp.concatenate([prior.astype(jnp.float32), projected.astype(jnp.float32)], axis=0)
    summed = jnp.zeros((tok_rows, projected.shape[1]), jnp.float32)
    for offset in range(kernel_len):
        summed = summed + kernel[offset].astype(jnp.float32) * padded[offset : offset + tok_rows]
    return jax.nn.silu(summed)


def unit_length(vectors):
    return vectors * lax.rsqrt(jnp.sum(vectors * vectors, axis=-1, keepdims=True) + norm_eps)


def mixer_inputs(
    hidden_in,
    pre_query,
    pre_key,
    pre_value,
    prior,
    conv_query,
    conv_key,
    conv_value,
    w_zgate,
    w_decay,
    w_beta,
    a_log,
    dt_bias,
):
    tok_rows = hidden_in.shape[0]
    query_cols = pre_query.shape[1]
    key_cols = pre_key.shape[1]
    ratio = VH // KH
    queries = unit_length(
        conv_silu(pre_query, conv_query, prior[:, :query_cols]).reshape(tok_rows, -1, DK)
    ) * DK ** (-0.5)
    key_vecs = unit_length(
        conv_silu(pre_key, conv_key, prior[:, query_cols : query_cols + key_cols]).reshape(
            tok_rows, -1, DK
        )
    )
    values = conv_silu(pre_value, conv_value, prior[:, query_cols + key_cols :]).reshape(
        tok_rows, -1, DV
    )
    queries = jnp.repeat(queries, ratio, axis=1)
    key_vecs = jnp.repeat(key_vecs, ratio, axis=1)
    zgate = jnp.dot(hidden_in, w_zgate, preferred_element_type=jnp.float32).astype(jnp.bfloat16)
    rate_logits = jnp.dot(hidden_in, w_decay, preferred_element_type=jnp.float32)
    log_decay = -jnp.exp(a_log) * jax.nn.softplus(rate_logits + dt_bias)
    write_rate = jax.nn.sigmoid(jnp.dot(hidden_in, w_beta, preferred_element_type=jnp.float32))
    return (queries, key_vecs, values, log_decay, write_rate, zgate)


def to_blocks(array_3d):
    tok_rows, head_count = (array_3d.shape[0], array_3d.shape[1])
    return array_3d.reshape(tok_rows // SPAN, SPAN, head_count, -1).transpose(0, 2, 1, 3)


def unit_lower_inverse(lower_part):
    block_len = lower_part.shape[-1]
    row_ids = np.arange(block_len)[:, None]
    col_ids = np.arange(block_len)[None, :]
    first = jnp.asarray((row_ids // 2 == col_ids // 2) & (row_ids != col_ids), jnp.float32)
    inverse = lax.optimization_barrier(
        jnp.asarray(np.eye(block_len), jnp.float32) - lower_part * first
    )
    size = 2
    while size < block_len:
        band = (row_ids // (2 * size) == col_ids // (2 * size)) & (row_ids // size != col_ids // size)
        off_blocks = lower_part * jnp.asarray(band, jnp.float32)
        step = jnp.einsum("...st,...tu->...su", inverse, off_blocks, precision=highest)
        inverse = inverse - jnp.einsum("...st,...tu->...su", step, inverse, precision=highest)
        size *= 2
    return inverse


def span_terms(queries, key_vecs, values, log_decay, write_rate):
    block_len = log_decay.shape[-1]
    cum_decay = jnp.cumsum(log_decay, axis=-1)
    row_ids = lax.broadcasted_iota(jnp.int32, (block_len, block_len), 0)
    col_ids = lax.broadcasted_iota(jnp.int32, (block_len, block_len), 1)
    inclusive = row_ids >= col_ids
    strict = row_ids > col_ids
    gap_mat = cum_decay[..., :, None] - cum_decay[..., None, :]
    falloff = jnp.where(inclusive, jnp.exp(jnp.where(inclusive, gap_mat, 0.0)), 0.0)
    key_dots = jnp.einsum("...sd,...td->...st", key_vecs, key_vecs, precision=highest)
    lower_part = jnp.where(strict, write_rate[..., :, None] * falloff * key_dots, 0.0)
    inverse = unit_lower_inverse(lower_part)
    wy_keys = jnp.einsum(
        "...st,...td->...sd",
        inverse,
        (write_rate * jnp.exp(cum_decay))[..., None] * key_vecs,
        precision=highest,
    )
    wy_values = jnp.einsum(
        "...st,...td->...sd", inverse, write_rate[..., None] * values, precision=highest
    )
    scores = falloff * jnp.einsum("...sd,...td->...st", queries, key_vecs, precision=highest)
    tail_keys = jnp.exp(cum_decay[..., -1:] - cum_decay)[..., None] * key_vecs
    whole_decay = jnp.exp(cum_decay[..., -1])[..., None, None]
    transition = whole_decay * jnp.eye(key_vecs.shape[-1], dtype=jnp.float32) - jnp.einsum(
        "...sd,...se->...de", tail_keys, wy_keys, precision=highest
    )
    written = jnp.einsum("...sd,...se->...de", tail_keys, wy_values, precision=highest)
    carry_map = jnp.exp(cum_decay)[..., None] * queries - jnp.einsum(
        "...st,...td->...sd", scores, wy_keys, precision=highest
    )
    local_out = jnp.einsum("...st,...te->...se", scores, wy_values, precision=highest)
    return (transition, written, carry_map, local_out)


def gated_output(produced, zgate, norm_gain):
    tok_rows = produced.shape[0]
    mean_sq = jnp.mean(produced * produced, axis=-1, keepdims=True)
    gate_vals = jax.nn.silu(zgate.astype(jnp.float32).reshape(produced.shape))
    normed = produced * lax.rsqrt(mean_sq + norm_eps) * norm_gain * gate_vals
    return normed.reshape(tok_rows, -1).astype(jnp.bfloat16)


def advance(state_now, per_span):
    transition, written, carry_map, local_out = per_span
    produced = jnp.einsum("hsd,hde->hse", carry_map, state_now, precision=highest) + local_out
    state_next = jnp.einsum("hde,hef->hdf", transition, state_now, precision=highest) + written
    return (state_next, produced)


def apply_shard(trans_mat, state_now, written):
    return jnp.einsum("hde,hef->hdf", trans_mat, state_now, precision=highest) + written


def shard_scan_kernel(
    shard_count, a_ref, b_ref, out_ref, cur_a, cur_b, out_a, out_b, got_a, got_b, send_sems, recv_sems
):
    me = lax.axis_index("seq")
    hg_me = lax.axis_index("hg")
    head_count = a_ref.shape[0]
    distances = []
    distance = 1
    while distance < shard_count:
        distances.append(distance)
        distance *= 2
    barrier = pltpu.get_barrier_semaphore()
    for distance in distances:
        for target in (lax.rem(me + distance, shard_count), lax.rem(me + shard_count - distance, shard_count)):
            pl.semaphore_signal(barrier, inc=1, device_id=(target, hg_me), device_id_type=MESH)
    pl.semaphore_wait(barrier, 2 * len(distances))
    cur_a[0] = a_ref[...]
    cur_b[0] = b_ref[...]
    out_a[0] = a_ref[...].astype(out_a.dtype)
    out_b[0] = b_ref[...].astype(out_b.dtype)
    sem_index = 0
    for round_index, distance in enumerate(distances):
        target = lax.rem(me + distance, shard_count)
        sends_a = round_index + 1 < len(distances)
        copies = [
            pltpu.make_async_remote_copy(
                src_ref=out_b.at[round_index],
                dst_ref=got_b.at[round_index],
                send_sem=send_sems.at[sem_index],
                recv_sem=recv_sems.at[sem_index],
                device_id=(target, hg_me),
                device_id_type=MESH,
            )
        ]
        if sends_a:
            copies.append(
                pltpu.make_async_remote_copy(
                    src_ref=out_a.at[round_index],
                    dst_ref=got_a.at[round_index],
                    send_sem=send_sems.at[sem_index + 1],
                    recv_sem=recv_sems.at[sem_index + 1],
                    device_id=(target, hg_me),
                    device_id_type=MESH,
                )
            )
        sem_index += len(copies)
        for copy in copies:
            copy.start()
        for copy in copies:
            copy.wait()
        has_prev = me >= distance
        for head in range(head_count):
            own_a = cur_a[round_index, head]
            own_b = cur_b[round_index, head]
            joined_b = (
                jnp.dot(own_a, got_b[round_index, head].astype(jnp.float32), precision=highest,
                        preferred_element_type=jnp.float32)
                + own_b
            )
            next_b = jnp.where(has_prev, joined_b, own_b)
            cur_b[round_index + 1, head] = next_b
            out_b[round_index + 1, head] = next_b.astype(out_b.dtype)
            if sends_a:
                joined_a = jnp.dot(own_a, got_a[round_index, head].astype(jnp.float32),
                                   precision=highest, preferred_element_type=jnp.float32)
                next_a = jnp.where(has_prev, joined_a, own_a)
                cur_a[round_index + 1, head] = next_a
                out_a[round_index + 1, head] = next_a.astype(out_a.dtype)
    last = len(distances)
    shift = pltpu.make_async_remote_copy(
        src_ref=out_b.at[last],
        dst_ref=got_b.at[last],
        send_sem=send_sems.at[sem_index],
        recv_sem=recv_sems.at[sem_index],
        device_id=(lax.rem(me + 1, shard_count), hg_me),
        device_id_type=MESH,
    )
    shift.start()
    shift.wait()
    out_ref[...] = jnp.where(me >= 1, got_b[last].astype(jnp.float32), 0.0)


def shard_scan(shard_a, shard_b, shard_count):
    rounds = max(1, (shard_count - 1).bit_length())
    return pl.pallas_call(
        functools.partial(shard_scan_kernel, shard_count),
        out_shape=jax.ShapeDtypeStruct(shard_b.shape, jnp.float32),
        in_specs=[pl.BlockSpec(memory_space=pltpu.VMEM)] * 2,
        out_specs=pl.BlockSpec(memory_space=pltpu.VMEM),
        scratch_shapes=[
            pltpu.VMEM((rounds + 1,) + shard_a.shape, jnp.float32),
            pltpu.VMEM((rounds + 1,) + shard_b.shape, jnp.float32),
            pltpu.VMEM((rounds + 1,) + shard_a.shape, jnp.bfloat16),
            pltpu.VMEM((rounds + 1,) + shard_b.shape, jnp.bfloat16),
            pltpu.VMEM((rounds + 1,) + shard_a.shape, jnp.bfloat16),
            pltpu.VMEM((rounds + 1,) + shard_b.shape, jnp.bfloat16),
            pltpu.SemaphoreType.DMA((2 * rounds + 1,)),
            pltpu.SemaphoreType.DMA((2 * rounds + 1,)),
        ],
        compiler_params=pltpu.CompilerParams(collective_id=1, has_side_effects=True),
    )(shard_a, shard_b)


def span_kernel(
    head_count, q_ref, k_ref, v_ref, gc_ref, gr_ref, bc_ref, shard_a_ref, shard_b_ref, mix_ref, entry_ref
):
    queries = q_ref[...]
    key_vecs = k_ref[...]
    values = v_ref[...]
    decay_col = gc_ref[...]
    decay_row = gr_ref[...]
    rate = bc_ref[...]
    block_len = queries.shape[1]
    row_ids = lax.broadcasted_iota(jnp.int32, (1, block_len, block_len), 1)
    col_ids = lax.broadcasted_iota(jnp.int32, (1, block_len, block_len), 2)
    inclusive = row_ids >= col_ids
    strict = row_ids > col_ids
    cum_col = jnp.sum(jnp.where(inclusive, decay_row, 0.0), axis=2, keepdims=True)
    cum_row = jnp.sum(jnp.where(row_ids <= col_ids, decay_col, 0.0), axis=1, keepdims=True)
    gap_mat = cum_col - cum_row
    falloff = jnp.where(inclusive, jnp.exp(jnp.where(inclusive, gap_mat, 0.0)), 0.0)
    key_dots = jnp.einsum("bsd,btd->bst", key_vecs, key_vecs, precision=highest,
                          preferred_element_type=jnp.float32)
    lower_part = jnp.where(strict, rate * falloff * key_dots, 0.0)
    inverse = jnp.where((row_ids // 2 == col_ids // 2) & strict, -lower_part, 0.0) + jnp.where(
        row_ids == col_ids, 1.0, 0.0
    )
    size = 2
    while size < block_len:
        band = (row_ids // (2 * size) == col_ids // (2 * size)) & (row_ids // size != col_ids // size)
        off_blocks = jnp.where(band, lower_part, 0.0)
        step = jnp.einsum("bst,btu->bsu", inverse, off_blocks, precision=highest,
                          preferred_element_type=jnp.float32)
        inverse = inverse - jnp.einsum("bst,btu->bsu", step, inverse, precision=highest,
                                       preferred_element_type=jnp.float32)
        size *= 2
    grow = jnp.exp(cum_col)
    wy_keys = jnp.einsum("bst,btd->bsd", inverse, (rate * grow) * key_vecs, precision=highest,
                         preferred_element_type=jnp.float32)
    wy_values = jnp.einsum("bst,btd->bsd", inverse, rate * values, precision=highest,
                           preferred_element_type=jnp.float32)
    scores = falloff * jnp.einsum("bsd,btd->bst", queries, key_vecs, precision=highest,
                                  preferred_element_type=jnp.float32)
    last = cum_row[:, :, block_len - 1 :]
    tail_keys_t = jnp.swapaxes(jnp.exp(last - cum_col) * key_vecs, 1, 2)
    width = key_vecs.shape[2]
    eye_rows = lax.broadcasted_iota(jnp.int32, (1, width, width), 1)
    eye_cols = lax.broadcasted_iota(jnp.int32, (1, width, width), 2)
    transition = jnp.where(eye_rows == eye_cols, jnp.exp(last), 0.0) - jnp.einsum(
        "bds,bse->bde", tail_keys_t, wy_keys, precision=highest, preferred_element_type=jnp.float32
    )
    written = jnp.einsum("bds,bse->bde", tail_keys_t, wy_values, precision=highest,
                         preferred_element_type=jnp.float32)
    carry_map = grow * queries - jnp.einsum("bst,btd->bsd", scores, wy_keys, precision=highest,
                                            preferred_element_type=jnp.float32)
    local_out = jnp.einsum("bst,bte->bse", scores, wy_values, precision=highest,
                           preferred_element_type=jnp.float32)
    for span in range(queries.shape[0] // head_count):
        heads = slice(span * head_count, (span + 1) * head_count)
        if span == 0:
            mix_ref[heads] = local_out[heads]
            entry_ref[heads] = carry_map[heads]
            prefix_a = transition[heads]
            prefix_b = written[heads]
            continue
        mix_ref[heads] = local_out[heads] + jnp.einsum(
            "hsd,hde->hse", carry_map[heads], prefix_b, precision=highest,
            preferred_element_type=jnp.float32)
        entry_ref[heads] = jnp.einsum("hsd,hde->hse", carry_map[heads], prefix_a, precision=highest,
                                      preferred_element_type=jnp.float32)
        prefix_b = written[heads] + jnp.einsum(
            "hde,hef->hdf", transition[heads], prefix_b, precision=highest,
            preferred_element_type=jnp.float32)
        prefix_a = jnp.einsum("hde,hef->hdf", transition[heads], prefix_a, precision=highest,
                              preferred_element_type=jnp.float32)
    shard_a_ref[...] = prefix_a
    shard_b_ref[...] = prefix_b


def span_terms_kernel(queries, key_vecs, values, log_decay, write_rate):
    lead = queries.shape[:2]
    block_len, width = queries.shape[2], queries.shape[3]
    flat = lambda x: x.reshape((-1,) + x.shape[2:])
    pairs = lead[0] * lead[1]
    decay = log_decay.reshape(pairs, block_len)
    rate = write_rate.reshape(pairs, block_len)
    shard_a, shard_b, local_mix, entry_map = pl.pallas_call(
        functools.partial(span_kernel, lead[1]),
        out_shape=[
            jax.ShapeDtypeStruct((lead[1], width, width), jnp.float32),
            jax.ShapeDtypeStruct((lead[1], width, values.shape[3]), jnp.float32),
            jax.ShapeDtypeStruct((pairs, block_len, values.shape[3]), jnp.float32),
            jax.ShapeDtypeStruct((pairs, block_len, width), jnp.float32),
        ],
        in_specs=[pl.BlockSpec(memory_space=pltpu.VMEM)] * 6,
        out_specs=[pl.BlockSpec(memory_space=pltpu.VMEM)] * 4,
    )(
        flat(queries),
        flat(key_vecs),
        flat(values),
        decay[:, :, None],
        decay[:, None, :],
        rate[:, :, None],
    )
    return (
        shard_a,
        shard_b,
        local_mix.reshape(lead + local_mix.shape[1:]),
        entry_map.reshape(lead + entry_map.shape[1:]),
    )


def group_sum_kernel(group_count, part_ref, out_ref, landed, send_sems, recv_sems, own_sem):
    me = lax.axis_index("hg")
    seq_me = lax.axis_index("seq")
    rows = out_ref.shape[0]
    barrier = pltpu.get_barrier_semaphore()
    for step in range(1, group_count):
        peer = lax.rem(me + step, group_count)
        pl.semaphore_signal(barrier, inc=1, device_id=(seq_me, peer), device_id_type=MESH)
    pl.semaphore_wait(barrier, group_count - 1)
    sends = []
    for step in range(1, group_count):
        peer = lax.rem(me + step, group_count)
        copy = pltpu.make_async_remote_copy(
            src_ref=part_ref.at[pl.ds(pl.multiple_of(peer * rows, 8), rows)],
            dst_ref=landed.at[me],
            send_sem=send_sems.at[step],
            recv_sem=recv_sems.at[me],
            device_id=(seq_me, peer),
            device_id_type=MESH,
        )
        copy.start()
        sends.append(copy)
    own = pltpu.make_async_copy(
        part_ref.at[pl.ds(pl.multiple_of(me * rows, 8), rows)], landed.at[me], own_sem
    )
    own.start()
    own.wait()
    for step in range(1, group_count):
        source = lax.rem(me + group_count - step, group_count)
        pltpu.make_async_remote_copy(
            src_ref=part_ref.at[pl.ds(0, rows)],
            dst_ref=landed.at[source],
            send_sem=send_sems.at[step],
            recv_sem=recv_sems.at[source],
            device_id=(seq_me, source),
            device_id_type=MESH,
        ).wait_recv()
    for copy in sends:
        copy.wait_send()
    total = landed[0].astype(jnp.float32)
    for slot in range(1, group_count):
        total = total + landed[slot].astype(jnp.float32)
    out_ref[...] = total.astype(out_ref.dtype)


def group_sum(part, group_count):
    if group_count == 1:
        return part
    rows = part.shape[0] // group_count
    cols = part.shape[1]
    return pl.pallas_call(
        functools.partial(group_sum_kernel, group_count),
        out_shape=jax.ShapeDtypeStruct((rows, cols), part.dtype),
        in_specs=[pl.BlockSpec(memory_space=pltpu.VMEM)],
        out_specs=pl.BlockSpec(memory_space=pltpu.VMEM),
        scratch_shapes=[
            pltpu.VMEM((group_count, rows, cols), part.dtype),
            pltpu.SemaphoreType.DMA((group_count,)),
            pltpu.SemaphoreType.DMA((group_count,)),
            pltpu.SemaphoreType.DMA,
        ],
        compiler_params=pltpu.CompilerParams(collective_id=0, has_side_effects=True),
    )(part)


def on_device(
    hidden_in,
    w_query,
    w_key,
    w_value,
    w_zgate,
    w_decay,
    w_beta,
    conv_query,
    conv_key,
    conv_value,
    a_log,
    dt_bias,
    norm_gain,
    w_out,
):
    tok_rows = hidden_in.shape[0]
    pre_query, pre_key, pre_value = project_inputs(hidden_in, w_query, w_key, w_value)
    kernel_len = conv_query.shape[0]
    rim_rows = tok_rows - kernel_len + 1
    rim_block = jnp.concatenate(
        [pre_query[rim_rows:], pre_key[rim_rows:], pre_value[rim_rows:]], axis=1
    )
    prior = passed_along(rim_block, "seq", 1)
    queries, key_vecs, values, log_decay, write_rate, zgate = mixer_inputs(
        hidden_in,
        pre_query,
        pre_key,
        pre_value,
        prior,
        conv_query,
        conv_key,
        conv_value,
        w_zgate,
        w_decay,
        w_beta,
        a_log,
        dt_bias,
    )
    shard_a, shard_b, local_mix, entry_map = span_terms_kernel(
        to_blocks(queries),
        to_blocks(key_vecs),
        to_blocks(values),
        to_blocks(log_decay[..., None])[..., 0],
        to_blocks(write_rate[..., None])[..., 0],
    )
    head_count = values.shape[1]
    state_in = shard_scan(shard_a, shard_b, lax.axis_size("seq"))
    produced = local_mix + jnp.einsum("jhsd,hde->jhse", entry_map, state_in, precision=highest)
    produced = produced.transpose(0, 2, 1, 3).reshape(tok_rows, head_count, DV)
    gated = gated_output(produced, zgate, norm_gain)
    part = jnp.dot(gated, w_out, preferred_element_type=jnp.float32).astype(jnp.bfloat16)
    return group_sum(part, lax.axis_size("hg"))


def solution(mesh):
    return jax.shard_map(
        on_device,
        mesh=mesh,
        in_specs=(
            P("seq", None),
            P(None, "hg"),
            P(None, "hg"),
            P(None, "hg"),
            P(None, "hg"),
            P(None, "hg"),
            P(None, "hg"),
            P(None, "hg"),
            P(None, "hg"),
            P(None, "hg"),
            P("hg"),
            P("hg"),
            P(),
            P("hg", None),
        ),
        out_specs=P(("seq", "hg"), None),
        check_vma=False,
    )
```

```python
import functools

import jax
import numpy as np
import jax.numpy as jnp
from jax import lax
from jax.experimental import pallas as pl
from jax.experimental.pallas import tpu as pltpu
from jax.sharding import PartitionSpec as P

MESH = pl.DeviceIdType.MESH

VH = 32
KH = 16
DK = 128
DV = 128
SPAN = 64


highest = lax.Precision.HIGH
norm_eps = 1e-06


def passed_along(block, axis, distance):
    devices = range(lax.axis_size(axis))
    route = [(i - distance, i) for i in devices if i - distance in devices]
    return lax.ppermute(block, axis, route)


def project_inputs(hidden_in, w_query, w_key, w_value):
    pre_query = jnp.dot(hidden_in, w_query, preferred_element_type=jnp.float32).astype(jnp.bfloat16)
    pre_key = jnp.dot(hidden_in, w_key, preferred_element_type=jnp.float32).astype(jnp.bfloat16)
    pre_value = jnp.dot(hidden_in, w_value, preferred_element_type=jnp.float32).astype(jnp.bfloat16)
    return (pre_query, pre_key, pre_value)


def conv_silu(projected, kernel, prior):
    kernel_len = kernel.shape[0]
    tok_rows = projected.shape[0]
    padded = jnp.concatenate([prior.astype(jnp.float32), projected.astype(jnp.float32)], axis=0)
    summed = jnp.zeros((tok_rows, projected.shape[1]), jnp.float32)
    for offset in range(kernel_len):
        summed = summed + kernel[offset].astype(jnp.float32) * padded[offset : offset + tok_rows]
    return jax.nn.silu(summed)


def unit_length(vectors):
    return vectors * lax.rsqrt(jnp.sum(vectors * vectors, axis=-1, keepdims=True) + norm_eps)


def mixer_inputs(
    hidden_in,
    pre_query,
    pre_key,
    pre_value,
    prior,
    conv_query,
    conv_key,
    conv_value,
    w_zgate,
    w_decay,
    w_beta,
    a_log,
    dt_bias,
):
    tok_rows = hidden_in.shape[0]
    query_cols = pre_query.shape[1]
    key_cols = pre_key.shape[1]
    ratio = VH // KH
    queries = unit_length(
        conv_silu(pre_query, conv_query, prior[:, :query_cols]).reshape(tok_rows, -1, DK)
    ) * DK ** (-0.5)
    key_vecs = unit_length(
        conv_silu(pre_key, conv_key, prior[:, query_cols : query_cols + key_cols]).reshape(
            tok_rows, -1, DK
        )
    )
    values = conv_silu(pre_value, conv_value, prior[:, query_cols + key_cols :]).reshape(
        tok_rows, -1, DV
    )
    queries = jnp.repeat(queries, ratio, axis=1)
    key_vecs = jnp.repeat(key_vecs, ratio, axis=1)
    zgate = jnp.dot(hidden_in, w_zgate, preferred_element_type=jnp.float32).astype(jnp.bfloat16)
    rate_logits = jnp.dot(hidden_in, w_decay, preferred_element_type=jnp.float32)
    log_decay = -jnp.exp(a_log) * jax.nn.softplus(rate_logits + dt_bias)
    write_rate = jax.nn.sigmoid(jnp.dot(hidden_in, w_beta, preferred_element_type=jnp.float32))
    return (queries, key_vecs, values, log_decay, write_rate, zgate)


def to_blocks(array_3d):
    tok_rows, head_count = (array_3d.shape[0], array_3d.shape[1])
    return array_3d.reshape(tok_rows // SPAN, SPAN, head_count, -1).transpose(0, 2, 1, 3)


def unit_lower_inverse(lower_part):
    block_len = lower_part.shape[-1]
    row_ids = np.arange(block_len)[:, None]
    col_ids = np.arange(block_len)[None, :]
    first = jnp.asarray((row_ids // 2 == col_ids // 2) & (row_ids != col_ids), jnp.float32)
    inverse = lax.optimization_barrier(
        jnp.asarray(np.eye(block_len), jnp.float32) - lower_part * first
    )
    size = 2
    while size < block_len:
        band = (row_ids // (2 * size) == col_ids // (2 * size)) & (row_ids // size != col_ids // size)
        off_blocks = lower_part * jnp.asarray(band, jnp.float32)
        step = jnp.einsum("...st,...tu->...su", inverse, off_blocks, precision=highest)
        inverse = inverse - jnp.einsum("...st,...tu->...su", step, inverse, precision=highest)
        size *= 2
    return inverse


def span_terms(queries, key_vecs, values, log_decay, write_rate):
    block_len = log_decay.shape[-1]
    cum_decay = jnp.cumsum(log_decay, axis=-1)
    row_ids = lax.broadcasted_iota(jnp.int32, (block_len, block_len), 0)
    col_ids = lax.broadcasted_iota(jnp.int32, (block_len, block_len), 1)
    inclusive = row_ids >= col_ids
    strict = row_ids > col_ids
    gap_mat = cum_decay[..., :, None] - cum_decay[..., None, :]
    falloff = jnp.where(inclusive, jnp.exp(jnp.where(inclusive, gap_mat, 0.0)), 0.0)
    key_dots = jnp.einsum("...sd,...td->...st", key_vecs, key_vecs, precision=highest)
    lower_part = jnp.where(strict, write_rate[..., :, None] * falloff * key_dots, 0.0)
    inverse = unit_lower_inverse(lower_part)
    wy_keys = jnp.einsum(
        "...st,...td->...sd",
        inverse,
        (write_rate * jnp.exp(cum_decay))[..., None] * key_vecs,
        precision=highest,
    )
    wy_values = jnp.einsum(
        "...st,...td->...sd", inverse, write_rate[..., None] * values, precision=highest
    )
    scores = falloff * jnp.einsum("...sd,...td->...st", queries, key_vecs, precision=highest)
    tail_keys = jnp.exp(cum_decay[..., -1:] - cum_decay)[..., None] * key_vecs
    whole_decay = jnp.exp(cum_decay[..., -1])[..., None, None]
    transition = whole_decay * jnp.eye(key_vecs.shape[-1], dtype=jnp.float32) - jnp.einsum(
        "...sd,...se->...de", tail_keys, wy_keys, precision=highest
    )
    written = jnp.einsum("...sd,...se->...de", tail_keys, wy_values, precision=highest)
    carry_map = jnp.exp(cum_decay)[..., None] * queries - jnp.einsum(
        "...st,...td->...sd", scores, wy_keys, precision=highest
    )
    local_out = jnp.einsum("...st,...te->...se", scores, wy_values, precision=highest)
    return (transition, written, carry_map, local_out)


def gated_output(produced, zgate, norm_gain):
    tok_rows = produced.shape[0]
    mean_sq = jnp.mean(produced * produced, axis=-1, keepdims=True)
    gate_vals = jax.nn.silu(zgate.astype(jnp.float32).reshape(produced.shape))
    normed = produced * lax.rsqrt(mean_sq + norm_eps) * norm_gain * gate_vals
    return normed.reshape(tok_rows, -1).astype(jnp.bfloat16)


def advance(state_now, per_span):
    transition, written, carry_map, local_out = per_span
    produced = jnp.einsum("hsd,hde->hse", carry_map, state_now, precision=highest) + local_out
    state_next = jnp.einsum("hde,hef->hdf", transition, state_now, precision=highest) + written
    return (state_next, produced)


def apply_shard(trans_mat, state_now, written):
    return jnp.einsum("hde,hef->hdf", trans_mat, state_now, precision=highest) + written


def shard_scan_kernel(
    shard_count, a_ref, b_ref, out_ref, cur_a, cur_b, out_a, out_b, got_a, got_b, send_sems, recv_sems
):
    me = lax.axis_index("seq")
    hg_me = lax.axis_index("hg")
    head_count = a_ref.shape[0]
    distances = []
    distance = 1
    while distance < shard_count:
        distances.append(distance)
        distance *= 2
    barrier = pltpu.get_barrier_semaphore()
    for distance in distances:
        for target in (lax.rem(me + distance, shard_count), lax.rem(me + shard_count - distance, shard_count)):
            pl.semaphore_signal(barrier, inc=1, device_id=(target, hg_me), device_id_type=MESH)
    pl.semaphore_wait(barrier, 2 * len(distances))
    cur_a[0] = a_ref[...]
    cur_b[0] = b_ref[...]
    out_a[0] = a_ref[...].astype(out_a.dtype)
    out_b[0] = b_ref[...].astype(out_b.dtype)
    sem_index = 0
    for round_index, distance in enumerate(distances):
        target = lax.rem(me + distance, shard_count)
        sends_a = round_index + 1 < len(distances)
        copies = [
            pltpu.make_async_remote_copy(
                src_ref=out_b.at[round_index],
                dst_ref=got_b.at[round_index],
                send_sem=send_sems.at[sem_index],
                recv_sem=recv_sems.at[sem_index],
                device_id=(target, hg_me),
                device_id_type=MESH,
            )
        ]
        if sends_a:
            copies.append(
                pltpu.make_async_remote_copy(
                    src_ref=out_a.at[round_index],
                    dst_ref=got_a.at[round_index],
                    send_sem=send_sems.at[sem_index + 1],
                    recv_sem=recv_sems.at[sem_index + 1],
                    device_id=(target, hg_me),
                    device_id_type=MESH,
                )
            )
        sem_index += len(copies)
        for copy in copies:
            copy.start()
        for copy in copies:
            copy.wait()
        has_prev = me >= distance
        for head in range(head_count):
            own_a = cur_a[round_index, head]
            own_b = cur_b[round_index, head]
            joined_b = (
                jnp.dot(own_a, got_b[round_index, head].astype(jnp.float32), precision=highest,
                        preferred_element_type=jnp.float32)
                + own_b
            )
            next_b = jnp.where(has_prev, joined_b, own_b)
            cur_b[round_index + 1, head] = next_b
            out_b[round_index + 1, head] = next_b.astype(out_b.dtype)
            if sends_a:
                joined_a = jnp.dot(own_a, got_a[round_index, head].astype(jnp.float32),
                                   precision=highest, preferred_element_type=jnp.float32)
                next_a = jnp.where(has_prev, joined_a, own_a)
                cur_a[round_index + 1, head] = next_a
                out_a[round_index + 1, head] = next_a.astype(out_a.dtype)
    last = len(distances)
    shift = pltpu.make_async_remote_copy(
        src_ref=out_b.at[last],
        dst_ref=got_b.at[last],
        send_sem=send_sems.at[sem_index],
        recv_sem=recv_sems.at[sem_index],
        device_id=(lax.rem(me + 1, shard_count), hg_me),
        device_id_type=MESH,
    )
    shift.start()
    shift.wait()
    out_ref[...] = jnp.where(me >= 1, got_b[last].astype(jnp.float32), 0.0)


def shard_scan(shard_a, shard_b, shard_count):
    rounds = max(1, (shard_count - 1).bit_length())
    return pl.pallas_call(
        functools.partial(shard_scan_kernel, shard_count),
        out_shape=jax.ShapeDtypeStruct(shard_b.shape, jnp.float32),
        in_specs=[pl.BlockSpec(memory_space=pltpu.VMEM)] * 2,
        out_specs=pl.BlockSpec(memory_space=pltpu.VMEM),
        scratch_shapes=[
            pltpu.VMEM((rounds + 1,) + shard_a.shape, jnp.float32),
            pltpu.VMEM((rounds + 1,) + shard_b.shape, jnp.float32),
            pltpu.VMEM((rounds + 1,) + shard_a.shape, jnp.bfloat16),
            pltpu.VMEM((rounds + 1,) + shard_b.shape, jnp.bfloat16),
            pltpu.VMEM((rounds + 1,) + shard_a.shape, jnp.bfloat16),
            pltpu.VMEM((rounds + 1,) + shard_b.shape, jnp.bfloat16),
            pltpu.SemaphoreType.DMA((2 * rounds + 1,)),
            pltpu.SemaphoreType.DMA((2 * rounds + 1,)),
        ],
        compiler_params=pltpu.CompilerParams(collective_id=1, has_side_effects=True),
    )(shard_a, shard_b)


def span_kernel(
    head_count, q_ref, k_ref, v_ref, gc_ref, gr_ref, bc_ref, shard_a_ref, shard_b_ref, mix_ref, entry_ref
):
    queries = q_ref[...]
    key_vecs = k_ref[...]
    values = v_ref[...]
    decay_col = gc_ref[...]
    decay_row = gr_ref[...]
    rate = bc_ref[...]
    block_len = queries.shape[1]
    row_ids = lax.broadcasted_iota(jnp.int32, (1, block_len, block_len), 1)
    col_ids = lax.broadcasted_iota(jnp.int32, (1, block_len, block_len), 2)
    inclusive = row_ids >= col_ids
    strict = row_ids > col_ids
    cum_col = jnp.sum(jnp.where(inclusive, decay_row, 0.0), axis=2, keepdims=True)
    cum_row = jnp.sum(jnp.where(row_ids <= col_ids, decay_col, 0.0), axis=1, keepdims=True)
    gap_mat = cum_col - cum_row
    falloff = jnp.where(inclusive, jnp.exp(jnp.where(inclusive, gap_mat, 0.0)), 0.0)
    key_dots = jnp.einsum("bsd,btd->bst", key_vecs, key_vecs, precision=highest,
                          preferred_element_type=jnp.float32)
    lower_part = jnp.where(strict, rate * falloff * key_dots, 0.0)
    inverse = jnp.where((row_ids // 2 == col_ids // 2) & strict, -lower_part, 0.0) + jnp.where(
        row_ids == col_ids, 1.0, 0.0
    )
    size = 2
    while size < block_len:
        band = (row_ids // (2 * size) == col_ids // (2 * size)) & (row_ids // size != col_ids // size)
        off_blocks = jnp.where(band, lower_part, 0.0)
        step = jnp.einsum("bst,btu->bsu", inverse, off_blocks, precision=highest,
                          preferred_element_type=jnp.float32)
        inverse = inverse - jnp.einsum("bst,btu->bsu", step, inverse, precision=highest,
                                       preferred_element_type=jnp.float32)
        size *= 2
    grow = jnp.exp(cum_col)
    wy_keys = jnp.einsum("bst,btd->bsd", inverse, (rate * grow) * key_vecs, precision=highest,
                         preferred_element_type=jnp.float32)
    wy_values = jnp.einsum("bst,btd->bsd", inverse, rate * values, precision=highest,
                           preferred_element_type=jnp.float32)
    scores = falloff * jnp.einsum("bsd,btd->bst", queries, key_vecs, precision=highest,
                                  preferred_element_type=jnp.float32)
    last = cum_row[:, :, block_len - 1 :]
    tail_keys_t = jnp.swapaxes(jnp.exp(last - cum_col) * key_vecs, 1, 2)
    width = key_vecs.shape[2]
    eye_rows = lax.broadcasted_iota(jnp.int32, (1, width, width), 1)
    eye_cols = lax.broadcasted_iota(jnp.int32, (1, width, width), 2)
    transition = jnp.where(eye_rows == eye_cols, jnp.exp(last), 0.0) - jnp.einsum(
        "bds,bse->bde", tail_keys_t, wy_keys, precision=highest, preferred_element_type=jnp.float32
    )
    written = jnp.einsum("bds,bse->bde", tail_keys_t, wy_values, precision=highest,
                         preferred_element_type=jnp.float32)
    carry_map = grow * queries - jnp.einsum("bst,btd->bsd", scores, wy_keys, precision=highest,
                                            preferred_element_type=jnp.float32)
    local_out = jnp.einsum("bst,bte->bse", scores, wy_values, precision=highest,
                           preferred_element_type=jnp.float32)
    for span in range(queries.shape[0] // head_count):
        heads = slice(span * head_count, (span + 1) * head_count)
        if span == 0:
            mix_ref[heads] = local_out[heads]
            entry_ref[heads] = carry_map[heads]
            prefix_a = transition[heads]
            prefix_b = written[heads]
            continue
        mix_ref[heads] = local_out[heads] + jnp.einsum(
            "hsd,hde->hse", carry_map[heads], prefix_b, precision=highest,
            preferred_element_type=jnp.float32)
        entry_ref[heads] = jnp.einsum("hsd,hde->hse", carry_map[heads], prefix_a, precision=highest,
                                      preferred_element_type=jnp.float32)
        prefix_b = written[heads] + jnp.einsum(
            "hde,hef->hdf", transition[heads], prefix_b, precision=highest,
            preferred_element_type=jnp.float32)
        prefix_a = jnp.einsum("hde,hef->hdf", transition[heads], prefix_a, precision=highest,
                              preferred_element_type=jnp.float32)
    shard_a_ref[...] = prefix_a
    shard_b_ref[...] = prefix_b


def span_terms_kernel(queries, key_vecs, values, log_decay, write_rate):
    lead = queries.shape[:2]
    block_len, width = queries.shape[2], queries.shape[3]
    flat = lambda x: x.reshape((-1,) + x.shape[2:])
    pairs = lead[0] * lead[1]
    decay = log_decay.reshape(pairs, block_len)
    rate = write_rate.reshape(pairs, block_len)
    shard_a, shard_b, local_mix, entry_map = pl.pallas_call(
        functools.partial(span_kernel, lead[1]),
        out_shape=[
            jax.ShapeDtypeStruct((lead[1], width, width), jnp.float32),
            jax.ShapeDtypeStruct((lead[1], width, values.shape[3]), jnp.float32),
            jax.ShapeDtypeStruct((pairs, block_len, values.shape[3]), jnp.float32),
            jax.ShapeDtypeStruct((pairs, block_len, width), jnp.float32),
        ],
        in_specs=[pl.BlockSpec(memory_space=pltpu.VMEM)] * 6,
        out_specs=[pl.BlockSpec(memory_space=pltpu.VMEM)] * 4,
    )(
        flat(queries),
        flat(key_vecs),
        flat(values),
        decay[:, :, None],
        decay[:, None, :],
        rate[:, :, None],
    )
    return (
        shard_a,
        shard_b,
        local_mix.reshape(lead + local_mix.shape[1:]),
        entry_map.reshape(lead + entry_map.shape[1:]),
    )


def group_sum_kernel(group_count, gated_ref, w_ref, out_ref, outgoing, landed, send_sems, recv_sems):
    me = lax.axis_index("hg")
    seq_me = lax.axis_index("seq")
    rows = out_ref.shape[0]
    barrier = pltpu.get_barrier_semaphore()
    for step in range(1, group_count):
        peer = lax.rem(me + step, group_count)
        pl.semaphore_signal(barrier, inc=1, device_id=(seq_me, peer), device_id_type=MESH)
    pl.semaphore_wait(barrier, group_count - 1)

    def term(owner):
        block = gated_ref[pl.ds(pl.multiple_of(owner * rows, 16), rows), :]
        return jnp.dot(block, w_ref[...], preferred_element_type=jnp.float32).astype(out_ref.dtype)

    sends = []
    for step in range(1, group_count):
        peer = lax.rem(me + step, group_count)
        outgoing[step] = term(peer)
        copy = pltpu.make_async_remote_copy(
            src_ref=outgoing.at[step],
            dst_ref=landed.at[me],
            send_sem=send_sems.at[step],
            recv_sem=recv_sems.at[me],
            device_id=(seq_me, peer),
            device_id_type=MESH,
        )
        copy.start()
        sends.append(copy)
    total = term(me).astype(jnp.float32)
    for step in range(1, group_count):
        source = lax.rem(me + group_count - step, group_count)
        pltpu.make_async_remote_copy(
            src_ref=outgoing.at[step],
            dst_ref=landed.at[source],
            send_sem=send_sems.at[step],
            recv_sem=recv_sems.at[source],
            device_id=(seq_me, source),
            device_id_type=MESH,
        ).wait_recv()
        total = total + landed[source].astype(jnp.float32)
    for copy in sends:
        copy.wait_send()
    out_ref[...] = total.astype(out_ref.dtype)


def group_sum(gated, w_out, group_count):
    if group_count == 1:
        return jnp.dot(gated, w_out, preferred_element_type=jnp.float32).astype(jnp.bfloat16)
    rows = gated.shape[0] // group_count
    cols = w_out.shape[1]
    return pl.pallas_call(
        functools.partial(group_sum_kernel, group_count),
        out_shape=jax.ShapeDtypeStruct((rows, cols), jnp.bfloat16),
        in_specs=[pl.BlockSpec(memory_space=pltpu.VMEM)] * 2,
        out_specs=pl.BlockSpec(memory_space=pltpu.VMEM),
        scratch_shapes=[
            pltpu.VMEM((group_count, rows, cols), jnp.bfloat16),
            pltpu.VMEM((group_count, rows, cols), jnp.bfloat16),
            pltpu.SemaphoreType.DMA((group_count,)),
            pltpu.SemaphoreType.DMA((group_count,)),
        ],
        compiler_params=pltpu.CompilerParams(collective_id=0, has_side_effects=True),
    )(gated, w_out)


def on_device(
    hidden_in,
    w_query,
    w_key,
    w_value,
    w_zgate,
    w_decay,
    w_beta,
    conv_query,
    conv_key,
    conv_value,
    a_log,
    dt_bias,
    norm_gain,
    w_out,
):
    tok_rows = hidden_in.shape[0]
    pre_query, pre_key, pre_value = project_inputs(hidden_in, w_query, w_key, w_value)
    kernel_len = conv_query.shape[0]
    rim_rows = tok_rows - kernel_len + 1
    rim_block = jnp.concatenate(
        [pre_query[rim_rows:], pre_key[rim_rows:], pre_value[rim_rows:]], axis=1
    )
    prior = passed_along(rim_block, "seq", 1)
    queries, key_vecs, values, log_decay, write_rate, zgate = mixer_inputs(
        hidden_in,
        pre_query,
        pre_key,
        pre_value,
        prior,
        conv_query,
        conv_key,
        conv_value,
        w_zgate,
        w_decay,
        w_beta,
        a_log,
        dt_bias,
    )
    shard_a, shard_b, local_mix, entry_map = span_terms_kernel(
        to_blocks(queries),
        to_blocks(key_vecs),
        to_blocks(values),
        to_blocks(log_decay[..., None])[..., 0],
        to_blocks(write_rate[..., None])[..., 0],
    )
    head_count = values.shape[1]
    state_in = shard_scan(shard_a, shard_b, lax.axis_size("seq"))
    produced = local_mix + jnp.einsum("jhsd,hde->jhse", entry_map, state_in, precision=highest)
    produced = produced.transpose(0, 2, 1, 3).reshape(tok_rows, head_count, DV)
    gated = gated_output(produced, zgate, norm_gain)
    return group_sum(gated, w_out, lax.axis_size("hg"))


def solution(mesh):
    return jax.shard_map(
        on_device,
        mesh=mesh,
        in_specs=(
            P("seq", None),
            P(None, "hg"),
            P(None, "hg"),
            P(None, "hg"),
            P(None, "hg"),
            P(None, "hg"),
            P(None, "hg"),
            P(None, "hg"),
            P(None, "hg"),
            P(None, "hg"),
            P("hg"),
            P("hg"),
            P(),
            P("hg", None),
        ),
        out_specs=P(("seq", "hg"), None),
        check_vma=False,
    )
```

```python
import functools

import jax
import numpy as np
import jax.numpy as jnp
from jax import lax
from jax.experimental import pallas as pl
from jax.experimental.pallas import tpu as pltpu
from jax.sharding import PartitionSpec as P

MESH = pl.DeviceIdType.MESH

VH = 32
KH = 16
DK = 128
DV = 128
SPAN = 64


highest = lax.Precision.HIGH
norm_eps = 1e-06


def passed_along(block, axis, distance):
    devices = range(lax.axis_size(axis))
    route = [(i - distance, i) for i in devices if i - distance in devices]
    return lax.ppermute(block, axis, route)


def project_inputs(hidden_in, w_query, w_key, w_value):
    pre_query = jnp.dot(hidden_in, w_query, preferred_element_type=jnp.float32).astype(jnp.bfloat16)
    pre_key = jnp.dot(hidden_in, w_key, preferred_element_type=jnp.float32).astype(jnp.bfloat16)
    pre_value = jnp.dot(hidden_in, w_value, preferred_element_type=jnp.float32).astype(jnp.bfloat16)
    return (pre_query, pre_key, pre_value)


def conv_silu(projected, kernel, prior):
    kernel_len = kernel.shape[0]
    tok_rows = projected.shape[0]
    padded = jnp.concatenate([prior.astype(jnp.float32), projected.astype(jnp.float32)], axis=0)
    summed = jnp.zeros((tok_rows, projected.shape[1]), jnp.float32)
    for offset in range(kernel_len):
        summed = summed + kernel[offset].astype(jnp.float32) * padded[offset : offset + tok_rows]
    return jax.nn.silu(summed)


def unit_length(vectors):
    return vectors * lax.rsqrt(jnp.sum(vectors * vectors, axis=-1, keepdims=True) + norm_eps)


def mixer_inputs(
    hidden_in,
    pre_query,
    pre_key,
    pre_value,
    prior,
    conv_query,
    conv_key,
    conv_value,
    w_zgate,
    w_decay,
    w_beta,
    a_log,
    dt_bias,
):
    tok_rows = hidden_in.shape[0]
    query_cols = pre_query.shape[1]
    key_cols = pre_key.shape[1]
    ratio = VH // KH
    queries = unit_length(
        conv_silu(pre_query, conv_query, prior[:, :query_cols]).reshape(tok_rows, -1, DK)
    ) * DK ** (-0.5)
    key_vecs = unit_length(
        conv_silu(pre_key, conv_key, prior[:, query_cols : query_cols + key_cols]).reshape(
            tok_rows, -1, DK
        )
    )
    values = conv_silu(pre_value, conv_value, prior[:, query_cols + key_cols :]).reshape(
        tok_rows, -1, DV
    )
    queries = jnp.repeat(queries, ratio, axis=1)
    key_vecs = jnp.repeat(key_vecs, ratio, axis=1)
    zgate = jnp.dot(hidden_in, w_zgate, preferred_element_type=jnp.float32).astype(jnp.bfloat16)
    rate_logits = jnp.dot(hidden_in, w_decay, preferred_element_type=jnp.float32)
    log_decay = -jnp.exp(a_log) * jax.nn.softplus(rate_logits + dt_bias)
    write_rate = jax.nn.sigmoid(jnp.dot(hidden_in, w_beta, preferred_element_type=jnp.float32))
    return (queries, key_vecs, values, log_decay, write_rate, zgate)


def to_blocks(array_3d):
    tok_rows, head_count = (array_3d.shape[0], array_3d.shape[1])
    return array_3d.reshape(tok_rows // SPAN, SPAN, head_count, -1).transpose(0, 2, 1, 3)


def unit_lower_inverse(lower_part):
    block_len = lower_part.shape[-1]
    row_ids = np.arange(block_len)[:, None]
    col_ids = np.arange(block_len)[None, :]
    first = jnp.asarray((row_ids // 2 == col_ids // 2) & (row_ids != col_ids), jnp.float32)
    inverse = lax.optimization_barrier(
        jnp.asarray(np.eye(block_len), jnp.float32) - lower_part * first
    )
    size = 2
    while size < block_len:
        band = (row_ids // (2 * size) == col_ids // (2 * size)) & (row_ids // size != col_ids // size)
        off_blocks = lower_part * jnp.asarray(band, jnp.float32)
        step = jnp.einsum("...st,...tu->...su", inverse, off_blocks, precision=highest)
        inverse = inverse - jnp.einsum("...st,...tu->...su", step, inverse, precision=highest)
        size *= 2
    return inverse


def span_terms(queries, key_vecs, values, log_decay, write_rate):
    block_len = log_decay.shape[-1]
    cum_decay = jnp.cumsum(log_decay, axis=-1)
    row_ids = lax.broadcasted_iota(jnp.int32, (block_len, block_len), 0)
    col_ids = lax.broadcasted_iota(jnp.int32, (block_len, block_len), 1)
    inclusive = row_ids >= col_ids
    strict = row_ids > col_ids
    gap_mat = cum_decay[..., :, None] - cum_decay[..., None, :]
    falloff = jnp.where(inclusive, jnp.exp(jnp.where(inclusive, gap_mat, 0.0)), 0.0)
    key_dots = jnp.einsum("...sd,...td->...st", key_vecs, key_vecs, precision=highest)
    lower_part = jnp.where(strict, write_rate[..., :, None] * falloff * key_dots, 0.0)
    inverse = unit_lower_inverse(lower_part)
    wy_keys = jnp.einsum(
        "...st,...td->...sd",
        inverse,
        (write_rate * jnp.exp(cum_decay))[..., None] * key_vecs,
        precision=highest,
    )
    wy_values = jnp.einsum(
        "...st,...td->...sd", inverse, write_rate[..., None] * values, precision=highest
    )
    scores = falloff * jnp.einsum("...sd,...td->...st", queries, key_vecs, precision=highest)
    tail_keys = jnp.exp(cum_decay[..., -1:] - cum_decay)[..., None] * key_vecs
    whole_decay = jnp.exp(cum_decay[..., -1])[..., None, None]
    transition = whole_decay * jnp.eye(key_vecs.shape[-1], dtype=jnp.float32) - jnp.einsum(
        "...sd,...se->...de", tail_keys, wy_keys, precision=highest
    )
    written = jnp.einsum("...sd,...se->...de", tail_keys, wy_values, precision=highest)
    carry_map = jnp.exp(cum_decay)[..., None] * queries - jnp.einsum(
        "...st,...td->...sd", scores, wy_keys, precision=highest
    )
    local_out = jnp.einsum("...st,...te->...se", scores, wy_values, precision=highest)
    return (transition, written, carry_map, local_out)


def gated_output(produced, zgate, norm_gain):
    tok_rows = produced.shape[0]
    mean_sq = jnp.mean(produced * produced, axis=-1, keepdims=True)
    gate_vals = jax.nn.silu(zgate.astype(jnp.float32).reshape(produced.shape))
    normed = produced * lax.rsqrt(mean_sq + norm_eps) * norm_gain * gate_vals
    return normed.reshape(tok_rows, -1).astype(jnp.bfloat16)


def advance(state_now, per_span):
    transition, written, carry_map, local_out = per_span
    produced = jnp.einsum("hsd,hde->hse", carry_map, state_now, precision=highest) + local_out
    state_next = jnp.einsum("hde,hef->hdf", transition, state_now, precision=highest) + written
    return (state_next, produced)


def apply_shard(trans_mat, state_now, written):
    return jnp.einsum("hde,hef->hdf", trans_mat, state_now, precision=highest) + written


def shard_scan_kernel(
    shard_count, a_ref, b_ref, out_ref, cur_a, cur_b, out_a, out_b, got_a, got_b, send_sems, recv_sems
):
    me = lax.axis_index("seq")
    hg_me = lax.axis_index("hg")
    head_count = a_ref.shape[0]
    distances = []
    distance = 1
    while distance < shard_count:
        distances.append(distance)
        distance *= 2
    barrier = pltpu.get_barrier_semaphore()
    for distance in distances:
        for target in (lax.rem(me + distance, shard_count), lax.rem(me + shard_count - distance, shard_count)):
            pl.semaphore_signal(barrier, inc=1, device_id=(target, hg_me), device_id_type=MESH)
    pl.semaphore_wait(barrier, 2 * len(distances))
    cur_a[0] = a_ref[...]
    cur_b[0] = b_ref[...]
    out_a[0] = a_ref[...].astype(out_a.dtype)
    out_b[0] = b_ref[...].astype(out_b.dtype)
    sem_index = 0
    for round_index, distance in enumerate(distances):
        target = lax.rem(me + distance, shard_count)
        sends_a = round_index + 1 < len(distances)
        copies = [
            pltpu.make_async_remote_copy(
                src_ref=out_b.at[round_index],
                dst_ref=got_b.at[round_index],
                send_sem=send_sems.at[sem_index],
                recv_sem=recv_sems.at[sem_index],
                device_id=(target, hg_me),
                device_id_type=MESH,
            )
        ]
        if sends_a:
            copies.append(
                pltpu.make_async_remote_copy(
                    src_ref=out_a.at[round_index],
                    dst_ref=got_a.at[round_index],
                    send_sem=send_sems.at[sem_index + 1],
                    recv_sem=recv_sems.at[sem_index + 1],
                    device_id=(target, hg_me),
                    device_id_type=MESH,
                )
            )
        sem_index += len(copies)
        for copy in copies:
            copy.start()
        for copy in copies:
            copy.wait()
        has_prev = me >= distance
        for head in range(head_count):
            own_a = cur_a[round_index, head]
            own_b = cur_b[round_index, head]
            joined_b = (
                jnp.dot(own_a, got_b[round_index, head].astype(jnp.float32), precision=highest,
                        preferred_element_type=jnp.float32)
                + own_b
            )
            next_b = jnp.where(has_prev, joined_b, own_b)
            cur_b[round_index + 1, head] = next_b
            out_b[round_index + 1, head] = next_b.astype(out_b.dtype)
            if sends_a:
                joined_a = jnp.dot(own_a, got_a[round_index, head].astype(jnp.float32),
                                   precision=highest, preferred_element_type=jnp.float32)
                next_a = jnp.where(has_prev, joined_a, own_a)
                cur_a[round_index + 1, head] = next_a
                out_a[round_index + 1, head] = next_a.astype(out_a.dtype)
    last = len(distances)
    shift = pltpu.make_async_remote_copy(
        src_ref=out_b.at[last],
        dst_ref=got_b.at[last],
        send_sem=send_sems.at[sem_index],
        recv_sem=recv_sems.at[sem_index],
        device_id=(lax.rem(me + 1, shard_count), hg_me),
        device_id_type=MESH,
    )
    shift.start()
    shift.wait()
    out_ref[...] = jnp.where(me >= 1, got_b[last].astype(jnp.float32), 0.0)


def shard_scan(shard_a, shard_b, shard_count):
    rounds = max(1, (shard_count - 1).bit_length())
    return pl.pallas_call(
        functools.partial(shard_scan_kernel, shard_count),
        out_shape=jax.ShapeDtypeStruct(shard_b.shape, jnp.float32),
        in_specs=[pl.BlockSpec(memory_space=pltpu.VMEM)] * 2,
        out_specs=pl.BlockSpec(memory_space=pltpu.VMEM),
        scratch_shapes=[
            pltpu.VMEM((rounds + 1,) + shard_a.shape, jnp.float32),
            pltpu.VMEM((rounds + 1,) + shard_b.shape, jnp.float32),
            pltpu.VMEM((rounds + 1,) + shard_a.shape, jnp.bfloat16),
            pltpu.VMEM((rounds + 1,) + shard_b.shape, jnp.bfloat16),
            pltpu.VMEM((rounds + 1,) + shard_a.shape, jnp.bfloat16),
            pltpu.VMEM((rounds + 1,) + shard_b.shape, jnp.bfloat16),
            pltpu.SemaphoreType.DMA((2 * rounds + 1,)),
            pltpu.SemaphoreType.DMA((2 * rounds + 1,)),
        ],
        compiler_params=pltpu.CompilerParams(collective_id=1, has_side_effects=True),
    )(shard_a, shard_b)


def span_kernel(
    head_count, q_ref, k_ref, v_ref, gc_ref, gr_ref, bc_ref, shard_a_ref, shard_b_ref, mix_ref, entry_ref,
    q_pairs, k_pairs, v_pairs, decay_pairs, rate_pairs
):
    width = q_ref.shape[2] // head_count
    for span in range(q_ref.shape[0]):
        for head in range(head_count):
            pair = span * head_count + head
            lanes = slice(head * width, (head + 1) * width)
            q_pairs[pair] = q_ref[span, :, lanes]
            k_pairs[pair] = k_ref[span, :, lanes]
            v_pairs[pair] = v_ref[span, :, lanes]
            decay_pairs[pair] = gc_ref[span, :, head : head + 1]
            rate_pairs[pair] = bc_ref[span, :, head : head + 1]
    queries = q_pairs[...]
    key_vecs = k_pairs[...]
    values = v_pairs[...]
    decay_col = decay_pairs[...]
    decay_row = gr_ref[...]
    rate = rate_pairs[...]
    block_len = queries.shape[1]
    row_ids = lax.broadcasted_iota(jnp.int32, (1, block_len, block_len), 1)
    col_ids = lax.broadcasted_iota(jnp.int32, (1, block_len, block_len), 2)
    inclusive = row_ids >= col_ids
    strict = row_ids > col_ids
    cum_col = jnp.sum(jnp.where(inclusive, decay_row, 0.0), axis=2, keepdims=True)
    cum_row = jnp.sum(jnp.where(row_ids <= col_ids, decay_col, 0.0), axis=1, keepdims=True)
    gap_mat = cum_col - cum_row
    falloff = jnp.where(inclusive, jnp.exp(jnp.where(inclusive, gap_mat, 0.0)), 0.0)
    key_dots = jnp.einsum("bsd,btd->bst", key_vecs, key_vecs, precision=highest,
                          preferred_element_type=jnp.float32)
    lower_part = jnp.where(strict, rate * falloff * key_dots, 0.0)
    inverse = jnp.where((row_ids // 2 == col_ids // 2) & strict, -lower_part, 0.0) + jnp.where(
        row_ids == col_ids, 1.0, 0.0
    )
    size = 2
    while size < block_len:
        band = (row_ids // (2 * size) == col_ids // (2 * size)) & (row_ids // size != col_ids // size)
        off_blocks = jnp.where(band, lower_part, 0.0)
        step = jnp.einsum("bst,btu->bsu", inverse, off_blocks, precision=highest,
                          preferred_element_type=jnp.float32)
        inverse = inverse - jnp.einsum("bst,btu->bsu", step, inverse, precision=highest,
                                       preferred_element_type=jnp.float32)
        size *= 2
    grow = jnp.exp(cum_col)
    wy_keys = jnp.einsum("bst,btd->bsd", inverse, (rate * grow) * key_vecs, precision=highest,
                         preferred_element_type=jnp.float32)
    wy_values = jnp.einsum("bst,btd->bsd", inverse, rate * values, precision=highest,
                           preferred_element_type=jnp.float32)
    scores = falloff * jnp.einsum("bsd,btd->bst", queries, key_vecs, precision=highest,
                                  preferred_element_type=jnp.float32)
    last = cum_row[:, :, block_len - 1 :]
    tail_keys_t = jnp.swapaxes(jnp.exp(last - cum_col) * key_vecs, 1, 2)
    width = key_vecs.shape[2]
    eye_rows = lax.broadcasted_iota(jnp.int32, (1, width, width), 1)
    eye_cols = lax.broadcasted_iota(jnp.int32, (1, width, width), 2)
    transition = jnp.where(eye_rows == eye_cols, jnp.exp(last), 0.0) - jnp.einsum(
        "bds,bse->bde", tail_keys_t, wy_keys, precision=highest, preferred_element_type=jnp.float32
    )
    written = jnp.einsum("bds,bse->bde", tail_keys_t, wy_values, precision=highest,
                         preferred_element_type=jnp.float32)
    carry_map = grow * queries - jnp.einsum("bst,btd->bsd", scores, wy_keys, precision=highest,
                                            preferred_element_type=jnp.float32)
    local_out = jnp.einsum("bst,bte->bse", scores, wy_values, precision=highest,
                           preferred_element_type=jnp.float32)
    for span in range(queries.shape[0] // head_count):
        heads = slice(span * head_count, (span + 1) * head_count)
        if span == 0:
            span_mix = local_out[heads]
            span_entry = carry_map[heads]
        else:
            span_mix = local_out[heads] + jnp.einsum(
                "hsd,hde->hse", carry_map[heads], prefix_b, precision=highest,
                preferred_element_type=jnp.float32)
            span_entry = jnp.einsum("hsd,hde->hse", carry_map[heads], prefix_a, precision=highest,
                                    preferred_element_type=jnp.float32)
        for head in range(head_count):
            lanes = slice(head * width, (head + 1) * width)
            mix_ref[span, :, lanes] = span_mix[head]
            entry_ref[span, :, lanes] = span_entry[head]
        if span == 0:
            prefix_a = transition[heads]
            prefix_b = written[heads]
            continue
        prefix_b = written[heads] + jnp.einsum(
            "hde,hef->hdf", transition[heads], prefix_b, precision=highest,
            preferred_element_type=jnp.float32)
        prefix_a = jnp.einsum("hde,hef->hdf", transition[heads], prefix_a, precision=highest,
                              preferred_element_type=jnp.float32)
    shard_a_ref[...] = prefix_a
    shard_b_ref[...] = prefix_b


def span_terms_kernel(queries, key_vecs, values, log_decay, write_rate):
    tok_rows, head_count, width = queries.shape
    spans = tok_rows // SPAN
    pairs = spans * head_count
    by_span = lambda x: x.reshape(spans, SPAN, -1)
    decay_row = to_blocks(log_decay[..., None])[..., 0].reshape(pairs, 1, SPAN)
    shard_a, shard_b, local_mix, entry_map = pl.pallas_call(
        functools.partial(span_kernel, head_count),
        out_shape=[
            jax.ShapeDtypeStruct((head_count, width, width), jnp.float32),
            jax.ShapeDtypeStruct((head_count, width, values.shape[2]), jnp.float32),
            jax.ShapeDtypeStruct((spans, SPAN, head_count * values.shape[2]), jnp.float32),
            jax.ShapeDtypeStruct((spans, SPAN, head_count * width), jnp.float32),
        ],
        in_specs=[pl.BlockSpec(memory_space=pltpu.VMEM)] * 6,
        out_specs=[pl.BlockSpec(memory_space=pltpu.VMEM)] * 4,
        scratch_shapes=[
            pltpu.VMEM((pairs, SPAN, width), jnp.float32),
            pltpu.VMEM((pairs, SPAN, width), jnp.float32),
            pltpu.VMEM((pairs, SPAN, values.shape[2]), jnp.float32),
            pltpu.VMEM((pairs, SPAN, 1), jnp.float32),
            pltpu.VMEM((pairs, SPAN, 1), jnp.float32),
        ],
    )(
        by_span(queries),
        by_span(key_vecs),
        by_span(values),
        by_span(log_decay),
        decay_row,
        by_span(write_rate),
    )
    return shard_a, shard_b, local_mix, entry_map


def group_sum_kernel(group_count, gated_ref, w_ref, out_ref, outgoing, landed, send_sems, recv_sems):
    me = lax.axis_index("hg")
    seq_me = lax.axis_index("seq")
    rows = out_ref.shape[0]
    barrier = pltpu.get_barrier_semaphore()
    for step in range(1, group_count):
        peer = lax.rem(me + step, group_count)
        pl.semaphore_signal(barrier, inc=1, device_id=(seq_me, peer), device_id_type=MESH)
    pl.semaphore_wait(barrier, group_count - 1)

    def term(owner):
        block = gated_ref[pl.ds(pl.multiple_of(owner * rows, 16), rows), :]
        return jnp.dot(block, w_ref[...], preferred_element_type=jnp.float32).astype(out_ref.dtype)

    sends = []
    for step in range(1, group_count):
        peer = lax.rem(me + step, group_count)
        outgoing[step] = term(peer)
        copy = pltpu.make_async_remote_copy(
            src_ref=outgoing.at[step],
            dst_ref=landed.at[me],
            send_sem=send_sems.at[step],
            recv_sem=recv_sems.at[me],
            device_id=(seq_me, peer),
            device_id_type=MESH,
        )
        copy.start()
        sends.append(copy)
    total = term(me).astype(jnp.float32)
    for step in range(1, group_count):
        source = lax.rem(me + group_count - step, group_count)
        pltpu.make_async_remote_copy(
            src_ref=outgoing.at[step],
            dst_ref=landed.at[source],
            send_sem=send_sems.at[step],
            recv_sem=recv_sems.at[source],
            device_id=(seq_me, source),
            device_id_type=MESH,
        ).wait_recv()
        total = total + landed[source].astype(jnp.float32)
    for copy in sends:
        copy.wait_send()
    out_ref[...] = total.astype(out_ref.dtype)


def group_sum(gated, w_out, group_count):
    if group_count == 1:
        return jnp.dot(gated, w_out, preferred_element_type=jnp.float32).astype(jnp.bfloat16)
    rows = gated.shape[0] // group_count
    cols = w_out.shape[1]
    return pl.pallas_call(
        functools.partial(group_sum_kernel, group_count),
        out_shape=jax.ShapeDtypeStruct((rows, cols), jnp.bfloat16),
        in_specs=[pl.BlockSpec(memory_space=pltpu.VMEM)] * 2,
        out_specs=pl.BlockSpec(memory_space=pltpu.VMEM),
        scratch_shapes=[
            pltpu.VMEM((group_count, rows, cols), jnp.bfloat16),
            pltpu.VMEM((group_count, rows, cols), jnp.bfloat16),
            pltpu.SemaphoreType.DMA((group_count,)),
            pltpu.SemaphoreType.DMA((group_count,)),
        ],
        compiler_params=pltpu.CompilerParams(collective_id=0, has_side_effects=True),
    )(gated, w_out)


def on_device(
    hidden_in,
    w_query,
    w_key,
    w_value,
    w_zgate,
    w_decay,
    w_beta,
    conv_query,
    conv_key,
    conv_value,
    a_log,
    dt_bias,
    norm_gain,
    w_out,
):
    tok_rows = hidden_in.shape[0]
    pre_query, pre_key, pre_value = project_inputs(hidden_in, w_query, w_key, w_value)
    kernel_len = conv_query.shape[0]
    rim_rows = tok_rows - kernel_len + 1
    rim_block = jnp.concatenate(
        [pre_query[rim_rows:], pre_key[rim_rows:], pre_value[rim_rows:]], axis=1
    )
    prior = passed_along(rim_block, "seq", 1)
    queries, key_vecs, values, log_decay, write_rate, zgate = mixer_inputs(
        hidden_in,
        pre_query,
        pre_key,
        pre_value,
        prior,
        conv_query,
        conv_key,
        conv_value,
        w_zgate,
        w_decay,
        w_beta,
        a_log,
        dt_bias,
    )
    shard_a, shard_b, local_mix, entry_map = span_terms_kernel(
        queries, key_vecs, values, log_decay, write_rate
    )
    head_count = values.shape[1]
    state_in = shard_scan(shard_a, shard_b, lax.axis_size("seq"))
    produced = local_mix.reshape(tok_rows, head_count, DV) + jnp.einsum(
        "thd,hde->the", entry_map.reshape(tok_rows, head_count, DK), state_in, precision=highest
    )
    gated = gated_output(produced, zgate, norm_gain)
    return group_sum(gated, w_out, lax.axis_size("hg"))


def solution(mesh):
    return jax.shard_map(
        on_device,
        mesh=mesh,
        in_specs=(
            P("seq", None),
            P(None, "hg"),
            P(None, "hg"),
            P(None, "hg"),
            P(None, "hg"),
            P(None, "hg"),
            P(None, "hg"),
            P(None, "hg"),
            P(None, "hg"),
            P(None, "hg"),
            P("hg"),
            P("hg"),
            P(),
            P("hg", None),
        ),
        out_specs=P(("seq", "hg"), None),
        check_vma=False,
    )
```

```python
import functools

import jax
import numpy as np
import jax.numpy as jnp
from jax import lax
from jax.experimental import pallas as pl
from jax.experimental.pallas import tpu as pltpu
from jax.sharding import PartitionSpec as P

MESH = pl.DeviceIdType.MESH

VH = 32
KH = 16
DK = 128
DV = 128
SPAN = 64


highest = lax.Precision.HIGH
norm_eps = 1e-06


def passed_along(block, axis, distance):
    devices = range(lax.axis_size(axis))
    route = [(i - distance, i) for i in devices if i - distance in devices]
    return lax.ppermute(block, axis, route)


def project_inputs(hidden_in, w_query, w_key, w_value):
    pre_query = jnp.dot(hidden_in, w_query, preferred_element_type=jnp.float32).astype(jnp.bfloat16)
    pre_key = jnp.dot(hidden_in, w_key, preferred_element_type=jnp.float32).astype(jnp.bfloat16)
    pre_value = jnp.dot(hidden_in, w_value, preferred_element_type=jnp.float32).astype(jnp.bfloat16)
    return (pre_query, pre_key, pre_value)


def conv_silu(projected, kernel, prior):
    kernel_len = kernel.shape[0]
    tok_rows = projected.shape[0]
    padded = jnp.concatenate([prior.astype(jnp.float32), projected.astype(jnp.float32)], axis=0)
    summed = jnp.zeros((tok_rows, projected.shape[1]), jnp.float32)
    for offset in range(kernel_len):
        summed = summed + kernel[offset].astype(jnp.float32) * padded[offset : offset + tok_rows]
    return jax.nn.silu(summed)


def unit_length(vectors):
    return vectors * lax.rsqrt(jnp.sum(vectors * vectors, axis=-1, keepdims=True) + norm_eps)


def mixer_inputs(
    hidden_in,
    pre_query,
    pre_key,
    pre_value,
    prior,
    conv_query,
    conv_key,
    conv_value,
    w_zgate,
    w_decay,
    w_beta,
    a_log,
    dt_bias,
):
    tok_rows = hidden_in.shape[0]
    query_cols = pre_query.shape[1]
    key_cols = pre_key.shape[1]
    ratio = VH // KH
    queries = unit_length(
        conv_silu(pre_query, conv_query, prior[:, :query_cols]).reshape(tok_rows, -1, DK)
    ) * DK ** (-0.5)
    key_vecs = unit_length(
        conv_silu(pre_key, conv_key, prior[:, query_cols : query_cols + key_cols]).reshape(
            tok_rows, -1, DK
        )
    )
    values = conv_silu(pre_value, conv_value, prior[:, query_cols + key_cols :]).reshape(
        tok_rows, -1, DV
    )
    queries = jnp.repeat(queries, ratio, axis=1)
    key_vecs = jnp.repeat(key_vecs, ratio, axis=1)
    zgate = jnp.dot(hidden_in, w_zgate, preferred_element_type=jnp.float32).astype(jnp.bfloat16)
    rate_logits = jnp.dot(hidden_in, w_decay, preferred_element_type=jnp.float32)
    log_decay = -jnp.exp(a_log) * jax.nn.softplus(rate_logits + dt_bias)
    write_rate = jax.nn.sigmoid(jnp.dot(hidden_in, w_beta, preferred_element_type=jnp.float32))
    return (queries, key_vecs, values, log_decay, write_rate, zgate)


def to_blocks(array_3d):
    tok_rows, head_count = (array_3d.shape[0], array_3d.shape[1])
    return array_3d.reshape(tok_rows // SPAN, SPAN, head_count, -1).transpose(0, 2, 1, 3)


def unit_lower_inverse(lower_part):
    block_len = lower_part.shape[-1]
    row_ids = np.arange(block_len)[:, None]
    col_ids = np.arange(block_len)[None, :]
    first = jnp.asarray((row_ids // 2 == col_ids // 2) & (row_ids != col_ids), jnp.float32)
    inverse = lax.optimization_barrier(
        jnp.asarray(np.eye(block_len), jnp.float32) - lower_part * first
    )
    size = 2
    while size < block_len:
        band = (row_ids // (2 * size) == col_ids // (2 * size)) & (row_ids // size != col_ids // size)
        off_blocks = lower_part * jnp.asarray(band, jnp.float32)
        step = jnp.einsum("...st,...tu->...su", inverse, off_blocks, precision=highest)
        inverse = inverse - jnp.einsum("...st,...tu->...su", step, inverse, precision=highest)
        size *= 2
    return inverse


def span_terms(queries, key_vecs, values, log_decay, write_rate):
    block_len = log_decay.shape[-1]
    cum_decay = jnp.cumsum(log_decay, axis=-1)
    row_ids = lax.broadcasted_iota(jnp.int32, (block_len, block_len), 0)
    col_ids = lax.broadcasted_iota(jnp.int32, (block_len, block_len), 1)
    inclusive = row_ids >= col_ids
    strict = row_ids > col_ids
    gap_mat = cum_decay[..., :, None] - cum_decay[..., None, :]
    falloff = jnp.where(inclusive, jnp.exp(jnp.where(inclusive, gap_mat, 0.0)), 0.0)
    key_dots = jnp.einsum("...sd,...td->...st", key_vecs, key_vecs, precision=highest)
    lower_part = jnp.where(strict, write_rate[..., :, None] * falloff * key_dots, 0.0)
    inverse = unit_lower_inverse(lower_part)
    wy_keys = jnp.einsum(
        "...st,...td->...sd",
        inverse,
        (write_rate * jnp.exp(cum_decay))[..., None] * key_vecs,
        precision=highest,
    )
    wy_values = jnp.einsum(
        "...st,...td->...sd", inverse, write_rate[..., None] * values, precision=highest
    )
    scores = falloff * jnp.einsum("...sd,...td->...st", queries, key_vecs, precision=highest)
    tail_keys = jnp.exp(cum_decay[..., -1:] - cum_decay)[..., None] * key_vecs
    whole_decay = jnp.exp(cum_decay[..., -1])[..., None, None]
    transition = whole_decay * jnp.eye(key_vecs.shape[-1], dtype=jnp.float32) - jnp.einsum(
        "...sd,...se->...de", tail_keys, wy_keys, precision=highest
    )
    written = jnp.einsum("...sd,...se->...de", tail_keys, wy_values, precision=highest)
    carry_map = jnp.exp(cum_decay)[..., None] * queries - jnp.einsum(
        "...st,...td->...sd", scores, wy_keys, precision=highest
    )
    local_out = jnp.einsum("...st,...te->...se", scores, wy_values, precision=highest)
    return (transition, written, carry_map, local_out)


def gated_output(produced, zgate, norm_gain):
    tok_rows = produced.shape[0]
    mean_sq = jnp.mean(produced * produced, axis=-1, keepdims=True)
    gate_vals = jax.nn.silu(zgate.astype(jnp.float32).reshape(produced.shape))
    normed = produced * lax.rsqrt(mean_sq + norm_eps) * norm_gain * gate_vals
    return normed.reshape(tok_rows, -1).astype(jnp.bfloat16)


def advance(state_now, per_span):
    transition, written, carry_map, local_out = per_span
    produced = jnp.einsum("hsd,hde->hse", carry_map, state_now, precision=highest) + local_out
    state_next = jnp.einsum("hde,hef->hdf", transition, state_now, precision=highest) + written
    return (state_next, produced)


def apply_shard(trans_mat, state_now, written):
    return jnp.einsum("hde,hef->hdf", trans_mat, state_now, precision=highest) + written


def shard_scan_kernel(
    shard_count, a_ref, b_ref, out_ref, cur_a, cur_b, out_ab, got_ab, send_sems, recv_sems
):
    me = lax.axis_index("seq")
    hg_me = lax.axis_index("hg")
    head_count = a_ref.shape[0]
    distances = []
    distance = 1
    while distance < shard_count:
        distances.append(distance)
        distance *= 2
    barrier = pltpu.get_barrier_semaphore()
    for distance in distances:
        for target in (lax.rem(me + distance, shard_count), lax.rem(me + shard_count - distance, shard_count)):
            pl.semaphore_signal(barrier, inc=1, device_id=(target, hg_me), device_id_type=MESH)
    pl.semaphore_wait(barrier, 2 * len(distances))
    cur_a[0] = a_ref[...]
    cur_b[0] = b_ref[...]
    out_ab[0, 0] = a_ref[...].astype(out_ab.dtype)
    out_ab[0, 1] = b_ref[...].astype(out_ab.dtype)
    sem_index = 0
    for round_index, distance in enumerate(distances):
        target = lax.rem(me + distance, shard_count)
        sends_a = round_index + 1 < len(distances)
        whole = slice(None) if sends_a else 1
        copies = [
            pltpu.make_async_remote_copy(
                src_ref=out_ab.at[round_index, whole],
                dst_ref=got_ab.at[round_index, whole],
                send_sem=send_sems.at[sem_index],
                recv_sem=recv_sems.at[sem_index],
                device_id=(target, hg_me),
                device_id_type=MESH,
            )
        ]
        sem_index += len(copies)
        for copy in copies:
            copy.start()
        for copy in copies:
            copy.wait()
        has_prev = me >= distance
        for head in range(head_count):
            own_a = cur_a[round_index, head]
            own_b = cur_b[round_index, head]
            joined_b = (
                jnp.dot(own_a, got_ab[round_index, 1, head].astype(jnp.float32), precision=highest,
                        preferred_element_type=jnp.float32)
                + own_b
            )
            next_b = jnp.where(has_prev, joined_b, own_b)
            cur_b[round_index + 1, head] = next_b
            out_ab[round_index + 1, 1, head] = next_b.astype(out_ab.dtype)
            if sends_a:
                joined_a = jnp.dot(own_a, got_ab[round_index, 0, head].astype(jnp.float32),
                                   precision=highest, preferred_element_type=jnp.float32)
                next_a = jnp.where(has_prev, joined_a, own_a)
                cur_a[round_index + 1, head] = next_a
                out_ab[round_index + 1, 0, head] = next_a.astype(out_ab.dtype)
    last = len(distances)
    shift = pltpu.make_async_remote_copy(
        src_ref=out_ab.at[last, 1],
        dst_ref=got_ab.at[last, 1],
        send_sem=send_sems.at[sem_index],
        recv_sem=recv_sems.at[sem_index],
        device_id=(lax.rem(me + 1, shard_count), hg_me),
        device_id_type=MESH,
    )
    shift.start()
    shift.wait()
    out_ref[...] = jnp.where(me >= 1, got_ab[last, 1].astype(jnp.float32), 0.0)


def shard_scan(shard_a, shard_b, shard_count):
    rounds = max(1, (shard_count - 1).bit_length())
    return pl.pallas_call(
        functools.partial(shard_scan_kernel, shard_count),
        out_shape=jax.ShapeDtypeStruct(shard_b.shape, jnp.float32),
        in_specs=[pl.BlockSpec(memory_space=pltpu.VMEM)] * 2,
        out_specs=pl.BlockSpec(memory_space=pltpu.VMEM),
        scratch_shapes=[
            pltpu.VMEM((rounds + 1,) + shard_a.shape, jnp.float32),
            pltpu.VMEM((rounds + 1,) + shard_b.shape, jnp.float32),
            pltpu.VMEM((rounds + 1, 2) + shard_a.shape, jnp.bfloat16),
            pltpu.VMEM((rounds + 1, 2) + shard_a.shape, jnp.bfloat16),
            pltpu.SemaphoreType.DMA((2 * rounds + 1,)),
            pltpu.SemaphoreType.DMA((2 * rounds + 1,)),
        ],
        compiler_params=pltpu.CompilerParams(collective_id=1, has_side_effects=True),
    )(shard_a, shard_b)


def span_kernel(
    head_count, q_ref, k_ref, v_ref, gc_ref, gr_ref, bc_ref, shard_a_ref, shard_b_ref, mix_ref, entry_ref
):
    queries = q_ref[...]
    key_vecs = k_ref[...]
    values = v_ref[...]
    decay_col = gc_ref[...]
    decay_row = gr_ref[...]
    rate = bc_ref[...]
    block_len = queries.shape[1]
    row_ids = lax.broadcasted_iota(jnp.int32, (1, block_len, block_len), 1)
    col_ids = lax.broadcasted_iota(jnp.int32, (1, block_len, block_len), 2)
    inclusive = row_ids >= col_ids
    strict = row_ids > col_ids
    cum_col = jnp.sum(jnp.where(inclusive, decay_row, 0.0), axis=2, keepdims=True)
    cum_row = jnp.sum(jnp.where(row_ids <= col_ids, decay_col, 0.0), axis=1, keepdims=True)
    gap_mat = cum_col - cum_row
    falloff = jnp.where(inclusive, jnp.exp(jnp.where(inclusive, gap_mat, 0.0)), 0.0)
    key_dots = jnp.einsum("bsd,btd->bst", key_vecs, key_vecs, precision=highest,
                          preferred_element_type=jnp.float32)
    lower_part = jnp.where(strict, rate * falloff * key_dots, 0.0)
    inverse = jnp.where((row_ids // 2 == col_ids // 2) & strict, -lower_part, 0.0) + jnp.where(
        row_ids == col_ids, 1.0, 0.0
    )
    size = 2
    while size < block_len:
        band = (row_ids // (2 * size) == col_ids // (2 * size)) & (row_ids // size != col_ids // size)
        off_blocks = jnp.where(band, lower_part, 0.0)
        step = jnp.einsum("bst,btu->bsu", inverse, off_blocks, precision=highest,
                          preferred_element_type=jnp.float32)
        inverse = inverse - jnp.einsum("bst,btu->bsu", step, inverse, precision=highest,
                                       preferred_element_type=jnp.float32)
        size *= 2
    grow = jnp.exp(cum_col)
    wy_keys = jnp.einsum("bst,btd->bsd", inverse, (rate * grow) * key_vecs, precision=highest,
                         preferred_element_type=jnp.float32)
    wy_values = jnp.einsum("bst,btd->bsd", inverse, rate * values, precision=highest,
                           preferred_element_type=jnp.float32)
    scores = falloff * jnp.einsum("bsd,btd->bst", queries, key_vecs, precision=highest,
                                  preferred_element_type=jnp.float32)
    last = cum_row[:, :, block_len - 1 :]
    tail_keys_t = jnp.swapaxes(jnp.exp(last - cum_col) * key_vecs, 1, 2)
    width = key_vecs.shape[2]
    eye_rows = lax.broadcasted_iota(jnp.int32, (1, width, width), 1)
    eye_cols = lax.broadcasted_iota(jnp.int32, (1, width, width), 2)
    transition = jnp.where(eye_rows == eye_cols, jnp.exp(last), 0.0) - jnp.einsum(
        "bds,bse->bde", tail_keys_t, wy_keys, precision=highest, preferred_element_type=jnp.float32
    )
    written = jnp.einsum("bds,bse->bde", tail_keys_t, wy_values, precision=highest,
                         preferred_element_type=jnp.float32)
    carry_map = grow * queries - jnp.einsum("bst,btd->bsd", scores, wy_keys, precision=highest,
                                            preferred_element_type=jnp.float32)
    local_out = jnp.einsum("bst,bte->bse", scores, wy_values, precision=highest,
                           preferred_element_type=jnp.float32)
    for span in range(queries.shape[0] // head_count):
        heads = slice(span * head_count, (span + 1) * head_count)
        if span == 0:
            mix_ref[heads] = local_out[heads]
            entry_ref[heads] = carry_map[heads]
            prefix_a = transition[heads]
            prefix_b = written[heads]
            continue
        mix_ref[heads] = local_out[heads] + jnp.einsum(
            "hsd,hde->hse", carry_map[heads], prefix_b, precision=highest,
            preferred_element_type=jnp.float32)
        entry_ref[heads] = jnp.einsum("hsd,hde->hse", carry_map[heads], prefix_a, precision=highest,
                                      preferred_element_type=jnp.float32)
        prefix_b = written[heads] + jnp.einsum(
            "hde,hef->hdf", transition[heads], prefix_b, precision=highest,
            preferred_element_type=jnp.float32)
        prefix_a = jnp.einsum("hde,hef->hdf", transition[heads], prefix_a, precision=highest,
                              preferred_element_type=jnp.float32)
    shard_a_ref[...] = prefix_a
    shard_b_ref[...] = prefix_b


def span_terms_kernel(queries, key_vecs, values, log_decay, write_rate):
    lead = queries.shape[:2]
    block_len, width = queries.shape[2], queries.shape[3]
    flat = lambda x: x.reshape((-1,) + x.shape[2:])
    pairs = lead[0] * lead[1]
    decay = log_decay.reshape(pairs, block_len)
    rate = write_rate.reshape(pairs, block_len)
    shard_a, shard_b, local_mix, entry_map = pl.pallas_call(
        functools.partial(span_kernel, lead[1]),
        out_shape=[
            jax.ShapeDtypeStruct((lead[1], width, width), jnp.float32),
            jax.ShapeDtypeStruct((lead[1], width, values.shape[3]), jnp.float32),
            jax.ShapeDtypeStruct((pairs, block_len, values.shape[3]), jnp.float32),
            jax.ShapeDtypeStruct((pairs, block_len, width), jnp.float32),
        ],
        in_specs=[pl.BlockSpec(memory_space=pltpu.VMEM)] * 6,
        out_specs=[pl.BlockSpec(memory_space=pltpu.VMEM)] * 4,
    )(
        flat(queries),
        flat(key_vecs),
        flat(values),
        decay[:, :, None],
        decay[:, None, :],
        rate[:, :, None],
    )
    return (
        shard_a,
        shard_b,
        local_mix.reshape(lead + local_mix.shape[1:]),
        entry_map.reshape(lead + entry_map.shape[1:]),
    )


def group_sum_kernel(group_count, part_ref, out_ref, landed, send_sems, recv_sems, own_sem):
    me = lax.axis_index("hg")
    seq_me = lax.axis_index("seq")
    rows = out_ref.shape[0]
    barrier = pltpu.get_barrier_semaphore()
    for step in range(1, group_count):
        peer = lax.rem(me + step, group_count)
        pl.semaphore_signal(barrier, inc=1, device_id=(seq_me, peer), device_id_type=MESH)
    pl.semaphore_wait(barrier, group_count - 1)
    sends = []
    for step in range(1, group_count):
        peer = lax.rem(me + step, group_count)
        copy = pltpu.make_async_remote_copy(
            src_ref=part_ref.at[pl.ds(pl.multiple_of(peer * rows, 8), rows)],
            dst_ref=landed.at[me],
            send_sem=send_sems.at[step],
            recv_sem=recv_sems.at[me],
            device_id=(seq_me, peer),
            device_id_type=MESH,
        )
        copy.start()
        sends.append(copy)
    own = pltpu.make_async_copy(
        part_ref.at[pl.ds(pl.multiple_of(me * rows, 8), rows)], landed.at[me], own_sem
    )
    own.start()
    own.wait()
    for step in range(1, group_count):
        source = lax.rem(me + group_count - step, group_count)
        pltpu.make_async_remote_copy(
            src_ref=part_ref.at[pl.ds(0, rows)],
            dst_ref=landed.at[source],
            send_sem=send_sems.at[step],
            recv_sem=recv_sems.at[source],
            device_id=(seq_me, source),
            device_id_type=MESH,
        ).wait_recv()
    for copy in sends:
        copy.wait_send()
    total = landed[0].astype(jnp.float32)
    for slot in range(1, group_count):
        total = total + landed[slot].astype(jnp.float32)
    out_ref[...] = total.astype(out_ref.dtype)


def group_sum(part, group_count):
    if group_count == 1:
        return part
    rows = part.shape[0] // group_count
    cols = part.shape[1]
    return pl.pallas_call(
        functools.partial(group_sum_kernel, group_count),
        out_shape=jax.ShapeDtypeStruct((rows, cols), part.dtype),
        in_specs=[pl.BlockSpec(memory_space=pltpu.VMEM)],
        out_specs=pl.BlockSpec(memory_space=pltpu.VMEM),
        scratch_shapes=[
            pltpu.VMEM((group_count, rows, cols), part.dtype),
            pltpu.SemaphoreType.DMA((group_count,)),
            pltpu.SemaphoreType.DMA((group_count,)),
            pltpu.SemaphoreType.DMA,
        ],
        compiler_params=pltpu.CompilerParams(collective_id=0, has_side_effects=True),
    )(part)


def on_device(
    hidden_in,
    w_query,
    w_key,
    w_value,
    w_zgate,
    w_decay,
    w_beta,
    conv_query,
    conv_key,
    conv_value,
    a_log,
    dt_bias,
    norm_gain,
    w_out,
):
    tok_rows = hidden_in.shape[0]
    pre_query, pre_key, pre_value = project_inputs(hidden_in, w_query, w_key, w_value)
    kernel_len = conv_query.shape[0]
    rim_rows = tok_rows - kernel_len + 1
    rim_block = jnp.concatenate(
        [pre_query[rim_rows:], pre_key[rim_rows:], pre_value[rim_rows:]], axis=1
    )
    prior = passed_along(rim_block, "seq", 1)
    queries, key_vecs, values, log_decay, write_rate, zgate = mixer_inputs(
        hidden_in,
        pre_query,
        pre_key,
        pre_value,
        prior,
        conv_query,
        conv_key,
        conv_value,
        w_zgate,
        w_decay,
        w_beta,
        a_log,
        dt_bias,
    )
    shard_a, shard_b, local_mix, entry_map = span_terms_kernel(
        to_blocks(queries),
        to_blocks(key_vecs),
        to_blocks(values),
        to_blocks(log_decay[..., None])[..., 0],
        to_blocks(write_rate[..., None])[..., 0],
    )
    head_count = values.shape[1]
    state_in = shard_scan(shard_a, shard_b, lax.axis_size("seq"))
    produced = local_mix + jnp.einsum("jhsd,hde->jhse", entry_map, state_in, precision=highest)
    produced = produced.transpose(0, 2, 1, 3).reshape(tok_rows, head_count, DV)
    gated = gated_output(produced, zgate, norm_gain)
    part = jnp.dot(gated, w_out, preferred_element_type=jnp.float32).astype(jnp.bfloat16)
    return group_sum(part, lax.axis_size("hg"))


def solution(mesh):
    return jax.shard_map(
        on_device,
        mesh=mesh,
        in_specs=(
            P("seq", None),
            P(None, "hg"),
            P(None, "hg"),
            P(None, "hg"),
            P(None, "hg"),
            P(None, "hg"),
            P(None, "hg"),
            P(None, "hg"),
            P(None, "hg"),
            P(None, "hg"),
            P("hg"),
            P("hg"),
            P(),
            P("hg", None),
        ),
        out_specs=P(("seq", "hg"), None),
        check_vma=False,
    )
```

```python
import functools

import jax
import numpy as np
import jax.numpy as jnp
from jax import lax
from jax.experimental import pallas as pl
from jax.experimental.pallas import tpu as pltpu
from jax.sharding import PartitionSpec as P

MESH = pl.DeviceIdType.MESH

VH = 32
KH = 16
DK = 128
DV = 128
SPAN = 64


highest = lax.Precision.HIGH
norm_eps = 1e-06


def passed_along(block, axis, distance):
    devices = range(lax.axis_size(axis))
    route = [(i - distance, i) for i in devices if i - distance in devices]
    return lax.ppermute(block, axis, route)


def project_inputs(hidden_in, w_query, w_key, w_value):
    pre_query = jnp.dot(hidden_in, w_query, preferred_element_type=jnp.float32).astype(jnp.bfloat16)
    pre_key = jnp.dot(hidden_in, w_key, preferred_element_type=jnp.float32).astype(jnp.bfloat16)
    pre_value = jnp.dot(hidden_in, w_value, preferred_element_type=jnp.float32).astype(jnp.bfloat16)
    return (pre_query, pre_key, pre_value)


def conv_silu(projected, kernel, prior):
    kernel_len = kernel.shape[0]
    tok_rows = projected.shape[0]
    padded = jnp.concatenate([prior.astype(jnp.float32), projected.astype(jnp.float32)], axis=0)
    summed = jnp.zeros((tok_rows, projected.shape[1]), jnp.float32)
    for offset in range(kernel_len):
        summed = summed + kernel[offset].astype(jnp.float32) * padded[offset : offset + tok_rows]
    return jax.nn.silu(summed)


def unit_length(vectors):
    return vectors * lax.rsqrt(jnp.sum(vectors * vectors, axis=-1, keepdims=True) + norm_eps)


def mixer_inputs(
    hidden_in,
    pre_query,
    pre_key,
    pre_value,
    prior,
    conv_query,
    conv_key,
    conv_value,
    w_zgate,
    w_decay,
    w_beta,
    a_log,
    dt_bias,
):
    tok_rows = hidden_in.shape[0]
    query_cols = pre_query.shape[1]
    key_cols = pre_key.shape[1]
    ratio = VH // KH
    queries = unit_length(
        conv_silu(pre_query, conv_query, prior[:, :query_cols]).reshape(tok_rows, -1, DK)
    ) * DK ** (-0.5)
    key_vecs = unit_length(
        conv_silu(pre_key, conv_key, prior[:, query_cols : query_cols + key_cols]).reshape(
            tok_rows, -1, DK
        )
    )
    values = conv_silu(pre_value, conv_value, prior[:, query_cols + key_cols :]).reshape(
        tok_rows, -1, DV
    )
    queries = jnp.repeat(queries, ratio, axis=1)
    key_vecs = jnp.repeat(key_vecs, ratio, axis=1)
    zgate = jnp.dot(hidden_in, w_zgate, preferred_element_type=jnp.float32).astype(jnp.bfloat16)
    rate_logits = jnp.dot(hidden_in, w_decay, preferred_element_type=jnp.float32)
    log_decay = -jnp.exp(a_log) * jax.nn.softplus(rate_logits + dt_bias)
    write_rate = jax.nn.sigmoid(jnp.dot(hidden_in, w_beta, preferred_element_type=jnp.float32))
    return (queries, key_vecs, values, log_decay, write_rate, zgate)


def to_blocks(array_3d):
    tok_rows, head_count = (array_3d.shape[0], array_3d.shape[1])
    return array_3d.reshape(tok_rows // SPAN, SPAN, head_count, -1).transpose(0, 2, 1, 3)


def unit_lower_inverse(lower_part):
    block_len = lower_part.shape[-1]
    row_ids = np.arange(block_len)[:, None]
    col_ids = np.arange(block_len)[None, :]
    first = jnp.asarray((row_ids // 2 == col_ids // 2) & (row_ids != col_ids), jnp.float32)
    inverse = lax.optimization_barrier(
        jnp.asarray(np.eye(block_len), jnp.float32) - lower_part * first
    )
    size = 2
    while size < block_len:
        band = (row_ids // (2 * size) == col_ids // (2 * size)) & (row_ids // size != col_ids // size)
        off_blocks = lower_part * jnp.asarray(band, jnp.float32)
        step = jnp.einsum("...st,...tu->...su", inverse, off_blocks, precision=highest)
        inverse = inverse - jnp.einsum("...st,...tu->...su", step, inverse, precision=highest)
        size *= 2
    return inverse


def span_terms(queries, key_vecs, values, log_decay, write_rate):
    block_len = log_decay.shape[-1]
    cum_decay = jnp.cumsum(log_decay, axis=-1)
    row_ids = lax.broadcasted_iota(jnp.int32, (block_len, block_len), 0)
    col_ids = lax.broadcasted_iota(jnp.int32, (block_len, block_len), 1)
    inclusive = row_ids >= col_ids
    strict = row_ids > col_ids
    gap_mat = cum_decay[..., :, None] - cum_decay[..., None, :]
    falloff = jnp.where(inclusive, jnp.exp(jnp.where(inclusive, gap_mat, 0.0)), 0.0)
    key_dots = jnp.einsum("...sd,...td->...st", key_vecs, key_vecs, precision=highest)
    lower_part = jnp.where(strict, write_rate[..., :, None] * falloff * key_dots, 0.0)
    inverse = unit_lower_inverse(lower_part)
    wy_keys = jnp.einsum(
        "...st,...td->...sd",
        inverse,
        (write_rate * jnp.exp(cum_decay))[..., None] * key_vecs,
        precision=highest,
    )
    wy_values = jnp.einsum(
        "...st,...td->...sd", inverse, write_rate[..., None] * values, precision=highest
    )
    scores = falloff * jnp.einsum("...sd,...td->...st", queries, key_vecs, precision=highest)
    tail_keys = jnp.exp(cum_decay[..., -1:] - cum_decay)[..., None] * key_vecs
    whole_decay = jnp.exp(cum_decay[..., -1])[..., None, None]
    transition = whole_decay * jnp.eye(key_vecs.shape[-1], dtype=jnp.float32) - jnp.einsum(
        "...sd,...se->...de", tail_keys, wy_keys, precision=highest
    )
    written = jnp.einsum("...sd,...se->...de", tail_keys, wy_values, precision=highest)
    carry_map = jnp.exp(cum_decay)[..., None] * queries - jnp.einsum(
        "...st,...td->...sd", scores, wy_keys, precision=highest
    )
    local_out = jnp.einsum("...st,...te->...se", scores, wy_values, precision=highest)
    return (transition, written, carry_map, local_out)


def gated_output(produced, zgate, norm_gain):
    tok_rows = produced.shape[0]
    mean_sq = jnp.mean(produced * produced, axis=-1, keepdims=True)
    gate_vals = jax.nn.silu(zgate.astype(jnp.float32).reshape(produced.shape))
    normed = produced * lax.rsqrt(mean_sq + norm_eps) * norm_gain * gate_vals
    return normed.reshape(tok_rows, -1).astype(jnp.bfloat16)


def advance(state_now, per_span):
    transition, written, carry_map, local_out = per_span
    produced = jnp.einsum("hsd,hde->hse", carry_map, state_now, precision=highest) + local_out
    state_next = jnp.einsum("hde,hef->hdf", transition, state_now, precision=highest) + written
    return (state_next, produced)


def apply_shard(trans_mat, state_now, written):
    return jnp.einsum("hde,hef->hdf", trans_mat, state_now, precision=highest) + written


def shard_scan_kernel(
    shard_count, a_ref, b_ref, out_ref, cur_a, cur_b, out_a, out_b, got_a, got_b, send_sems, recv_sems
):
    me = lax.axis_index("seq")
    hg_me = lax.axis_index("hg")
    head_count = a_ref.shape[0]
    distances = []
    distance = 1
    while distance < shard_count:
        distances.append(distance)
        distance *= 2
    barrier = pltpu.get_barrier_semaphore()
    for distance in distances:
        for target in (lax.rem(me + distance, shard_count), lax.rem(me + shard_count - distance, shard_count)):
            pl.semaphore_signal(barrier, inc=1, device_id=(target, hg_me), device_id_type=MESH)
    pl.semaphore_wait(barrier, 2 * len(distances))
    cur_a[0] = a_ref[...]
    cur_b[0] = b_ref[...]
    out_a[0] = a_ref[...].astype(out_a.dtype)
    out_b[0] = b_ref[...].astype(out_b.dtype)
    sem_index = 0
    for round_index, distance in enumerate(distances):
        target = lax.rem(me + distance, shard_count)
        sends_a = round_index + 1 < len(distances)
        copies = [
            pltpu.make_async_remote_copy(
                src_ref=out_b.at[round_index],
                dst_ref=got_b.at[round_index],
                send_sem=send_sems.at[sem_index],
                recv_sem=recv_sems.at[sem_index],
                device_id=(target, hg_me),
                device_id_type=MESH,
            )
        ]
        if sends_a:
            copies.append(
                pltpu.make_async_remote_copy(
                    src_ref=out_a.at[round_index],
                    dst_ref=got_a.at[round_index],
                    send_sem=send_sems.at[sem_index + 1],
                    recv_sem=recv_sems.at[sem_index + 1],
                    device_id=(target, hg_me),
                    device_id_type=MESH,
                )
            )
        sem_index += len(copies)
        for copy in copies:
            copy.start()
        for copy in copies:
            copy.wait()
        has_prev = me >= distance
        for head in range(head_count):
            own_a = cur_a[round_index, head]
            own_b = cur_b[round_index, head]
            joined_b = (
                jnp.dot(own_a, got_b[round_index, head].astype(jnp.float32), precision=highest,
                        preferred_element_type=jnp.float32)
                + own_b
            )
            next_b = jnp.where(has_prev, joined_b, own_b)
            cur_b[round_index + 1, head] = next_b
            out_b[round_index + 1, head] = next_b.astype(out_b.dtype)
            if sends_a:
                joined_a = jnp.dot(own_a, got_a[round_index, head].astype(jnp.float32),
                                   precision=highest, preferred_element_type=jnp.float32)
                next_a = jnp.where(has_prev, joined_a, own_a)
                cur_a[round_index + 1, head] = next_a
                out_a[round_index + 1, head] = next_a.astype(out_a.dtype)
    last = len(distances)
    shift = pltpu.make_async_remote_copy(
        src_ref=out_b.at[last],
        dst_ref=got_b.at[last],
        send_sem=send_sems.at[sem_index],
        recv_sem=recv_sems.at[sem_index],
        device_id=(lax.rem(me + 1, shard_count), hg_me),
        device_id_type=MESH,
    )
    shift.start()
    shift.wait()
    out_ref[...] = jnp.where(me >= 1, got_b[last].astype(jnp.float32), 0.0)


def shard_scan(shard_a, shard_b, shard_count):
    rounds = max(1, (shard_count - 1).bit_length())
    return pl.pallas_call(
        functools.partial(shard_scan_kernel, shard_count),
        out_shape=jax.ShapeDtypeStruct(shard_b.shape, jnp.float32),
        in_specs=[pl.BlockSpec(memory_space=pltpu.VMEM)] * 2,
        out_specs=pl.BlockSpec(memory_space=pltpu.VMEM),
        scratch_shapes=[
            pltpu.VMEM((rounds + 1,) + shard_a.shape, jnp.float32),
            pltpu.VMEM((rounds + 1,) + shard_b.shape, jnp.float32),
            pltpu.VMEM((rounds + 1,) + shard_a.shape, jnp.bfloat16),
            pltpu.VMEM((rounds + 1,) + shard_b.shape, jnp.bfloat16),
            pltpu.VMEM((rounds + 1,) + shard_a.shape, jnp.bfloat16),
            pltpu.VMEM((rounds + 1,) + shard_b.shape, jnp.bfloat16),
            pltpu.SemaphoreType.DMA((2 * rounds + 1,)),
            pltpu.SemaphoreType.DMA((2 * rounds + 1,)),
        ],
        compiler_params=pltpu.CompilerParams(collective_id=1, has_side_effects=True),
    )(shard_a, shard_b)


def span_kernel(
    head_count, q_ref, k_ref, v_ref, gc_ref, gr_ref, shard_a_ref, shard_b_ref, mix_ref, entry_ref
):
    queries = q_ref[...]
    key_vecs = k_ref[...]
    values = v_ref[...]
    decay_col = gc_ref[:, :, 0:1]
    decay_row = gr_ref[...]
    rate = gc_ref[:, :, 1:2]
    block_len = queries.shape[1]
    row_ids = lax.broadcasted_iota(jnp.int32, (1, block_len, block_len), 1)
    col_ids = lax.broadcasted_iota(jnp.int32, (1, block_len, block_len), 2)
    inclusive = row_ids >= col_ids
    strict = row_ids > col_ids
    cum_col = jnp.sum(jnp.where(inclusive, decay_row, 0.0), axis=2, keepdims=True)
    cum_row = jnp.sum(jnp.where(row_ids <= col_ids, decay_col, 0.0), axis=1, keepdims=True)
    gap_mat = cum_col - cum_row
    falloff = jnp.where(inclusive, jnp.exp(jnp.where(inclusive, gap_mat, 0.0)), 0.0)
    key_dots = jnp.einsum("bsd,btd->bst", key_vecs, key_vecs, precision=highest,
                          preferred_element_type=jnp.float32)
    lower_part = jnp.where(strict, rate * falloff * key_dots, 0.0)
    inverse = jnp.where((row_ids // 2 == col_ids // 2) & strict, -lower_part, 0.0) + jnp.where(
        row_ids == col_ids, 1.0, 0.0
    )
    size = 2
    while size < block_len:
        band = (row_ids // (2 * size) == col_ids // (2 * size)) & (row_ids // size != col_ids // size)
        off_blocks = jnp.where(band, lower_part, 0.0)
        step = jnp.einsum("bst,btu->bsu", inverse, off_blocks, precision=highest,
                          preferred_element_type=jnp.float32)
        inverse = inverse - jnp.einsum("bst,btu->bsu", step, inverse, precision=highest,
                                       preferred_element_type=jnp.float32)
        size *= 2
    grow = jnp.exp(cum_col)
    wy_keys = jnp.einsum("bst,btd->bsd", inverse, (rate * grow) * key_vecs, precision=highest,
                         preferred_element_type=jnp.float32)
    wy_values = jnp.einsum("bst,btd->bsd", inverse, rate * values, precision=highest,
                           preferred_element_type=jnp.float32)
    scores = falloff * jnp.einsum("bsd,btd->bst", queries, key_vecs, precision=highest,
                                  preferred_element_type=jnp.float32)
    last = cum_row[:, :, block_len - 1 :]
    tail_keys_t = jnp.swapaxes(jnp.exp(last - cum_col) * key_vecs, 1, 2)
    width = key_vecs.shape[2]
    eye_rows = lax.broadcasted_iota(jnp.int32, (1, width, width), 1)
    eye_cols = lax.broadcasted_iota(jnp.int32, (1, width, width), 2)
    transition = jnp.where(eye_rows == eye_cols, jnp.exp(last), 0.0) - jnp.einsum(
        "bds,bse->bde", tail_keys_t, wy_keys, precision=highest, preferred_element_type=jnp.float32
    )
    written = jnp.einsum("bds,bse->bde", tail_keys_t, wy_values, precision=highest,
                         preferred_element_type=jnp.float32)
    carry_map = grow * queries - jnp.einsum("bst,btd->bsd", scores, wy_keys, precision=highest,
                                            preferred_element_type=jnp.float32)
    local_out = jnp.einsum("bst,bte->bse", scores, wy_values, precision=highest,
                           preferred_element_type=jnp.float32)
    for span in range(queries.shape[0] // head_count):
        heads = slice(span * head_count, (span + 1) * head_count)
        if span == 0:
            mix_ref[heads] = local_out[heads]
            entry_ref[heads] = carry_map[heads]
            prefix_a = transition[heads]
            prefix_b = written[heads]
            continue
        mix_ref[heads] = local_out[heads] + jnp.einsum(
            "hsd,hde->hse", carry_map[heads], prefix_b, precision=highest,
            preferred_element_type=jnp.float32)
        entry_ref[heads] = jnp.einsum("hsd,hde->hse", carry_map[heads], prefix_a, precision=highest,
                                      preferred_element_type=jnp.float32)
        prefix_b = written[heads] + jnp.einsum(
            "hde,hef->hdf", transition[heads], prefix_b, precision=highest,
            preferred_element_type=jnp.float32)
        prefix_a = jnp.einsum("hde,hef->hdf", transition[heads], prefix_a, precision=highest,
                              preferred_element_type=jnp.float32)
    shard_a_ref[...] = prefix_a
    shard_b_ref[...] = prefix_b


def span_terms_kernel(queries, key_vecs, values, log_decay, write_rate):
    lead = queries.shape[:2]
    block_len, width = queries.shape[2], queries.shape[3]
    flat = lambda x: x.reshape((-1,) + x.shape[2:])
    pairs = lead[0] * lead[1]
    decay = log_decay.reshape(pairs, block_len)
    rate = write_rate.reshape(pairs, block_len)
    shard_a, shard_b, local_mix, entry_map = pl.pallas_call(
        functools.partial(span_kernel, lead[1]),
        out_shape=[
            jax.ShapeDtypeStruct((lead[1], width, width), jnp.float32),
            jax.ShapeDtypeStruct((lead[1], width, values.shape[3]), jnp.float32),
            jax.ShapeDtypeStruct((pairs, block_len, values.shape[3]), jnp.float32),
            jax.ShapeDtypeStruct((pairs, block_len, width), jnp.float32),
        ],
        in_specs=[pl.BlockSpec(memory_space=pltpu.VMEM)] * 5,
        out_specs=[pl.BlockSpec(memory_space=pltpu.VMEM)] * 4,
    )(
        flat(queries),
        flat(key_vecs),
        flat(values),
        jnp.stack([decay, rate], axis=-1),
        decay[:, None, :],
    )
    return (
        shard_a,
        shard_b,
        local_mix.reshape(lead + local_mix.shape[1:]),
        entry_map.reshape(lead + entry_map.shape[1:]),
    )


def group_sum_kernel(group_count, part_ref, out_ref, landed, send_sems, recv_sems, own_sem):
    me = lax.axis_index("hg")
    seq_me = lax.axis_index("seq")
    rows = out_ref.shape[0]
    barrier = pltpu.get_barrier_semaphore()
    for step in range(1, group_count):
        peer = lax.rem(me + step, group_count)
        pl.semaphore_signal(barrier, inc=1, device_id=(seq_me, peer), device_id_type=MESH)
    pl.semaphore_wait(barrier, group_count - 1)
    sends = []
    for step in range(1, group_count):
        peer = lax.rem(me + step, group_count)
        copy = pltpu.make_async_remote_copy(
            src_ref=part_ref.at[pl.ds(pl.multiple_of(peer * rows, 8), rows)],
            dst_ref=landed.at[me],
            send_sem=send_sems.at[step],
            recv_sem=recv_sems.at[me],
            device_id=(seq_me, peer),
            device_id_type=MESH,
        )
        copy.start()
        sends.append(copy)
    own = pltpu.make_async_copy(
        part_ref.at[pl.ds(pl.multiple_of(me * rows, 8), rows)], landed.at[me], own_sem
    )
    own.start()
    own.wait()
    for step in range(1, group_count):
        source = lax.rem(me + group_count - step, group_count)
        pltpu.make_async_remote_copy(
            src_ref=part_ref.at[pl.ds(0, rows)],
            dst_ref=landed.at[source],
            send_sem=send_sems.at[step],
            recv_sem=recv_sems.at[source],
            device_id=(seq_me, source),
            device_id_type=MESH,
        ).wait_recv()
    for copy in sends:
        copy.wait_send()
    total = landed[0].astype(jnp.float32)
    for slot in range(1, group_count):
        total = total + landed[slot].astype(jnp.float32)
    out_ref[...] = total.astype(out_ref.dtype)


def group_sum(part, group_count):
    if group_count == 1:
        return part
    rows = part.shape[0] // group_count
    cols = part.shape[1]
    return pl.pallas_call(
        functools.partial(group_sum_kernel, group_count),
        out_shape=jax.ShapeDtypeStruct((rows, cols), part.dtype),
        in_specs=[pl.BlockSpec(memory_space=pltpu.VMEM)],
        out_specs=pl.BlockSpec(memory_space=pltpu.VMEM),
        scratch_shapes=[
            pltpu.VMEM((group_count, rows, cols), part.dtype),
            pltpu.SemaphoreType.DMA((group_count,)),
            pltpu.SemaphoreType.DMA((group_count,)),
            pltpu.SemaphoreType.DMA,
        ],
        compiler_params=pltpu.CompilerParams(collective_id=0, has_side_effects=True),
    )(part)


def on_device(
    hidden_in,
    w_query,
    w_key,
    w_value,
    w_zgate,
    w_decay,
    w_beta,
    conv_query,
    conv_key,
    conv_value,
    a_log,
    dt_bias,
    norm_gain,
    w_out,
):
    tok_rows = hidden_in.shape[0]
    pre_query, pre_key, pre_value = project_inputs(hidden_in, w_query, w_key, w_value)
    kernel_len = conv_query.shape[0]
    rim_rows = tok_rows - kernel_len + 1
    rim_block = jnp.concatenate(
        [pre_query[rim_rows:], pre_key[rim_rows:], pre_value[rim_rows:]], axis=1
    )
    prior = passed_along(rim_block, "seq", 1)
    queries, key_vecs, values, log_decay, write_rate, zgate = mixer_inputs(
        hidden_in,
        pre_query,
        pre_key,
        pre_value,
        prior,
        conv_query,
        conv_key,
        conv_value,
        w_zgate,
        w_decay,
        w_beta,
        a_log,
        dt_bias,
    )
    shard_a, shard_b, local_mix, entry_map = span_terms_kernel(
        to_blocks(queries),
        to_blocks(key_vecs),
        to_blocks(values),
        to_blocks(log_decay[..., None])[..., 0],
        to_blocks(write_rate[..., None])[..., 0],
    )
    head_count = values.shape[1]
    state_in = shard_scan(shard_a, shard_b, lax.axis_size("seq"))
    produced = local_mix + jnp.einsum("jhsd,hde->jhse", entry_map, state_in, precision=highest)
    produced = produced.transpose(0, 2, 1, 3).reshape(tok_rows, head_count, DV)
    gated = gated_output(produced, zgate, norm_gain)
    part = jnp.dot(gated, w_out, preferred_element_type=jnp.float32).astype(jnp.bfloat16)
    return group_sum(part, lax.axis_size("hg"))


def solution(mesh):
    return jax.shard_map(
        on_device,
        mesh=mesh,
        in_specs=(
            P("seq", None),
            P(None, "hg"),
            P(None, "hg"),
            P(None, "hg"),
            P(None, "hg"),
            P(None, "hg"),
            P(None, "hg"),
            P(None, "hg"),
            P(None, "hg"),
            P(None, "hg"),
            P("hg"),
            P("hg"),
            P(),
            P("hg", None),
        ),
        out_specs=P(("seq", "hg"), None),
        check_vma=False,
    )
```

```python
import functools

import jax
import numpy as np
import jax.numpy as jnp
from jax import lax
from jax.experimental import pallas as pl
from jax.experimental.pallas import tpu as pltpu
from jax.sharding import PartitionSpec as P

MESH = pl.DeviceIdType.MESH

VH = 32
KH = 16
DK = 128
DV = 128
SPAN = 64


highest = lax.Precision.HIGH
norm_eps = 1e-06


def passed_along(block, axis, distance):
    devices = range(lax.axis_size(axis))
    route = [(i - distance, i) for i in devices if i - distance in devices]
    return lax.ppermute(block, axis, route)


def project_inputs(hidden_in, w_query, w_key, w_value):
    pre_query = jnp.dot(hidden_in, w_query, preferred_element_type=jnp.float32).astype(jnp.bfloat16)
    pre_key = jnp.dot(hidden_in, w_key, preferred_element_type=jnp.float32).astype(jnp.bfloat16)
    pre_value = jnp.dot(hidden_in, w_value, preferred_element_type=jnp.float32).astype(jnp.bfloat16)
    return (pre_query, pre_key, pre_value)


def conv_silu(projected, kernel, prior):
    kernel_len = kernel.shape[0]
    tok_rows = projected.shape[0]
    padded = jnp.concatenate([prior.astype(jnp.float32), projected.astype(jnp.float32)], axis=0)
    summed = jnp.zeros((tok_rows, projected.shape[1]), jnp.float32)
    for offset in range(kernel_len):
        summed = summed + kernel[offset].astype(jnp.float32) * padded[offset : offset + tok_rows]
    return jax.nn.silu(summed)


def unit_length(vectors):
    return vectors * lax.rsqrt(jnp.sum(vectors * vectors, axis=-1, keepdims=True) + norm_eps)


def mixer_inputs(
    hidden_in,
    pre_query,
    pre_key,
    pre_value,
    prior,
    conv_query,
    conv_key,
    conv_value,
    w_zgate,
    w_decay,
    w_beta,
    a_log,
    dt_bias,
):
    tok_rows = hidden_in.shape[0]
    query_cols = pre_query.shape[1]
    key_cols = pre_key.shape[1]
    ratio = VH // KH
    queries = unit_length(
        conv_silu(pre_query, conv_query, prior[:, :query_cols]).reshape(tok_rows, -1, DK)
    ) * DK ** (-0.5)
    key_vecs = unit_length(
        conv_silu(pre_key, conv_key, prior[:, query_cols : query_cols + key_cols]).reshape(
            tok_rows, -1, DK
        )
    )
    values = conv_silu(pre_value, conv_value, prior[:, query_cols + key_cols :]).reshape(
        tok_rows, -1, DV
    )
    queries = jnp.repeat(queries, ratio, axis=1)
    key_vecs = jnp.repeat(key_vecs, ratio, axis=1)
    zgate = jnp.dot(hidden_in, w_zgate, preferred_element_type=jnp.float32).astype(jnp.bfloat16)
    rate_logits = jnp.dot(hidden_in, w_decay, preferred_element_type=jnp.float32)
    log_decay = -jnp.exp(a_log) * jax.nn.softplus(rate_logits + dt_bias)
    write_rate = jax.nn.sigmoid(jnp.dot(hidden_in, w_beta, preferred_element_type=jnp.float32))
    return (queries, key_vecs, values, log_decay, write_rate, zgate)


def to_blocks(array_3d):
    tok_rows, head_count = (array_3d.shape[0], array_3d.shape[1])
    return array_3d.reshape(tok_rows // SPAN, SPAN, head_count, -1).transpose(0, 2, 1, 3)


def unit_lower_inverse(lower_part):
    block_len = lower_part.shape[-1]
    row_ids = np.arange(block_len)[:, None]
    col_ids = np.arange(block_len)[None, :]
    first = jnp.asarray((row_ids // 2 == col_ids // 2) & (row_ids != col_ids), jnp.float32)
    inverse = lax.optimization_barrier(
        jnp.asarray(np.eye(block_len), jnp.float32) - lower_part * first
    )
    size = 2
    while size < block_len:
        band = (row_ids // (2 * size) == col_ids // (2 * size)) & (row_ids // size != col_ids // size)
        off_blocks = lower_part * jnp.asarray(band, jnp.float32)
        step = jnp.einsum("...st,...tu->...su", inverse, off_blocks, precision=highest)
        inverse = inverse - jnp.einsum("...st,...tu->...su", step, inverse, precision=highest)
        size *= 2
    return inverse


def span_terms(queries, key_vecs, values, log_decay, write_rate):
    block_len = log_decay.shape[-1]
    cum_decay = jnp.cumsum(log_decay, axis=-1)
    row_ids = lax.broadcasted_iota(jnp.int32, (block_len, block_len), 0)
    col_ids = lax.broadcasted_iota(jnp.int32, (block_len, block_len), 1)
    inclusive = row_ids >= col_ids
    strict = row_ids > col_ids
    gap_mat = cum_decay[..., :, None] - cum_decay[..., None, :]
    falloff = jnp.where(inclusive, jnp.exp(jnp.where(inclusive, gap_mat, 0.0)), 0.0)
    key_dots = jnp.einsum("...sd,...td->...st", key_vecs, key_vecs, precision=highest)
    lower_part = jnp.where(strict, write_rate[..., :, None] * falloff * key_dots, 0.0)
    inverse = unit_lower_inverse(lower_part)
    wy_keys = jnp.einsum(
        "...st,...td->...sd",
        inverse,
        (write_rate * jnp.exp(cum_decay))[..., None] * key_vecs,
        precision=highest,
    )
    wy_values = jnp.einsum(
        "...st,...td->...sd", inverse, write_rate[..., None] * values, precision=highest
    )
    scores = falloff * jnp.einsum("...sd,...td->...st", queries, key_vecs, precision=highest)
    tail_keys = jnp.exp(cum_decay[..., -1:] - cum_decay)[..., None] * key_vecs
    whole_decay = jnp.exp(cum_decay[..., -1])[..., None, None]
    transition = whole_decay * jnp.eye(key_vecs.shape[-1], dtype=jnp.float32) - jnp.einsum(
        "...sd,...se->...de", tail_keys, wy_keys, precision=highest
    )
    written = jnp.einsum("...sd,...se->...de", tail_keys, wy_values, precision=highest)
    carry_map = jnp.exp(cum_decay)[..., None] * queries - jnp.einsum(
        "...st,...td->...sd", scores, wy_keys, precision=highest
    )
    local_out = jnp.einsum("...st,...te->...se", scores, wy_values, precision=highest)
    return (transition, written, carry_map, local_out)


def gated_output(produced, zgate, norm_gain):
    tok_rows = produced.shape[0]
    mean_sq = jnp.mean(produced * produced, axis=-1, keepdims=True)
    gate_vals = jax.nn.silu(zgate.astype(jnp.float32).reshape(produced.shape))
    normed = produced * lax.rsqrt(mean_sq + norm_eps) * norm_gain * gate_vals
    return normed.reshape(tok_rows, -1).astype(jnp.bfloat16)


def advance(state_now, per_span):
    transition, written, carry_map, local_out = per_span
    produced = jnp.einsum("hsd,hde->hse", carry_map, state_now, precision=highest) + local_out
    state_next = jnp.einsum("hde,hef->hdf", transition, state_now, precision=highest) + written
    return (state_next, produced)


def apply_shard(trans_mat, state_now, written):
    return jnp.einsum("hde,hef->hdf", trans_mat, state_now, precision=highest) + written


def shard_scan_kernel(
    shard_count, a_ref, b_ref, out_ref, cur_a, cur_b, out_a, out_b, got_a, got_b, send_sems, recv_sems
):
    me = lax.axis_index("seq")
    hg_me = lax.axis_index("hg")
    head_count = a_ref.shape[0]
    distances = []
    distance = 1
    while distance < shard_count:
        distances.append(distance)
        distance *= 2
    barrier = pltpu.get_barrier_semaphore()
    for distance in distances:
        for target in (lax.rem(me + distance, shard_count), lax.rem(me + shard_count - distance, shard_count)):
            pl.semaphore_signal(barrier, inc=1, device_id=(target, hg_me), device_id_type=MESH)
    pl.semaphore_wait(barrier, 2 * len(distances))
    cur_a[0] = a_ref[...]
    cur_b[0] = b_ref[...]
    out_a[0] = a_ref[...].astype(out_a.dtype)
    out_b[0] = b_ref[...].astype(out_b.dtype)
    sem_index = 0
    for round_index, distance in enumerate(distances):
        target = lax.rem(me + distance, shard_count)
        sends_a = round_index + 1 < len(distances)
        copies = [
            pltpu.make_async_remote_copy(
                src_ref=out_b.at[round_index],
                dst_ref=got_b.at[round_index],
                send_sem=send_sems.at[sem_index],
                recv_sem=recv_sems.at[sem_index],
                device_id=(target, hg_me),
                device_id_type=MESH,
            )
        ]
        if sends_a:
            copies.append(
                pltpu.make_async_remote_copy(
                    src_ref=out_a.at[round_index],
                    dst_ref=got_a.at[round_index],
                    send_sem=send_sems.at[sem_index + 1],
                    recv_sem=recv_sems.at[sem_index + 1],
                    device_id=(target, hg_me),
                    device_id_type=MESH,
                )
            )
        sem_index += len(copies)
        has_prev = me >= distance
        has_next = me + distance < shard_count

        @pl.when(has_next)
        def _():
            for copy in copies:
                copy.start()

        @pl.when(has_prev)
        def _():
            for copy in copies:
                copy.wait_recv()

        @pl.when(jnp.logical_not(has_prev))
        def _():
            got_b[round_index] = jnp.zeros(got_b.shape[1:], got_b.dtype)
            if sends_a:
                got_a[round_index] = jnp.zeros(got_a.shape[1:], got_a.dtype)

        @pl.when(has_next)
        def _():
            for copy in copies:
                copy.wait_send()
        for head in range(head_count):
            own_a = cur_a[round_index, head]
            own_b = cur_b[round_index, head]
            joined_b = (
                jnp.dot(own_a, got_b[round_index, head].astype(jnp.float32), precision=highest,
                        preferred_element_type=jnp.float32)
                + own_b
            )
            next_b = jnp.where(has_prev, joined_b, own_b)
            cur_b[round_index + 1, head] = next_b
            out_b[round_index + 1, head] = next_b.astype(out_b.dtype)
            if sends_a:
                joined_a = jnp.dot(own_a, got_a[round_index, head].astype(jnp.float32),
                                   precision=highest, preferred_element_type=jnp.float32)
                next_a = jnp.where(has_prev, joined_a, own_a)
                cur_a[round_index + 1, head] = next_a
                out_a[round_index + 1, head] = next_a.astype(out_a.dtype)
    last = len(distances)
    shift = pltpu.make_async_remote_copy(
        src_ref=out_b.at[last],
        dst_ref=got_b.at[last],
        send_sem=send_sems.at[sem_index],
        recv_sem=recv_sems.at[sem_index],
        device_id=(lax.rem(me + 1, shard_count), hg_me),
        device_id_type=MESH,
    )
    shift.start()
    shift.wait()
    out_ref[...] = jnp.where(me >= 1, got_b[last].astype(jnp.float32), 0.0)


def shard_scan(shard_a, shard_b, shard_count):
    rounds = max(1, (shard_count - 1).bit_length())
    return pl.pallas_call(
        functools.partial(shard_scan_kernel, shard_count),
        out_shape=jax.ShapeDtypeStruct(shard_b.shape, jnp.float32),
        in_specs=[pl.BlockSpec(memory_space=pltpu.VMEM)] * 2,
        out_specs=pl.BlockSpec(memory_space=pltpu.VMEM),
        scratch_shapes=[
            pltpu.VMEM((rounds + 1,) + shard_a.shape, jnp.float32),
            pltpu.VMEM((rounds + 1,) + shard_b.shape, jnp.float32),
            pltpu.VMEM((rounds + 1,) + shard_a.shape, jnp.bfloat16),
            pltpu.VMEM((rounds + 1,) + shard_b.shape, jnp.bfloat16),
            pltpu.VMEM((rounds + 1,) + shard_a.shape, jnp.bfloat16),
            pltpu.VMEM((rounds + 1,) + shard_b.shape, jnp.bfloat16),
            pltpu.SemaphoreType.DMA((2 * rounds + 1,)),
            pltpu.SemaphoreType.DMA((2 * rounds + 1,)),
        ],
        compiler_params=pltpu.CompilerParams(collective_id=1, has_side_effects=True),
    )(shard_a, shard_b)


def span_kernel(
    head_count, q_ref, k_ref, v_ref, gc_ref, gr_ref, shard_a_ref, shard_b_ref, mix_ref, entry_ref
):
    queries = q_ref[...]
    key_vecs = k_ref[...]
    values = v_ref[...]
    decay_col = gc_ref[:, :, 0:1]
    decay_row = gr_ref[...]
    rate = gc_ref[:, :, 1:2]
    block_len = queries.shape[1]
    row_ids = lax.broadcasted_iota(jnp.int32, (1, block_len, block_len), 1)
    col_ids = lax.broadcasted_iota(jnp.int32, (1, block_len, block_len), 2)
    inclusive = row_ids >= col_ids
    strict = row_ids > col_ids
    cum_col = jnp.sum(jnp.where(inclusive, decay_row, 0.0), axis=2, keepdims=True)
    cum_row = jnp.sum(jnp.where(row_ids <= col_ids, decay_col, 0.0), axis=1, keepdims=True)
    gap_mat = cum_col - cum_row
    falloff = jnp.where(inclusive, jnp.exp(jnp.where(inclusive, gap_mat, 0.0)), 0.0)
    key_dots = jnp.einsum("bsd,btd->bst", key_vecs, key_vecs, precision=highest,
                          preferred_element_type=jnp.float32)
    lower_part = jnp.where(strict, rate * falloff * key_dots, 0.0)
    inverse = jnp.where((row_ids // 2 == col_ids // 2) & strict, -lower_part, 0.0) + jnp.where(
        row_ids == col_ids, 1.0, 0.0
    )
    size = 2
    while size < block_len:
        band = (row_ids // (2 * size) == col_ids // (2 * size)) & (row_ids // size != col_ids // size)
        off_blocks = jnp.where(band, lower_part, 0.0)
        step = jnp.einsum("bst,btu->bsu", inverse, off_blocks, precision=highest,
                          preferred_element_type=jnp.float32)
        inverse = inverse - jnp.einsum("bst,btu->bsu", step, inverse, precision=highest,
                                       preferred_element_type=jnp.float32)
        size *= 2
    grow = jnp.exp(cum_col)
    wy_keys = jnp.einsum("bst,btd->bsd", inverse, (rate * grow) * key_vecs, precision=highest,
                         preferred_element_type=jnp.float32)
    wy_values = jnp.einsum("bst,btd->bsd", inverse, rate * values, precision=highest,
                           preferred_element_type=jnp.float32)
    scores = falloff * jnp.einsum("bsd,btd->bst", queries, key_vecs, precision=highest,
                                  preferred_element_type=jnp.float32)
    last = cum_row[:, :, block_len - 1 :]
    tail_keys_t = jnp.swapaxes(jnp.exp(last - cum_col) * key_vecs, 1, 2)
    width = key_vecs.shape[2]
    eye_rows = lax.broadcasted_iota(jnp.int32, (1, width, width), 1)
    eye_cols = lax.broadcasted_iota(jnp.int32, (1, width, width), 2)
    transition = jnp.where(eye_rows == eye_cols, jnp.exp(last), 0.0) - jnp.einsum(
        "bds,bse->bde", tail_keys_t, wy_keys, precision=highest, preferred_element_type=jnp.float32
    )
    written = jnp.einsum("bds,bse->bde", tail_keys_t, wy_values, precision=highest,
                         preferred_element_type=jnp.float32)
    carry_map = grow * queries - jnp.einsum("bst,btd->bsd", scores, wy_keys, precision=highest,
                                            preferred_element_type=jnp.float32)
    local_out = jnp.einsum("bst,bte->bse", scores, wy_values, precision=highest,
                           preferred_element_type=jnp.float32)
    for span in range(queries.shape[0] // head_count):
        heads = slice(span * head_count, (span + 1) * head_count)
        if span == 0:
            mix_ref[heads] = local_out[heads]
            entry_ref[heads] = carry_map[heads]
            prefix_a = transition[heads]
            prefix_b = written[heads]
            continue
        mix_ref[heads] = local_out[heads] + jnp.einsum(
            "hsd,hde->hse", carry_map[heads], prefix_b, precision=highest,
            preferred_element_type=jnp.float32)
        entry_ref[heads] = jnp.einsum("hsd,hde->hse", carry_map[heads], prefix_a, precision=highest,
                                      preferred_element_type=jnp.float32)
        prefix_b = written[heads] + jnp.einsum(
            "hde,hef->hdf", transition[heads], prefix_b, precision=highest,
            preferred_element_type=jnp.float32)
        prefix_a = jnp.einsum("hde,hef->hdf", transition[heads], prefix_a, precision=highest,
                              preferred_element_type=jnp.float32)
    shard_a_ref[...] = prefix_a
    shard_b_ref[...] = prefix_b


def span_terms_kernel(queries, key_vecs, values, log_decay, write_rate):
    lead = queries.shape[:2]
    block_len, width = queries.shape[2], queries.shape[3]
    flat = lambda x: x.reshape((-1,) + x.shape[2:])
    pairs = lead[0] * lead[1]
    decay = log_decay.reshape(pairs, block_len)
    rate = write_rate.reshape(pairs, block_len)
    shard_a, shard_b, local_mix, entry_map = pl.pallas_call(
        functools.partial(span_kernel, lead[1]),
        out_shape=[
            jax.ShapeDtypeStruct((lead[1], width, width), jnp.float32),
            jax.ShapeDtypeStruct((lead[1], width, values.shape[3]), jnp.float32),
            jax.ShapeDtypeStruct((pairs, block_len, values.shape[3]), jnp.float32),
            jax.ShapeDtypeStruct((pairs, block_len, width), jnp.float32),
        ],
        in_specs=[pl.BlockSpec(memory_space=pltpu.VMEM)] * 5,
        out_specs=[pl.BlockSpec(memory_space=pltpu.VMEM)] * 4,
    )(
        flat(queries),
        flat(key_vecs),
        flat(values),
        jnp.stack([decay, rate], axis=-1),
        decay[:, None, :],
    )
    return (
        shard_a,
        shard_b,
        local_mix.reshape(lead + local_mix.shape[1:]),
        entry_map.reshape(lead + entry_map.shape[1:]),
    )


def group_sum_kernel(group_count, part_ref, out_ref, landed, send_sems, recv_sems, own_sem):
    me = lax.axis_index("hg")
    seq_me = lax.axis_index("seq")
    rows = out_ref.shape[0]
    barrier = pltpu.get_barrier_semaphore()
    for step in range(1, group_count):
        peer = lax.rem(me + step, group_count)
        pl.semaphore_signal(barrier, inc=1, device_id=(seq_me, peer), device_id_type=MESH)
    pl.semaphore_wait(barrier, group_count - 1)
    sends = []
    for step in range(1, group_count):
        peer = lax.rem(me + step, group_count)
        copy = pltpu.make_async_remote_copy(
            src_ref=part_ref.at[pl.ds(pl.multiple_of(peer * rows, 8), rows)],
            dst_ref=landed.at[me],
            send_sem=send_sems.at[step],
            recv_sem=recv_sems.at[me],
            device_id=(seq_me, peer),
            device_id_type=MESH,
        )
        copy.start()
        sends.append(copy)
    own = pltpu.make_async_copy(
        part_ref.at[pl.ds(pl.multiple_of(me * rows, 8), rows)], landed.at[me], own_sem
    )
    own.start()
    own.wait()
    for step in range(1, group_count):
        source = lax.rem(me + group_count - step, group_count)
        pltpu.make_async_remote_copy(
            src_ref=part_ref.at[pl.ds(0, rows)],
            dst_ref=landed.at[source],
            send_sem=send_sems.at[step],
            recv_sem=recv_sems.at[source],
            device_id=(seq_me, source),
            device_id_type=MESH,
        ).wait_recv()
    for copy in sends:
        copy.wait_send()
    total = landed[0].astype(jnp.float32)
    for slot in range(1, group_count):
        total = total + landed[slot].astype(jnp.float32)
    out_ref[...] = total.astype(out_ref.dtype)


def group_sum(part, group_count):
    if group_count == 1:
        return part
    rows = part.shape[0] // group_count
    cols = part.shape[1]
    return pl.pallas_call(
        functools.partial(group_sum_kernel, group_count),
        out_shape=jax.ShapeDtypeStruct((rows, cols), part.dtype),
        in_specs=[pl.BlockSpec(memory_space=pltpu.VMEM)],
        out_specs=pl.BlockSpec(memory_space=pltpu.VMEM),
        scratch_shapes=[
            pltpu.VMEM((group_count, rows, cols), part.dtype),
            pltpu.SemaphoreType.DMA((group_count,)),
            pltpu.SemaphoreType.DMA((group_count,)),
            pltpu.SemaphoreType.DMA,
        ],
        compiler_params=pltpu.CompilerParams(collective_id=0, has_side_effects=True),
    )(part)


def on_device(
    hidden_in,
    w_query,
    w_key,
    w_value,
    w_zgate,
    w_decay,
    w_beta,
    conv_query,
    conv_key,
    conv_value,
    a_log,
    dt_bias,
    norm_gain,
    w_out,
):
    tok_rows = hidden_in.shape[0]
    pre_query, pre_key, pre_value = project_inputs(hidden_in, w_query, w_key, w_value)
    kernel_len = conv_query.shape[0]
    rim_rows = tok_rows - kernel_len + 1
    rim_block = jnp.concatenate(
        [pre_query[rim_rows:], pre_key[rim_rows:], pre_value[rim_rows:]], axis=1
    )
    prior = passed_along(rim_block, "seq", 1)
    queries, key_vecs, values, log_decay, write_rate, zgate = mixer_inputs(
        hidden_in,
        pre_query,
        pre_key,
        pre_value,
        prior,
        conv_query,
        conv_key,
        conv_value,
        w_zgate,
        w_decay,
        w_beta,
        a_log,
        dt_bias,
    )
    shard_a, shard_b, local_mix, entry_map = span_terms_kernel(
        to_blocks(queries),
        to_blocks(key_vecs),
        to_blocks(values),
        to_blocks(log_decay[..., None])[..., 0],
        to_blocks(write_rate[..., None])[..., 0],
    )
    head_count = values.shape[1]
    state_in = shard_scan(shard_a, shard_b, lax.axis_size("seq"))
    produced = local_mix + jnp.einsum("jhsd,hde->jhse", entry_map, state_in, precision=highest)
    produced = produced.transpose(0, 2, 1, 3).reshape(tok_rows, head_count, DV)
    gated = gated_output(produced, zgate, norm_gain)
    part = jnp.dot(gated, w_out, preferred_element_type=jnp.float32).astype(jnp.bfloat16)
    return group_sum(part, lax.axis_size("hg"))


def solution(mesh):
    return jax.shard_map(
        on_device,
        mesh=mesh,
        in_specs=(
            P("seq", None),
            P(None, "hg"),
            P(None, "hg"),
            P(None, "hg"),
            P(None, "hg"),
            P(None, "hg"),
            P(None, "hg"),
            P(None, "hg"),
            P(None, "hg"),
            P(None, "hg"),
            P("hg"),
            P("hg"),
            P(),
            P("hg", None),
        ),
        out_specs=P(("seq", "hg"), None),
        check_vma=False,
    )
```

```python
import functools

import jax
import numpy as np
import jax.numpy as jnp
from jax import lax
from jax.experimental import pallas as pl
from jax.experimental.pallas import tpu as pltpu
from jax.sharding import PartitionSpec as P

MESH = pl.DeviceIdType.MESH

VH = 32
KH = 16
DK = 128
DV = 128
SPAN = 64


highest = lax.Precision.HIGH
norm_eps = 1e-06


def passed_along(block, axis, distance):
    devices = range(lax.axis_size(axis))
    route = [(i - distance, i) for i in devices if i - distance in devices]
    return lax.ppermute(block, axis, route)


def project_inputs(hidden_in, w_query, w_key, w_value):
    pre_query = jnp.dot(hidden_in, w_query, preferred_element_type=jnp.float32).astype(jnp.bfloat16)
    pre_key = jnp.dot(hidden_in, w_key, preferred_element_type=jnp.float32).astype(jnp.bfloat16)
    pre_value = jnp.dot(hidden_in, w_value, preferred_element_type=jnp.float32).astype(jnp.bfloat16)
    return (pre_query, pre_key, pre_value)


def conv_silu(projected, kernel, prior):
    kernel_len = kernel.shape[0]
    tok_rows = projected.shape[0]
    padded = jnp.concatenate([prior.astype(jnp.float32), projected.astype(jnp.float32)], axis=0)
    summed = jnp.zeros((tok_rows, projected.shape[1]), jnp.float32)
    for offset in range(kernel_len):
        summed = summed + kernel[offset].astype(jnp.float32) * padded[offset : offset + tok_rows]
    return jax.nn.silu(summed)


def unit_length(vectors):
    return vectors * lax.rsqrt(jnp.sum(vectors * vectors, axis=-1, keepdims=True) + norm_eps)


def mixer_inputs(
    hidden_in,
    pre_query,
    pre_key,
    pre_value,
    prior,
    conv_query,
    conv_key,
    conv_value,
    w_zgate,
    w_decay,
    w_beta,
    a_log,
    dt_bias,
):
    tok_rows = hidden_in.shape[0]
    query_cols = pre_query.shape[1]
    key_cols = pre_key.shape[1]
    ratio = VH // KH
    queries = unit_length(
        conv_silu(pre_query, conv_query, prior[:, :query_cols]).reshape(tok_rows, -1, DK)
    ) * DK ** (-0.5)
    key_vecs = unit_length(
        conv_silu(pre_key, conv_key, prior[:, query_cols : query_cols + key_cols]).reshape(
            tok_rows, -1, DK
        )
    )
    values = conv_silu(pre_value, conv_value, prior[:, query_cols + key_cols :]).reshape(
        tok_rows, -1, DV
    )
    queries = jnp.repeat(queries, ratio, axis=1)
    key_vecs = jnp.repeat(key_vecs, ratio, axis=1)
    zgate = jnp.dot(hidden_in, w_zgate, preferred_element_type=jnp.float32).astype(jnp.bfloat16)
    rate_logits = jnp.dot(hidden_in, w_decay, preferred_element_type=jnp.float32)
    log_decay = -jnp.exp(a_log) * jax.nn.softplus(rate_logits + dt_bias)
    write_rate = jax.nn.sigmoid(jnp.dot(hidden_in, w_beta, preferred_element_type=jnp.float32))
    return (queries, key_vecs, values, log_decay, write_rate, zgate)


def to_blocks(array_3d):
    tok_rows, head_count = (array_3d.shape[0], array_3d.shape[1])
    return array_3d.reshape(tok_rows // SPAN, SPAN, head_count, -1).transpose(0, 2, 1, 3)


def unit_lower_inverse(lower_part):
    block_len = lower_part.shape[-1]
    row_ids = np.arange(block_len)[:, None]
    col_ids = np.arange(block_len)[None, :]
    first = jnp.asarray((row_ids // 2 == col_ids // 2) & (row_ids != col_ids), jnp.float32)
    inverse = lax.optimization_barrier(
        jnp.asarray(np.eye(block_len), jnp.float32) - lower_part * first
    )
    size = 2
    while size < block_len:
        band = (row_ids // (2 * size) == col_ids // (2 * size)) & (row_ids // size != col_ids // size)
        off_blocks = lower_part * jnp.asarray(band, jnp.float32)
        step = jnp.einsum("...st,...tu->...su", inverse, off_blocks, precision=highest)
        inverse = inverse - jnp.einsum("...st,...tu->...su", step, inverse, precision=highest)
        size *= 2
    return inverse


def span_terms(queries, key_vecs, values, log_decay, write_rate):
    block_len = log_decay.shape[-1]
    cum_decay = jnp.cumsum(log_decay, axis=-1)
    row_ids = lax.broadcasted_iota(jnp.int32, (block_len, block_len), 0)
    col_ids = lax.broadcasted_iota(jnp.int32, (block_len, block_len), 1)
    inclusive = row_ids >= col_ids
    strict = row_ids > col_ids
    gap_mat = cum_decay[..., :, None] - cum_decay[..., None, :]
    falloff = jnp.where(inclusive, jnp.exp(jnp.where(inclusive, gap_mat, 0.0)), 0.0)
    key_dots = jnp.einsum("...sd,...td->...st", key_vecs, key_vecs, precision=highest)
    lower_part = jnp.where(strict, write_rate[..., :, None] * falloff * key_dots, 0.0)
    inverse = unit_lower_inverse(lower_part)
    wy_keys = jnp.einsum(
        "...st,...td->...sd",
        inverse,
        (write_rate * jnp.exp(cum_decay))[..., None] * key_vecs,
        precision=highest,
    )
    wy_values = jnp.einsum(
        "...st,...td->...sd", inverse, write_rate[..., None] * values, precision=highest
    )
    scores = falloff * jnp.einsum("...sd,...td->...st", queries, key_vecs, precision=highest)
    tail_keys = jnp.exp(cum_decay[..., -1:] - cum_decay)[..., None] * key_vecs
    whole_decay = jnp.exp(cum_decay[..., -1])[..., None, None]
    transition = whole_decay * jnp.eye(key_vecs.shape[-1], dtype=jnp.float32) - jnp.einsum(
        "...sd,...se->...de", tail_keys, wy_keys, precision=highest
    )
    written = jnp.einsum("...sd,...se->...de", tail_keys, wy_values, precision=highest)
    carry_map = jnp.exp(cum_decay)[..., None] * queries - jnp.einsum(
        "...st,...td->...sd", scores, wy_keys, precision=highest
    )
    local_out = jnp.einsum("...st,...te->...se", scores, wy_values, precision=highest)
    return (transition, written, carry_map, local_out)


def gated_output(produced, zgate, norm_gain):
    tok_rows = produced.shape[0]
    mean_sq = jnp.mean(produced * produced, axis=-1, keepdims=True)
    gate_vals = jax.nn.silu(zgate.astype(jnp.float32).reshape(produced.shape))
    normed = produced * lax.rsqrt(mean_sq + norm_eps) * norm_gain * gate_vals
    return normed.reshape(tok_rows, -1).astype(jnp.bfloat16)


def advance(state_now, per_span):
    transition, written, carry_map, local_out = per_span
    produced = jnp.einsum("hsd,hde->hse", carry_map, state_now, precision=highest) + local_out
    state_next = jnp.einsum("hde,hef->hdf", transition, state_now, precision=highest) + written
    return (state_next, produced)


def apply_shard(trans_mat, state_now, written):
    return jnp.einsum("hde,hef->hdf", trans_mat, state_now, precision=highest) + written


def shard_scan_kernel(
    shard_count, a_ref, b_ref, out_ref, cur_a, cur_b, out_a, out_b, got_a, got_b, send_sems, recv_sems
):
    me = lax.axis_index("seq")
    hg_me = lax.axis_index("hg")
    head_count = a_ref.shape[0]
    distances = []
    distance = 1
    while distance < shard_count:
        distances.append(distance)
        distance *= 2
    barrier = pltpu.get_barrier_semaphore()
    for distance in distances:
        for target in (lax.rem(me + distance, shard_count), lax.rem(me + shard_count - distance, shard_count)):
            pl.semaphore_signal(barrier, inc=1, device_id=(target, hg_me), device_id_type=MESH)
    pl.semaphore_wait(barrier, 2 * len(distances))
    cur_a[0] = a_ref[...]
    cur_b[0] = b_ref[...]
    out_a[0] = a_ref[...].astype(out_a.dtype)
    out_b[0] = b_ref[...].astype(out_b.dtype)
    sem_index = 0
    for round_index, distance in enumerate(distances):
        target = lax.rem(me + distance, shard_count)
        sends_a = round_index + 1 < len(distances)
        copies = [
            pltpu.make_async_remote_copy(
                src_ref=out_b.at[round_index],
                dst_ref=got_b.at[round_index],
                send_sem=send_sems.at[sem_index],
                recv_sem=recv_sems.at[sem_index],
                device_id=(target, hg_me),
                device_id_type=MESH,
            )
        ]
        if sends_a:
            copies.append(
                pltpu.make_async_remote_copy(
                    src_ref=out_a.at[round_index],
                    dst_ref=got_a.at[round_index],
                    send_sem=send_sems.at[sem_index + 1],
                    recv_sem=recv_sems.at[sem_index + 1],
                    device_id=(target, hg_me),
                    device_id_type=MESH,
                )
            )
        sem_index += len(copies)
        for copy in copies:
            copy.start()
        for copy in copies:
            copy.wait()
        has_prev = me >= distance
        for head in range(head_count):
            own_a = cur_a[round_index, head]
            own_b = cur_b[round_index, head]
            joined_b = (
                jnp.dot(own_a, got_b[round_index, head].astype(jnp.float32), precision=highest,
                        preferred_element_type=jnp.float32)
                + own_b
            )
            next_b = jnp.where(has_prev, joined_b, own_b)
            cur_b[round_index + 1, head] = next_b
            out_b[round_index + 1, head] = next_b.astype(out_b.dtype)
            if sends_a:
                joined_a = jnp.dot(own_a, got_a[round_index, head].astype(jnp.float32),
                                   precision=highest, preferred_element_type=jnp.float32)
                next_a = jnp.where(has_prev, joined_a, own_a)
                cur_a[round_index + 1, head] = next_a
                out_a[round_index + 1, head] = next_a.astype(out_a.dtype)
    last = len(distances)
    shift = pltpu.make_async_remote_copy(
        src_ref=out_b.at[last],
        dst_ref=got_b.at[last],
        send_sem=send_sems.at[sem_index],
        recv_sem=recv_sems.at[sem_index],
        device_id=(lax.rem(me + 1, shard_count), hg_me),
        device_id_type=MESH,
    )
    shift.start()
    shift.wait()
    out_ref[...] = jnp.where(me >= 1, got_b[last].astype(jnp.float32), 0.0)


def shard_scan(shard_a, shard_b, shard_count):
    rounds = max(1, (shard_count - 1).bit_length())
    return pl.pallas_call(
        functools.partial(shard_scan_kernel, shard_count),
        out_shape=jax.ShapeDtypeStruct(shard_b.shape, jnp.float32),
        in_specs=[pl.BlockSpec(memory_space=pltpu.VMEM)] * 2,
        out_specs=pl.BlockSpec(memory_space=pltpu.VMEM),
        scratch_shapes=[
            pltpu.VMEM((rounds + 1,) + shard_a.shape, jnp.float32),
            pltpu.VMEM((rounds + 1,) + shard_b.shape, jnp.float32),
            pltpu.VMEM((rounds + 1,) + shard_a.shape, jnp.bfloat16),
            pltpu.VMEM((rounds + 1,) + shard_b.shape, jnp.bfloat16),
            pltpu.VMEM((rounds + 1,) + shard_a.shape, jnp.bfloat16),
            pltpu.VMEM((rounds + 1,) + shard_b.shape, jnp.bfloat16),
            pltpu.SemaphoreType.DMA((2 * rounds + 1,)),
            pltpu.SemaphoreType.DMA((2 * rounds + 1,)),
        ],
        compiler_params=pltpu.CompilerParams(collective_id=1, has_side_effects=True),
    )(shard_a, shard_b)


def span_kernel(
    head_count, q_ref, k_ref, v_ref, gc_ref, gr_ref, shard_a_ref, shard_b_ref, mix_ref, entry_ref
):
    queries = q_ref[...]
    key_vecs = k_ref[...]
    values = v_ref[...]
    decay_col = gc_ref[:, :, 0:1]
    decay_row = gr_ref[...]
    rate = gc_ref[:, :, 1:2]
    block_len = queries.shape[1]
    row_ids = lax.broadcasted_iota(jnp.int32, (1, block_len, block_len), 1)
    col_ids = lax.broadcasted_iota(jnp.int32, (1, block_len, block_len), 2)
    inclusive = row_ids >= col_ids
    strict = row_ids > col_ids
    cum_col = jnp.sum(jnp.where(inclusive, decay_row, 0.0), axis=2, keepdims=True)
    cum_row = jnp.sum(jnp.where(row_ids <= col_ids, decay_col, 0.0), axis=1, keepdims=True)
    gap_mat = cum_col - cum_row
    falloff = jnp.where(inclusive, jnp.exp(jnp.where(inclusive, gap_mat, 0.0)), 0.0)
    key_dots = jnp.einsum("bsd,btd->bst", key_vecs, key_vecs, precision=highest,
                          preferred_element_type=jnp.float32)
    lower_part = jnp.where(strict, rate * falloff * key_dots, 0.0)
    inverse = jnp.where((row_ids // 2 == col_ids // 2) & strict, -lower_part, 0.0) + jnp.where(
        row_ids == col_ids, 1.0, 0.0
    )
    size = 2
    while size < block_len:
        band = (row_ids // (2 * size) == col_ids // (2 * size)) & (row_ids // size != col_ids // size)
        off_blocks = jnp.where(band, lower_part, 0.0)
        step = jnp.einsum("bst,btu->bsu", inverse, off_blocks, precision=highest,
                          preferred_element_type=jnp.float32)
        inverse = inverse - jnp.einsum("bst,btu->bsu", step, inverse, precision=highest,
                                       preferred_element_type=jnp.float32)
        size *= 2
    grow = jnp.exp(cum_col)
    wy_keys = jnp.einsum("bst,btd->bsd", inverse, (rate * grow) * key_vecs, precision=highest,
                         preferred_element_type=jnp.float32)
    wy_values = jnp.einsum("bst,btd->bsd", inverse, rate * values, precision=highest,
                           preferred_element_type=jnp.float32)
    scores = falloff * jnp.einsum("bsd,btd->bst", queries, key_vecs, precision=highest,
                                  preferred_element_type=jnp.float32)
    last = cum_row[:, :, block_len - 1 :]
    tail_keys_t = jnp.swapaxes(jnp.exp(last - cum_col) * key_vecs, 1, 2)
    width = key_vecs.shape[2]
    eye_rows = lax.broadcasted_iota(jnp.int32, (1, width, width), 1)
    eye_cols = lax.broadcasted_iota(jnp.int32, (1, width, width), 2)
    transition = jnp.where(eye_rows == eye_cols, jnp.exp(last), 0.0) - jnp.einsum(
        "bds,bse->bde", tail_keys_t, wy_keys, precision=highest, preferred_element_type=jnp.float32
    )
    written = jnp.einsum("bds,bse->bde", tail_keys_t, wy_values, precision=highest,
                         preferred_element_type=jnp.float32)
    carry_map = grow * queries - jnp.einsum("bst,btd->bsd", scores, wy_keys, precision=highest,
                                            preferred_element_type=jnp.float32)
    local_out = jnp.einsum("bst,bte->bse", scores, wy_values, precision=highest,
                           preferred_element_type=jnp.float32)
    for span in range(queries.shape[0] // head_count):
        heads = slice(span * head_count, (span + 1) * head_count)
        if span == 0:
            mix_ref[heads] = local_out[heads]
            entry_ref[heads] = carry_map[heads]
            prefix_a = transition[heads]
            prefix_b = written[heads]
            continue
        mix_ref[heads] = local_out[heads] + jnp.einsum(
            "hsd,hde->hse", carry_map[heads], prefix_b, precision=highest,
            preferred_element_type=jnp.float32)
        entry_ref[heads] = jnp.einsum("hsd,hde->hse", carry_map[heads], prefix_a, precision=highest,
                                      preferred_element_type=jnp.float32)
        prefix_b = written[heads] + jnp.einsum(
            "hde,hef->hdf", transition[heads], prefix_b, precision=highest,
            preferred_element_type=jnp.float32)
        prefix_a = jnp.einsum("hde,hef->hdf", transition[heads], prefix_a, precision=highest,
                              preferred_element_type=jnp.float32)
    shard_a_ref[...] = prefix_a
    shard_b_ref[...] = prefix_b


def span_terms_kernel(queries, key_vecs, values, log_decay, write_rate):
    lead = queries.shape[:2]
    block_len, width = queries.shape[2], queries.shape[3]
    flat = lambda x: x.reshape((-1,) + x.shape[2:])
    pairs = lead[0] * lead[1]
    decay = log_decay.reshape(pairs, block_len)
    rate = write_rate.reshape(pairs, block_len)
    shard_a, shard_b, local_mix, entry_map = pl.pallas_call(
        functools.partial(span_kernel, lead[1]),
        out_shape=[
            jax.ShapeDtypeStruct((lead[1], width, width), jnp.float32),
            jax.ShapeDtypeStruct((lead[1], width, values.shape[3]), jnp.float32),
            jax.ShapeDtypeStruct((pairs, block_len, values.shape[3]), jnp.float32),
            jax.ShapeDtypeStruct((pairs, block_len, width), jnp.float32),
        ],
        in_specs=[pl.BlockSpec(memory_space=pltpu.VMEM)] * 5,
        out_specs=[pl.BlockSpec(memory_space=pltpu.VMEM)] * 4,
    )(
        flat(queries),
        flat(key_vecs),
        flat(values),
        jnp.stack([decay, rate], axis=-1),
        decay[:, None, :],
    )
    return (
        shard_a,
        shard_b,
        local_mix.reshape(lead + local_mix.shape[1:]),
        entry_map.reshape(lead + entry_map.shape[1:]),
    )


def group_sum_kernel(group_count, part_ref, out_ref, landed, send_sems, recv_sems):
    me = lax.axis_index("hg")
    seq_me = lax.axis_index("seq")
    rows = out_ref.shape[0]
    barrier = pltpu.get_barrier_semaphore()
    for step in range(1, group_count):
        peer = lax.rem(me + step, group_count)
        pl.semaphore_signal(barrier, inc=1, device_id=(seq_me, peer), device_id_type=MESH)
    pl.semaphore_wait(barrier, group_count - 1)
    sends = []
    for step in range(1, group_count):
        peer = lax.rem(me + step, group_count)
        copy = pltpu.make_async_remote_copy(
            src_ref=part_ref.at[pl.ds(pl.multiple_of(peer * rows, 8), rows)],
            dst_ref=landed.at[me],
            send_sem=send_sems.at[step],
            recv_sem=recv_sems.at[me],
            device_id=(seq_me, peer),
            device_id_type=MESH,
        )
        copy.start()
        sends.append(copy)
    total = part_ref[pl.ds(pl.multiple_of(me * rows, 8), rows), :].astype(jnp.float32)
    for step in range(1, group_count):
        source = lax.rem(me + group_count - step, group_count)
        pltpu.make_async_remote_copy(
            src_ref=part_ref.at[pl.ds(0, rows)],
            dst_ref=landed.at[source],
            send_sem=send_sems.at[step],
            recv_sem=recv_sems.at[source],
            device_id=(seq_me, source),
            device_id_type=MESH,
        ).wait_recv()
        total = total + landed[source].astype(jnp.float32)
    for copy in sends:
        copy.wait_send()
    out_ref[...] = total.astype(out_ref.dtype)


def group_sum(part, group_count):
    if group_count == 1:
        return part
    rows = part.shape[0] // group_count
    cols = part.shape[1]
    return pl.pallas_call(
        functools.partial(group_sum_kernel, group_count),
        out_shape=jax.ShapeDtypeStruct((rows, cols), part.dtype),
        in_specs=[pl.BlockSpec(memory_space=pltpu.VMEM)],
        out_specs=pl.BlockSpec(memory_space=pltpu.VMEM),
        scratch_shapes=[
            pltpu.VMEM((group_count, rows, cols), part.dtype),
            pltpu.SemaphoreType.DMA((group_count,)),
            pltpu.SemaphoreType.DMA((group_count,)),
        ],
        compiler_params=pltpu.CompilerParams(collective_id=0, has_side_effects=True),
    )(part)


def on_device(
    hidden_in,
    w_query,
    w_key,
    w_value,
    w_zgate,
    w_decay,
    w_beta,
    conv_query,
    conv_key,
    conv_value,
    a_log,
    dt_bias,
    norm_gain,
    w_out,
):
    tok_rows = hidden_in.shape[0]
    pre_query, pre_key, pre_value = project_inputs(hidden_in, w_query, w_key, w_value)
    kernel_len = conv_query.shape[0]
    rim_rows = tok_rows - kernel_len + 1
    rim_block = jnp.concatenate(
        [pre_query[rim_rows:], pre_key[rim_rows:], pre_value[rim_rows:]], axis=1
    )
    prior = passed_along(rim_block, "seq", 1)
    queries, key_vecs, values, log_decay, write_rate, zgate = mixer_inputs(
        hidden_in,
        pre_query,
        pre_key,
        pre_value,
        prior,
        conv_query,
        conv_key,
        conv_value,
        w_zgate,
        w_decay,
        w_beta,
        a_log,
        dt_bias,
    )
    shard_a, shard_b, local_mix, entry_map = span_terms_kernel(
        to_blocks(queries),
        to_blocks(key_vecs),
        to_blocks(values),
        to_blocks(log_decay[..., None])[..., 0],
        to_blocks(write_rate[..., None])[..., 0],
    )
    head_count = values.shape[1]
    state_in = shard_scan(shard_a, shard_b, lax.axis_size("seq"))
    produced = local_mix + jnp.einsum("jhsd,hde->jhse", entry_map, state_in, precision=highest)
    produced = produced.transpose(0, 2, 1, 3).reshape(tok_rows, head_count, DV)
    gated = gated_output(produced, zgate, norm_gain)
    part = jnp.dot(gated, w_out, preferred_element_type=jnp.float32).astype(jnp.bfloat16)
    return group_sum(part, lax.axis_size("hg"))


def solution(mesh):
    return jax.shard_map(
        on_device,
        mesh=mesh,
        in_specs=(
            P("seq", None),
            P(None, "hg"),
            P(None, "hg"),
            P(None, "hg"),
            P(None, "hg"),
            P(None, "hg"),
            P(None, "hg"),
            P(None, "hg"),
            P(None, "hg"),
            P(None, "hg"),
            P("hg"),
            P("hg"),
            P(),
            P("hg", None),
        ),
        out_specs=P(("seq", "hg"), None),
        check_vma=False,
    )
```

```python
import functools

import jax
import numpy as np
import jax.numpy as jnp
from jax import lax
from jax.experimental import pallas as pl
from jax.experimental.pallas import tpu as pltpu
from jax.sharding import PartitionSpec as P

MESH = pl.DeviceIdType.MESH

VH = 32
KH = 16
DK = 128
DV = 128
SPAN = 64


highest = lax.Precision.HIGH
norm_eps = 1e-06


def passed_along(block, axis, distance):
    devices = range(lax.axis_size(axis))
    route = [(i - distance, i) for i in devices if i - distance in devices]
    return lax.ppermute(block, axis, route)


def project_inputs(hidden_in, w_query, w_key, w_value):
    pre_query = jnp.dot(hidden_in, w_query, preferred_element_type=jnp.float32).astype(jnp.bfloat16)
    pre_key = jnp.dot(hidden_in, w_key, preferred_element_type=jnp.float32).astype(jnp.bfloat16)
    pre_value = jnp.dot(hidden_in, w_value, preferred_element_type=jnp.float32).astype(jnp.bfloat16)
    return (pre_query, pre_key, pre_value)


def conv_silu(projected, kernel, prior):
    kernel_len = kernel.shape[0]
    tok_rows = projected.shape[0]
    padded = jnp.concatenate([prior.astype(jnp.float32), projected.astype(jnp.float32)], axis=0)
    summed = jnp.zeros((tok_rows, projected.shape[1]), jnp.float32)
    for offset in range(kernel_len):
        summed = summed + kernel[offset].astype(jnp.float32) * padded[offset : offset + tok_rows]
    return jax.nn.silu(summed)


def unit_length(vectors):
    return vectors * lax.rsqrt(jnp.sum(vectors * vectors, axis=-1, keepdims=True) + norm_eps)


def mixer_inputs(
    hidden_in,
    pre_query,
    pre_key,
    pre_value,
    prior,
    conv_query,
    conv_key,
    conv_value,
    w_zgate,
    w_decay,
    w_beta,
    a_log,
    dt_bias,
):
    tok_rows = hidden_in.shape[0]
    query_cols = pre_query.shape[1]
    key_cols = pre_key.shape[1]
    ratio = VH // KH
    queries = unit_length(
        conv_silu(pre_query, conv_query, prior[:, :query_cols]).reshape(tok_rows, -1, DK)
    ) * DK ** (-0.5)
    key_vecs = unit_length(
        conv_silu(pre_key, conv_key, prior[:, query_cols : query_cols + key_cols]).reshape(
            tok_rows, -1, DK
        )
    )
    values = conv_silu(pre_value, conv_value, prior[:, query_cols + key_cols :]).reshape(
        tok_rows, -1, DV
    )
    queries = jnp.repeat(queries, ratio, axis=1)
    key_vecs = jnp.repeat(key_vecs, ratio, axis=1)
    zgate = jnp.dot(hidden_in, w_zgate, preferred_element_type=jnp.float32).astype(jnp.bfloat16)
    rate_logits = jnp.dot(hidden_in, w_decay, preferred_element_type=jnp.float32)
    log_decay = -jnp.exp(a_log) * jax.nn.softplus(rate_logits + dt_bias)
    write_rate = jax.nn.sigmoid(jnp.dot(hidden_in, w_beta, preferred_element_type=jnp.float32))
    return (queries, key_vecs, values, log_decay, write_rate, zgate)


def to_blocks(array_3d):
    tok_rows, head_count = (array_3d.shape[0], array_3d.shape[1])
    return array_3d.reshape(tok_rows // SPAN, SPAN, head_count, -1).transpose(0, 2, 1, 3)


def unit_lower_inverse(lower_part):
    block_len = lower_part.shape[-1]
    row_ids = np.arange(block_len)[:, None]
    col_ids = np.arange(block_len)[None, :]
    first = jnp.asarray((row_ids // 2 == col_ids // 2) & (row_ids != col_ids), jnp.float32)
    inverse = lax.optimization_barrier(
        jnp.asarray(np.eye(block_len), jnp.float32) - lower_part * first
    )
    size = 2
    while size < block_len:
        band = (row_ids // (2 * size) == col_ids // (2 * size)) & (row_ids // size != col_ids // size)
        off_blocks = lower_part * jnp.asarray(band, jnp.float32)
        step = jnp.einsum("...st,...tu->...su", inverse, off_blocks, precision=highest)
        inverse = inverse - jnp.einsum("...st,...tu->...su", step, inverse, precision=highest)
        size *= 2
    return inverse


def span_terms(queries, key_vecs, values, log_decay, write_rate):
    block_len = log_decay.shape[-1]
    cum_decay = jnp.cumsum(log_decay, axis=-1)
    row_ids = lax.broadcasted_iota(jnp.int32, (block_len, block_len), 0)
    col_ids = lax.broadcasted_iota(jnp.int32, (block_len, block_len), 1)
    inclusive = row_ids >= col_ids
    strict = row_ids > col_ids
    gap_mat = cum_decay[..., :, None] - cum_decay[..., None, :]
    falloff = jnp.where(inclusive, jnp.exp(jnp.where(inclusive, gap_mat, 0.0)), 0.0)
    key_dots = jnp.einsum("...sd,...td->...st", key_vecs, key_vecs, precision=highest)
    lower_part = jnp.where(strict, write_rate[..., :, None] * falloff * key_dots, 0.0)
    inverse = unit_lower_inverse(lower_part)
    wy_keys = jnp.einsum(
        "...st,...td->...sd",
        inverse,
        (write_rate * jnp.exp(cum_decay))[..., None] * key_vecs,
        precision=highest,
    )
    wy_values = jnp.einsum(
        "...st,...td->...sd", inverse, write_rate[..., None] * values, precision=highest
    )
    scores = falloff * jnp.einsum("...sd,...td->...st", queries, key_vecs, precision=highest)
    tail_keys = jnp.exp(cum_decay[..., -1:] - cum_decay)[..., None] * key_vecs
    whole_decay = jnp.exp(cum_decay[..., -1])[..., None, None]
    transition = whole_decay * jnp.eye(key_vecs.shape[-1], dtype=jnp.float32) - jnp.einsum(
        "...sd,...se->...de", tail_keys, wy_keys, precision=highest
    )
    written = jnp.einsum("...sd,...se->...de", tail_keys, wy_values, precision=highest)
    carry_map = jnp.exp(cum_decay)[..., None] * queries - jnp.einsum(
        "...st,...td->...sd", scores, wy_keys, precision=highest
    )
    local_out = jnp.einsum("...st,...te->...se", scores, wy_values, precision=highest)
    return (transition, written, carry_map, local_out)


def gated_output(produced, zgate, norm_gain):
    tok_rows = produced.shape[0]
    mean_sq = jnp.mean(produced * produced, axis=-1, keepdims=True)
    gate_vals = jax.nn.silu(zgate.astype(jnp.float32).reshape(produced.shape))
    normed = produced * lax.rsqrt(mean_sq + norm_eps) * norm_gain * gate_vals
    return normed.reshape(tok_rows, -1).astype(jnp.bfloat16)


def advance(state_now, per_span):
    transition, written, carry_map, local_out = per_span
    produced = jnp.einsum("hsd,hde->hse", carry_map, state_now, precision=highest) + local_out
    state_next = jnp.einsum("hde,hef->hdf", transition, state_now, precision=highest) + written
    return (state_next, produced)


def apply_shard(trans_mat, state_now, written):
    return jnp.einsum("hde,hef->hdf", trans_mat, state_now, precision=highest) + written


def shard_scan_kernel(
    shard_count, a_ref, b_ref, out_ref, cur_a, cur_b, out_a, out_b, got_a, got_b, send_sems, recv_sems
):
    me = lax.axis_index("seq")
    hg_me = lax.axis_index("hg")
    head_count = a_ref.shape[0]
    distances = []
    distance = 1
    while distance < shard_count:
        distances.append(distance)
        distance *= 2
    barrier = pltpu.get_barrier_semaphore()
    for distance in distances:
        for target in (lax.rem(me + distance, shard_count), lax.rem(me + shard_count - distance, shard_count)):
            pl.semaphore_signal(barrier, inc=1, device_id=(target, hg_me), device_id_type=MESH)
    pl.semaphore_wait(barrier, 2 * len(distances))
    out_a[0] = a_ref[...].astype(out_a.dtype)
    out_b[0] = b_ref[...].astype(out_b.dtype)
    sem_index = 0
    for round_index, distance in enumerate(distances):
        target = lax.rem(me + distance, shard_count)
        sends_a = round_index + 1 < len(distances)
        copies = [
            pltpu.make_async_remote_copy(
                src_ref=out_b.at[round_index],
                dst_ref=got_b.at[round_index],
                send_sem=send_sems.at[sem_index],
                recv_sem=recv_sems.at[sem_index],
                device_id=(target, hg_me),
                device_id_type=MESH,
            )
        ]
        if sends_a:
            copies.append(
                pltpu.make_async_remote_copy(
                    src_ref=out_a.at[round_index],
                    dst_ref=got_a.at[round_index],
                    send_sem=send_sems.at[sem_index + 1],
                    recv_sem=recv_sems.at[sem_index + 1],
                    device_id=(target, hg_me),
                    device_id_type=MESH,
                )
            )
        sem_index += len(copies)
        for copy in copies:
            copy.start()
        for copy in copies:
            copy.wait()
        has_prev = me >= distance
        for head in range(head_count):
            own_a = a_ref[head] if round_index == 0 else cur_a[round_index, head]
            own_b = b_ref[head] if round_index == 0 else cur_b[round_index, head]
            joined_b = (
                jnp.dot(own_a, got_b[round_index, head].astype(jnp.float32), precision=highest,
                        preferred_element_type=jnp.float32)
                + own_b
            )
            next_b = jnp.where(has_prev, joined_b, own_b)
            cur_b[round_index + 1, head] = next_b
            out_b[round_index + 1, head] = next_b.astype(out_b.dtype)
            if sends_a:
                joined_a = jnp.dot(own_a, got_a[round_index, head].astype(jnp.float32),
                                   precision=highest, preferred_element_type=jnp.float32)
                next_a = jnp.where(has_prev, joined_a, own_a)
                cur_a[round_index + 1, head] = next_a
                out_a[round_index + 1, head] = next_a.astype(out_a.dtype)
    last = len(distances)
    shift = pltpu.make_async_remote_copy(
        src_ref=out_b.at[last],
        dst_ref=got_b.at[last],
        send_sem=send_sems.at[sem_index],
        recv_sem=recv_sems.at[sem_index],
        device_id=(lax.rem(me + 1, shard_count), hg_me),
        device_id_type=MESH,
    )
    shift.start()
    shift.wait()
    out_ref[...] = jnp.where(me >= 1, got_b[last].astype(jnp.float32), 0.0)


def shard_scan(shard_a, shard_b, shard_count):
    rounds = max(1, (shard_count - 1).bit_length())
    return pl.pallas_call(
        functools.partial(shard_scan_kernel, shard_count),
        out_shape=jax.ShapeDtypeStruct(shard_b.shape, jnp.float32),
        in_specs=[pl.BlockSpec(memory_space=pltpu.VMEM)] * 2,
        out_specs=pl.BlockSpec(memory_space=pltpu.VMEM),
        scratch_shapes=[
            pltpu.VMEM((rounds + 1,) + shard_a.shape, jnp.float32),
            pltpu.VMEM((rounds + 1,) + shard_b.shape, jnp.float32),
            pltpu.VMEM((rounds + 1,) + shard_a.shape, jnp.bfloat16),
            pltpu.VMEM((rounds + 1,) + shard_b.shape, jnp.bfloat16),
            pltpu.VMEM((rounds + 1,) + shard_a.shape, jnp.bfloat16),
            pltpu.VMEM((rounds + 1,) + shard_b.shape, jnp.bfloat16),
            pltpu.SemaphoreType.DMA((2 * rounds + 1,)),
            pltpu.SemaphoreType.DMA((2 * rounds + 1,)),
        ],
        compiler_params=pltpu.CompilerParams(collective_id=1, has_side_effects=True),
    )(shard_a, shard_b)


def span_kernel(
    head_count, q_ref, k_ref, v_ref, gc_ref, gr_ref, shard_a_ref, shard_b_ref, mix_ref, entry_ref
):
    queries = q_ref[...]
    key_vecs = k_ref[...]
    values = v_ref[...]
    decay_col = gc_ref[:, :, 0:1]
    decay_row = gr_ref[...]
    rate = gc_ref[:, :, 1:2]
    block_len = queries.shape[1]
    row_ids = lax.broadcasted_iota(jnp.int32, (1, block_len, block_len), 1)
    col_ids = lax.broadcasted_iota(jnp.int32, (1, block_len, block_len), 2)
    inclusive = row_ids >= col_ids
    strict = row_ids > col_ids
    cum_col = jnp.sum(jnp.where(inclusive, decay_row, 0.0), axis=2, keepdims=True)
    cum_row = jnp.sum(jnp.where(row_ids <= col_ids, decay_col, 0.0), axis=1, keepdims=True)
    gap_mat = cum_col - cum_row
    falloff = jnp.where(inclusive, jnp.exp(jnp.where(inclusive, gap_mat, 0.0)), 0.0)
    key_dots = jnp.einsum("bsd,btd->bst", key_vecs, key_vecs, precision=highest,
                          preferred_element_type=jnp.float32)
    lower_part = jnp.where(strict, rate * falloff * key_dots, 0.0)
    inverse = jnp.where((row_ids // 2 == col_ids // 2) & strict, -lower_part, 0.0) + jnp.where(
        row_ids == col_ids, 1.0, 0.0
    )
    size = 2
    while size < block_len:
        band = (row_ids // (2 * size) == col_ids // (2 * size)) & (row_ids // size != col_ids // size)
        off_blocks = jnp.where(band, lower_part, 0.0)
        step = jnp.einsum("bst,btu->bsu", inverse, off_blocks, precision=highest,
                          preferred_element_type=jnp.float32)
        inverse = inverse - jnp.einsum("bst,btu->bsu", step, inverse, precision=highest,
                                       preferred_element_type=jnp.float32)
        size *= 2
    grow = jnp.exp(cum_col)
    wy_keys = jnp.einsum("bst,btd->bsd", inverse, (rate * grow) * key_vecs, precision=highest,
                         preferred_element_type=jnp.float32)
    wy_values = jnp.einsum("bst,btd->bsd", inverse, rate * values, precision=highest,
                           preferred_element_type=jnp.float32)
    scores = falloff * jnp.einsum("bsd,btd->bst", queries, key_vecs, precision=highest,
                                  preferred_element_type=jnp.float32)
    last = cum_row[:, :, block_len - 1 :]
    tail_keys_t = jnp.swapaxes(jnp.exp(last - cum_col) * key_vecs, 1, 2)
    width = key_vecs.shape[2]
    eye_rows = lax.broadcasted_iota(jnp.int32, (1, width, width), 1)
    eye_cols = lax.broadcasted_iota(jnp.int32, (1, width, width), 2)
    transition = jnp.where(eye_rows == eye_cols, jnp.exp(last), 0.0) - jnp.einsum(
        "bds,bse->bde", tail_keys_t, wy_keys, precision=highest, preferred_element_type=jnp.float32
    )
    written = jnp.einsum("bds,bse->bde", tail_keys_t, wy_values, precision=highest,
                         preferred_element_type=jnp.float32)
    carry_map = grow * queries - jnp.einsum("bst,btd->bsd", scores, wy_keys, precision=highest,
                                            preferred_element_type=jnp.float32)
    local_out = jnp.einsum("bst,bte->bse", scores, wy_values, precision=highest,
                           preferred_element_type=jnp.float32)
    for span in range(queries.shape[0] // head_count):
        heads = slice(span * head_count, (span + 1) * head_count)
        if span == 0:
            mix_ref[heads] = local_out[heads]
            entry_ref[heads] = carry_map[heads]
            prefix_a = transition[heads]
            prefix_b = written[heads]
            continue
        mix_ref[heads] = local_out[heads] + jnp.einsum(
            "hsd,hde->hse", carry_map[heads], prefix_b, precision=highest,
            preferred_element_type=jnp.float32)
        entry_ref[heads] = jnp.einsum("hsd,hde->hse", carry_map[heads], prefix_a, precision=highest,
                                      preferred_element_type=jnp.float32)
        prefix_b = written[heads] + jnp.einsum(
            "hde,hef->hdf", transition[heads], prefix_b, precision=highest,
            preferred_element_type=jnp.float32)
        prefix_a = jnp.einsum("hde,hef->hdf", transition[heads], prefix_a, precision=highest,
                              preferred_element_type=jnp.float32)
    shard_a_ref[...] = prefix_a
    shard_b_ref[...] = prefix_b


def span_terms_kernel(queries, key_vecs, values, log_decay, write_rate):
    lead = queries.shape[:2]
    block_len, width = queries.shape[2], queries.shape[3]
    flat = lambda x: x.reshape((-1,) + x.shape[2:])
    pairs = lead[0] * lead[1]
    decay = log_decay.reshape(pairs, block_len)
    rate = write_rate.reshape(pairs, block_len)
    shard_a, shard_b, local_mix, entry_map = pl.pallas_call(
        functools.partial(span_kernel, lead[1]),
        out_shape=[
            jax.ShapeDtypeStruct((lead[1], width, width), jnp.float32),
            jax.ShapeDtypeStruct((lead[1], width, values.shape[3]), jnp.float32),
            jax.ShapeDtypeStruct((pairs, block_len, values.shape[3]), jnp.float32),
            jax.ShapeDtypeStruct((pairs, block_len, width), jnp.float32),
        ],
        in_specs=[pl.BlockSpec(memory_space=pltpu.VMEM)] * 5,
        out_specs=[pl.BlockSpec(memory_space=pltpu.VMEM)] * 4,
    )(
        flat(queries),
        flat(key_vecs),
        flat(values),
        jnp.stack([decay, rate], axis=-1),
        decay[:, None, :],
    )
    return (
        shard_a,
        shard_b,
        local_mix.reshape(lead + local_mix.shape[1:]),
        entry_map.reshape(lead + entry_map.shape[1:]),
    )


def group_sum_kernel(group_count, part_ref, out_ref, landed, send_sems, recv_sems):
    me = lax.axis_index("hg")
    seq_me = lax.axis_index("seq")
    rows = out_ref.shape[0]
    barrier = pltpu.get_barrier_semaphore()
    for step in range(1, group_count):
        peer = lax.rem(me + step, group_count)
        pl.semaphore_signal(barrier, inc=1, device_id=(seq_me, peer), device_id_type=MESH)
    pl.semaphore_wait(barrier, group_count - 1)
    sends = []
    for step in range(1, group_count):
        peer = lax.rem(me + step, group_count)
        copy = pltpu.make_async_remote_copy(
            src_ref=part_ref.at[pl.ds(pl.multiple_of(peer * rows, 8), rows)],
            dst_ref=landed.at[me],
            send_sem=send_sems.at[step],
            recv_sem=recv_sems.at[me],
            device_id=(seq_me, peer),
            device_id_type=MESH,
        )
        copy.start()
        sends.append(copy)
    total = part_ref[pl.ds(pl.multiple_of(me * rows, 8), rows), :].astype(jnp.float32)
    for step in range(1, group_count):
        source = lax.rem(me + group_count - step, group_count)
        pltpu.make_async_remote_copy(
            src_ref=part_ref.at[pl.ds(0, rows)],
            dst_ref=landed.at[source],
            send_sem=send_sems.at[step],
            recv_sem=recv_sems.at[source],
            device_id=(seq_me, source),
            device_id_type=MESH,
        ).wait_recv()
        total = total + landed[source].astype(jnp.float32)
    for copy in sends:
        copy.wait_send()
    out_ref[...] = total.astype(out_ref.dtype)


def group_sum(part, group_count):
    if group_count == 1:
        return part
    rows = part.shape[0] // group_count
    cols = part.shape[1]
    return pl.pallas_call(
        functools.partial(group_sum_kernel, group_count),
        out_shape=jax.ShapeDtypeStruct((rows, cols), part.dtype),
        in_specs=[pl.BlockSpec(memory_space=pltpu.VMEM)],
        out_specs=pl.BlockSpec(memory_space=pltpu.VMEM),
        scratch_shapes=[
            pltpu.VMEM((group_count, rows, cols), part.dtype),
            pltpu.SemaphoreType.DMA((group_count,)),
            pltpu.SemaphoreType.DMA((group_count,)),
        ],
        compiler_params=pltpu.CompilerParams(collective_id=0, has_side_effects=True),
    )(part)


def on_device(
    hidden_in,
    w_query,
    w_key,
    w_value,
    w_zgate,
    w_decay,
    w_beta,
    conv_query,
    conv_key,
    conv_value,
    a_log,
    dt_bias,
    norm_gain,
    w_out,
):
    tok_rows = hidden_in.shape[0]
    pre_query, pre_key, pre_value = project_inputs(hidden_in, w_query, w_key, w_value)
    kernel_len = conv_query.shape[0]
    rim_rows = tok_rows - kernel_len + 1
    rim_block = jnp.concatenate(
        [pre_query[rim_rows:], pre_key[rim_rows:], pre_value[rim_rows:]], axis=1
    )
    prior = passed_along(rim_block, "seq", 1)
    queries, key_vecs, values, log_decay, write_rate, zgate = mixer_inputs(
        hidden_in,
        pre_query,
        pre_key,
        pre_value,
        prior,
        conv_query,
        conv_key,
        conv_value,
        w_zgate,
        w_decay,
        w_beta,
        a_log,
        dt_bias,
    )
    shard_a, shard_b, local_mix, entry_map = span_terms_kernel(
        to_blocks(queries),
        to_blocks(key_vecs),
        to_blocks(values),
        to_blocks(log_decay[..., None])[..., 0],
        to_blocks(write_rate[..., None])[..., 0],
    )
    head_count = values.shape[1]
    state_in = shard_scan(shard_a, shard_b, lax.axis_size("seq"))
    produced = local_mix + jnp.einsum("jhsd,hde->jhse", entry_map, state_in, precision=highest)
    produced = produced.transpose(0, 2, 1, 3).reshape(tok_rows, head_count, DV)
    gated = gated_output(produced, zgate, norm_gain)
    part = jnp.dot(gated, w_out, preferred_element_type=jnp.float32).astype(jnp.bfloat16)
    return group_sum(part, lax.axis_size("hg"))


def solution(mesh):
    return jax.shard_map(
        on_device,
        mesh=mesh,
        in_specs=(
            P("seq", None),
            P(None, "hg"),
            P(None, "hg"),
            P(None, "hg"),
            P(None, "hg"),
            P(None, "hg"),
            P(None, "hg"),
            P(None, "hg"),
            P(None, "hg"),
            P(None, "hg"),
            P("hg"),
            P("hg"),
            P(),
            P("hg", None),
        ),
        out_specs=P(("seq", "hg"), None),
        check_vma=False,
    )
```
